32 devices in a mesh: group: 2 (over y), ctx: 4 (over z), tp: 4 (over x, core).
Axes of the slice: x: 2, y: 2, z: 4, core: 2. Of those that a mesh axis runs over, the one named last changes fastest.
Arguments:
- queries: bfloat16 [1024, 4096], P(('group', 'ctx'), 'tp'), parts along dimension 0, as said below
- key_rows: bfloat16 [1024, 1024], P(('group', 'ctx'), 'tp'), parts along dimension 0, as said below
- value_rows: bfloat16 [1024, 1024], P(('group', 'ctx'), 'tp'), parts along dimension 0, may hold values from -6 to 6
- doc_start: int32 [1024], P(('group', 'ctx')), parts along dimension 0, may hold values from 0 to 511, as said below
- doc_end: int32 [1024], P(('group', 'ctx')), parts along dimension 0, may hold values from 1 to 512, as said below
- block_target: int32 [16], P(('group', 'ctx')), parts along dimension 0, may hold values from 0 to 7, as said below
- out_weight: bfloat16 [4096, 2048], P('tp', 'ctx'), may hold values from -0.09375 to 0.09375
Outputs:
- balanced_out: bfloat16 [1024, 2048], P(('group', 'ctx', 'tp')), parts along dimension 0
The draws below stay inside these ranges and needn't reach their ends.
There are 2 independent parts, one for each index of `group`. The reference program is written for one: setup_inputs(seed, part) draws one part's arguments, and reference() takes and returns one part's arrays. A program takes and returns all parts, laid end to end along the dimension named above; an argument that names none is the same for every part. Nothing has to cross between parts.
Inputs may be any that keep to these rules, and one draw needn't show every extreme that they name: Documents are consecutive runs of rows; row i's document begins at row doc_start[i] <= i; each document has 1 to 128 rows and one has exactly 128. Row i's document ends just before row doc_end[i] > i; doc_start and doc_end describe the same documents. A permutation of the 8 row blocks of 64 rows: block b goes to index block_target[b] // 2 of ctx at position block_target[b] % 2; the 2 blocks of one index of ctx go to 2 different indices. `queries`: entries lie within -6 to 6. `key_rows`: entries lie within -6 to 6.
All inputs are finite; a program needn't handle non-finite values.
Results may differ from the reference program's by a relative error of at most 0.012.
Values may be sent and summed in bfloat16 or wider, within the bound.
No kernel may reach another device: no remote copies, remote signals or barrier semaphores. Data moves between devices by JAX's collectives and lax.ppermute only.
A program may use at most 64 MiB of HBM per device.

```python
import jax
import jax.numpy as jnp
from jax import lax

HEADS = 32
KV_HEADS = 8
HEAD_DIM = 128
D_OUT = 2048
TOKENS = 512
MOST = 128
BLK = 64
BPD = 2
N_CTX = 4


def doc_bounds(key):
    base_key = jax.random.fold_in(key, 7)
    length_key, place_key = jax.random.split(base_key)
    lengths = jax.random.randint(length_key, (TOKENS,), 2, MOST + 1)
    chosen = jax.random.randint(place_key, (), 0, 2)
    row_ids = jnp.arange(TOKENS, dtype=jnp.int32)
    lengths = jnp.where(row_ids == chosen, MOST, lengths).astype(jnp.int32)
    ends = jnp.cumsum(lengths).astype(jnp.int32)
    starts = ends - lengths
    marks = jnp.zeros((TOKENS,), jnp.int32).at[starts].set(1, mode='drop')
    marks = marks.at[TOKENS - 1].set(1)
    first_row = lax.cummax(jnp.where(marks > 0, row_ids, 0), axis=0)
    next_start = lax.cummin(jnp.where(marks > 0, row_ids, TOKENS), axis=0, reverse=True)
    end_row = jnp.concatenate([next_start[1:], jnp.full((1,), TOKENS, jnp.int32)])
    return (first_row.astype(jnp.int32), end_row.astype(jnp.int32))


def draw_doc_start(key, part):
    first_row, end_row = doc_bounds(key)
    return first_row


def draw_doc_end(key, part):
    first_row, end_row = doc_bounds(key)
    return end_row


def draw_block_target(key, part):
    base_key = jax.random.fold_in(key, 13)
    keys_list = jax.random.split(base_key, 4)
    relabel = jax.random.permutation(keys_list[0], N_CTX)
    source_shift = jax.random.permutation(keys_list[1], N_CTX)
    offsets = jax.random.permutation(keys_list[2], N_CTX)[:BPD]
    slot_tables = jax.vmap(lambda sub_key: jax.random.permutation(sub_key, BPD))(jax.random.split(keys_list[3], N_CTX))
    sources = jnp.arange(N_CTX, dtype=jnp.int32)[:, None]
    dest_device = relabel[(source_shift[sources] + offsets[None, :]) % N_CTX]
    block_index = jnp.broadcast_to(jnp.arange(BPD, dtype=jnp.int32)[None, :], (N_CTX, BPD))
    dest_slot = slot_tables[dest_device, block_index]
    return (dest_device * BPD + dest_slot).reshape(-1).astype(jnp.int32)


def draw_queries(key, part):
    base = jnp.clip(1.5 * jax.random.normal(jax.random.fold_in(key, 21), (TOKENS, HEADS * HEAD_DIM), jnp.float32), -6.0, 6.0)
    return base.astype(jnp.bfloat16)


def draw_key_rows(key, part):
    base = jnp.clip(1.5 * jax.random.normal(jax.random.fold_in(key, 22), (TOKENS, KV_HEADS * HEAD_DIM), jnp.float32), -6.0, 6.0)
    return base.astype(jnp.bfloat16)


def block_scale(key, dims, shards, least, high):
    level = 1.0
    for dim, blocks in shards:
        steps = jax.random.uniform(jax.random.fold_in(jax.random.fold_in(key, 6), dim), (blocks,), jnp.float32, least / len(shards), high / len(shards))
        level = level * jnp.repeat(jnp.exp(steps), dims[dim] // blocks).reshape((-1,) + (1,) * (len(dims) - 1 - dim))
    return level


def centred(rng, dims, scale, limit, shards=(), kind=jnp.bfloat16):
    entries = scale * jax.random.normal(rng, dims, jnp.float32)
    if shards:
        entries = entries * block_scale(rng, dims, shards, -0.22, 0.18)
    return jnp.clip(entries, -limit, limit).astype(kind)


def setup_inputs(seed: int = 0, part: int = 0) -> dict:
    seeds = jax.random.split(jax.random.key(seed), 8)
    part_keys = jax.random.split(jax.random.fold_in(seeds[7], part), 8)
    queries = draw_queries(jax.random.fold_in(jax.random.fold_in(seeds[7], part), 71), part)
    key_rows = draw_key_rows(jax.random.fold_in(jax.random.fold_in(seeds[7], part), 71), part)
    value_rows = centred(part_keys[2], (TOKENS, KV_HEADS * HEAD_DIM), 1.0, 6.0, ((0, 4), (1, 4)))
    doc_start = draw_doc_start(jax.random.fold_in(jax.random.fold_in(seeds[7], part), 71), part)
    doc_end = draw_doc_end(jax.random.fold_in(jax.random.fold_in(seeds[7], part), 71), part)
    block_target = draw_block_target(jax.random.fold_in(jax.random.fold_in(seeds[7], part), 71), part)
    out_weight = centred(seeds[6], (HEADS * HEAD_DIM, D_OUT), (HEADS * HEAD_DIM) ** -0.5, 0.09375, ((0, 4), (1, 4)))
    return {"queries": queries, "key_rows": key_rows, "value_rows": value_rows, "doc_start": doc_start, "doc_end": doc_end, "block_target": block_target, "out_weight": out_weight}


neg_large = -1e30


def reference(queries, key_rows, value_rows, doc_start, doc_end, block_target, out_weight):
    row_ids = jnp.arange(TOKENS, dtype=jnp.int32)
    visible = (row_ids[None, :] <= row_ids[:, None]) & (row_ids[None, :] >= doc_start[:, None]) & (doc_end[None, :] > row_ids[:, None])
    query_heads = queries.reshape(TOKENS, HEADS, HEAD_DIM)
    key_heads = key_rows.reshape(TOKENS, KV_HEADS, HEAD_DIM)
    value_heads = value_rows.reshape(TOKENS, KV_HEADS, HEAD_DIM)
    group_size = HEADS // KV_HEADS
    scale = HEAD_DIM ** -0.5

    def one_head(head_index):
        kv_index = head_index // group_size
        query_one = query_heads[:, head_index, :]
        key_one = key_heads[:, kv_index, :]
        value_one = value_heads[:, kv_index, :]
        scores = jnp.dot(query_one, key_one.T, preferred_element_type=jnp.float32) * scale
        row_max = jnp.max(jnp.where(visible, scores, neg_large), axis=1)
        weights = jnp.where(visible, jnp.exp(scores - row_max[:, None]), 0.0)
        weight_sum = jnp.sum(weights, axis=1)
        summed = jnp.dot(weights.astype(jnp.bfloat16), value_one, preferred_element_type=jnp.float32)
        return (summed / weight_sum[:, None]).astype(jnp.bfloat16)

    per_head = lax.map(one_head, jnp.arange(HEADS, dtype=jnp.int32))
    attended = jnp.transpose(per_head, (1, 0, 2)).reshape(TOKENS, HEADS * HEAD_DIM)
    projected = jnp.dot(attended, out_weight, preferred_element_type=jnp.float32).astype(jnp.bfloat16)
    placed = (block_target[row_ids // BLK] * BLK + row_ids % BLK).astype(jnp.int32)
    return jnp.zeros((TOKENS, D_OUT), jnp.bfloat16).at[placed].set(projected)
```

```python
import functools
import math

import jax
import jax.numpy as jnp
from jax import lax
from jax.experimental import pallas as pl
from jax.experimental.pallas import tpu as pltpu
from jax.sharding import PartitionSpec as P

HEAD_DIM = 128
NEG_LARGE = -1e30


def vmem(count):
    return [pl.BlockSpec(memory_space=pltpu.VMEM)] * count


def smem(count):
    return [pl.BlockSpec(memory_space=pltpu.SMEM)] * count


def params():
    return pltpu.CompilerParams(vmem_limit_bytes=16 * 1024 * 1024)


def cost(flops, moved):
    return pl.CostEstimate(flops=int(flops), bytes_accessed=int(moved), transcendentals=0)


def column(row):
    size = row.shape[1]
    return jnp.transpose(jnp.broadcast_to(row, (size, size)))


def attend_kernel(blocks, q_ref, kh_ref, ko_ref, vh_ref, vo_ref, st_ref, eh_ref, eo_ref, out_ref):
    rows = q_ref.shape[0]
    kv_here = ko_ref.shape[1] // HEAD_DIM
    group = q_ref.shape[1] // HEAD_DIM // kv_here
    core = lax.axis_index("tp") % 2
    base = lax.axis_index("ctx") * rows
    half = rows // blocks // 2
    query_pos = base + lax.broadcasted_iota(jnp.int32, (rows, rows), 0)
    query_start = column(st_ref[...])
    masks = []
    for shift, end_ref in ((rows, eh_ref), (0, eo_ref)):
        key_pos = base - shift + lax.broadcasted_iota(jnp.int32, (rows, rows), 1)
        masks.append(
            (key_pos <= query_pos) & (key_pos >= query_start) & (end_ref[...] > query_pos)
        )
    visible = jnp.concatenate(masks, axis=1)
    visible = jnp.concatenate([visible] * group, axis=0)
    for kv in range(kv_here):
        lanes = pl.ds(kv * HEAD_DIM, HEAD_DIM)
        keys = jnp.concatenate([kh_ref[:, lanes], ko_ref[:, lanes]], axis=0)
        values = jnp.concatenate([vh_ref[:, lanes], vo_ref[:, lanes]], axis=0)
        query = jnp.concatenate(
            [q_ref[:, pl.ds((kv * group + g) * HEAD_DIM, HEAD_DIM)] for g in range(group)], axis=0
        )
        scores = (
            lax.dot_general(
                query, keys, (((1,), (1,)), ((), ())), preferred_element_type=jnp.float32
            )
            * HEAD_DIM**-0.5
        )
        row_max = jnp.max(jnp.where(visible, scores, NEG_LARGE), axis=1, keepdims=True)
        weights = jnp.where(visible, jnp.exp(scores - row_max), 0.0)
        weight_sum = jnp.sum(weights, axis=1, keepdims=True)
        summed = jnp.dot(
            weights.astype(jnp.bfloat16), values, preferred_element_type=jnp.float32
        )
        attended = (summed / weight_sum).astype(jnp.bfloat16)
        for g in range(group):
            for p in range(blocks):
                for h in range(2):
                    first = g * rows + (p * 2 + h) * half
                    place = pl.multiple_of((h ^ core) * (blocks * half) + p * half, half)
                    out_ref[pl.ds(place, half), pl.ds((kv * group + g) * HEAD_DIM, HEAD_DIM)] = (
                        attended[first : first + half]
                    )


def attend(blocks, queries, key_halo, key_own, value_halo, value_own, start, end_halo, end_own):
    rows = queries.shape[0]
    return pl.pallas_call(
        functools.partial(attend_kernel, blocks),
        out_shape=jax.ShapeDtypeStruct(queries.shape, jnp.bfloat16),
        in_specs=vmem(8),
        out_specs=pl.BlockSpec(memory_space=pltpu.VMEM),
        compiler_params=params(),
        cost_estimate=cost(8 * rows * rows * queries.shape[1], 6 * queries.size),
    )(queries, key_halo, key_own, value_halo, value_own, start, end_halo, end_own)


def project_kernel(chunk_count, *refs):
    chunks, weight_ref, mine_ref, other_ref = refs[:-3], refs[-3], refs[-2], refs[-1]
    rows = chunks[0].shape[0]
    half = rows // 2
    if chunk_count == 1 and len(chunks) == 2:
        place = lax.axis_index("ctx")
        inner = (place == 1) | (place == 2)
        stacked = jnp.where(inner, chunks[0][...], chunks[1][...])
    else:
        stacked = jnp.concatenate([c[...] for c in chunks], axis=0)
    share = jnp.dot(stacked, weight_ref[...], preferred_element_type=jnp.float32).astype(
        jnp.bfloat16
    )
    for n in range(chunk_count):
        mine_ref[pl.ds(n * half, half), :] = share[n * rows : n * rows + half]
        other_ref[pl.ds(n * half, half), :] = share[n * rows + half : (n + 1) * rows]


def project(chunk_count, chunks, weight):
    rows = chunks[0].shape[0] * chunk_count // 2
    out = jax.ShapeDtypeStruct((rows, weight.shape[1]), jnp.bfloat16)
    return pl.pallas_call(
        functools.partial(project_kernel, chunk_count),
        out_shape=(out, out),
        in_specs=vmem(len(chunks) + 1),
        out_specs=(pl.BlockSpec(memory_space=pltpu.VMEM),) * 2,
        compiler_params=params(),
        cost_estimate=cost(4 * rows * weight.size, 2 * weight.size),
    )(*chunks, weight)


def total_kernel(*refs):
    terms, out_ref = refs[:-1], refs[-1]
    out_ref[...] = sum(t[...].astype(jnp.float32) for t in terms).astype(out_ref.dtype)


def total(terms):
    return pl.pallas_call(
        total_kernel,
        out_shape=jax.ShapeDtypeStruct(terms[0].shape, jnp.bfloat16),
        in_specs=vmem(len(terms)),
        out_specs=pl.BlockSpec(memory_space=pltpu.VMEM),
        compiler_params=params(),
        cost_estimate=cost(4 * terms[0].size, 10 * terms[0].size),
    )(*terms)


def pick_kernel(blocks, *refs):
    targets, refs = refs[:4], refs[4:]
    own_ref, pair_ref, late_refs, outs, held = refs[0], refs[1], refs[2:6], refs[6:10], refs[10]
    half = own_ref.shape[0] // blocks
    x = lax.axis_index("tp") // 2
    c = lax.axis_index("ctx")
    late = sum(t[...].astype(jnp.float32) for t in late_refs).astype(jnp.bfloat16)
    held[pl.ds(0, blocks * half), :] = own_ref[...]
    held[pl.ds(blocks * half, blocks * half), :] = pair_ref[pl.ds(blocks * half, blocks * half), :]
    held[pl.ds(2 * blocks * half, blocks * half), :] = late
    held[pl.ds(3 * blocks * half, blocks * half), :] = pair_ref[pl.ds(0, blocks * half), :]
    for k in range(4):
        wanted = (c ^ k) * blocks + x
        where = jnp.int32(0)
        for d in range(4):
            for p in range(blocks):
                where = jnp.where(targets[d][p] == wanted, d * blocks + p, where)
        outs[k][...] = held[pl.ds(pl.multiple_of(where * half, half), half), :]


def pick(blocks, targets, own, pair, late):
    rows, cols = own.shape
    out = jax.ShapeDtypeStruct((rows // blocks, cols), jnp.bfloat16)
    return pl.pallas_call(
        functools.partial(pick_kernel, blocks),
        out_shape=(out,) * 4,
        in_specs=smem(4) + vmem(6),
        out_specs=(pl.BlockSpec(memory_space=pltpu.VMEM),) * 4,
        scratch_shapes=[pltpu.VMEM((4 * rows, cols), jnp.bfloat16)],
        compiler_params=params(),
        cost_estimate=cost(4 * own.size, 20 * own.size),
    )(*targets, own, pair, *late)


def join_kernel(*refs):
    pieces, out_ref = refs[:-1], refs[-1]
    cols = pieces[0].shape[1]
    c = lax.axis_index("ctx")
    for k in range(4):
        out_ref[:, pl.ds(pl.multiple_of((c ^ k) * cols, cols), cols)] = pieces[k][...]


def join(pieces):
    rows, cols = pieces[0].shape
    return pl.pallas_call(
        join_kernel,
        out_shape=jax.ShapeDtypeStruct((rows, 4 * cols), jnp.bfloat16),
        in_specs=vmem(4),
        out_specs=pl.BlockSpec(memory_space=pltpu.VMEM),
        compiler_params=params(),
        cost_estimate=cost(0, 16 * pieces[0].size),
    )(*pieces)


def flip(array, axis, bits, members=(0, 1, 2, 3)):
    return lax.ppermute(array, axis, [(i, i ^ bits) for i in members])


def tp_total(mine, other):
    return mine, flip(other, "tp", 1), flip(mine, "tp", 2), flip(other, "tp", 3)


def small_ring(queries, key_rows, value_rows, doc_start, doc_end, block_target, out_weight):
    rows = queries.shape[0]
    blocks = block_target.shape[0]
    following = [(0, 1), (1, 2), (2, 3)]
    ends = doc_end.reshape(1, rows)
    key_halo = lax.ppermute(key_rows, "ctx", following)
    value_halo = lax.ppermute(value_rows, "ctx", following)
    end_halo = lax.ppermute(ends, "ctx", following)
    attended = attend(
        blocks,
        queries,
        key_halo,
        key_rows,
        value_halo,
        value_rows,
        doc_start.reshape(1, rows),
        end_halo,
        ends,
    )
    got_3 = flip(attended, "ctx", 3)
    got_1 = flip(attended, "ctx", 1)
    got_2_inner = lax.ppermute(attended, "ctx", [(0, 2), (3, 1)])
    got_2_outer = lax.ppermute(got_3, "ctx", [(1, 0), (2, 3)])
    targets = [block_target] + [flip(block_target, "ctx", d) for d in (1, 2, 3)]
    own = total(tp_total(*project(1, (attended,), out_weight)))
    pair = total(tp_total(*project(2, (got_3, got_1), out_weight)))
    late = tp_total(*project(1, (got_2_inner, got_2_outer), out_weight))
    kept, *sent = pick(blocks, targets, own, pair, late)
    return join([kept] + [flip(sent[k - 1], "ctx", k) for k in (1, 2, 3)])


def attend_block(soft_state, query_grid, query_pos, query_start, key_block, value_block, key_end, key_pos):
    running_max, weight_sum, weighted = soft_state
    scores = jnp.einsum(
        "rkgd,nkd->rkgn", query_grid, key_block, preferred_element_type=jnp.float32
    ) * HEAD_DIM ** (-0.5)
    visible = (
        (key_pos[None, :] <= query_pos[:, None])
        & (key_pos[None, :] >= query_start[:, None])
        & (key_end[None, :] > query_pos[:, None])
    )
    visible = visible[:, None, None, :]
    new_max = jnp.maximum(running_max, jnp.max(jnp.where(visible, scores, NEG_LARGE), axis=-1))
    weights = jnp.where(visible, jnp.exp(scores - new_max[..., None]), 0.0)
    fading = jnp.exp(running_max - new_max)
    weight_sum = weight_sum * fading + jnp.sum(weights, axis=-1)
    weighted = weighted * fading[..., None] + jnp.einsum(
        "rkgn,nkd->rkgd",
        weights.astype(jnp.bfloat16),
        value_block,
        preferred_element_type=jnp.float32,
    )
    return (new_max, weight_sum, weighted)


def attend_all(queries, query_pos, query_start, key_part, value_part, end_part):
    rows = queries.shape[0]
    key_count = key_part.shape[0]
    kv_here = key_part.shape[1] // HEAD_DIM
    query_grid = queries.reshape(rows, kv_here, -1, HEAD_DIM)
    block_len = math.gcd(key_count, 512)
    block_count = key_count // block_len
    items = (
        key_part.reshape(block_count, block_len, kv_here, HEAD_DIM),
        value_part.reshape(block_count, block_len, kv_here, HEAD_DIM),
        end_part.reshape(block_count, block_len),
        jnp.arange(key_count, dtype=jnp.int32).reshape(block_count, block_len),
    )
    start_state = (
        jnp.full(query_grid.shape[:3], NEG_LARGE, jnp.float32),
        jnp.zeros(query_grid.shape[:3], jnp.float32),
        jnp.zeros(query_grid.shape, jnp.float32),
    )

    def one_block(state, item):
        return attend_block(state, query_grid, query_pos, query_start, *item), None

    (_, weight_sum, weighted), _ = lax.scan(one_block, start_state, items)
    return (weighted / weight_sum[..., None]).astype(jnp.bfloat16).reshape(rows, -1)


def any_ring(queries, key_rows, value_rows, doc_start, doc_end, block_target, out_weight):
    rows = queries.shape[0]
    blocks = block_target.shape[0]
    block_rows = rows // blocks
    ctx_count = lax.axis_size("ctx")
    tp_count = lax.axis_size("tp")
    gather = functools.partial(lax.all_gather, axis_name="ctx", axis=0, tiled=True)
    query_pos = lax.axis_index("ctx") * rows + jnp.arange(rows, dtype=jnp.int32)
    attended = attend_all(
        queries, query_pos, doc_start, gather(key_rows), gather(value_rows), gather(doc_end)
    )
    targets = gather(block_target)
    source = jnp.zeros_like(targets).at[targets].set(jnp.arange(targets.size, dtype=jnp.int32))
    source_rows = (source[:, None] * block_rows + jnp.arange(block_rows, dtype=jnp.int32)).reshape(-1)
    balanced = jnp.take(gather(attended), source_rows, axis=0)
    share = jnp.dot(balanced, out_weight, preferred_element_type=jnp.float32).astype(jnp.bfloat16)
    share = share.reshape(ctx_count, tp_count, rows // tp_count, -1)
    summed = lax.psum_scatter(share, "tp", scatter_dimension=1, tiled=True)
    pieces = lax.all_to_all(summed[:, 0], "ctx", split_axis=0, concat_axis=0, tiled=True)
    return jnp.swapaxes(pieces, 0, 1).reshape(rows // tp_count, -1)


def shards(queries, key_rows, value_rows, doc_start, doc_end, block_target, out_weight):
    ctx_count, tp_count = lax.axis_size("ctx"), lax.axis_size("tp")
    rows, blocks = queries.shape[0], block_target.shape[0]
    longest = rows * ctx_count // 2 - rows
    near = longest <= rows and ctx_count == 4 and tp_count == 4 and blocks == 2
    plan = small_ring if near and rows % (4 * blocks * 2) == 0 else any_ring
    return plan(queries, key_rows, value_rows, doc_start, doc_end, block_target, out_weight)


def solution(mesh):
    in_specs = (
        P(("group", "ctx"), "tp"),
        P(("group", "ctx"), "tp"),
        P(("group", "ctx"), "tp"),
        P(("group", "ctx")),
        P(("group", "ctx")),
        P(("group", "ctx")),
        P("tp", "ctx"),
    )
    out_specs = P(("group", "ctx", "tp"), None)
    return jax.shard_map(shards, mesh=mesh, in_specs=in_specs, out_specs=out_specs, check_vma=False)
```

```python
import functools
import math

import jax
import jax.numpy as jnp
from jax import lax
from jax.experimental import pallas as pl
from jax.experimental.pallas import tpu as pltpu
from jax.sharding import PartitionSpec as P

HEAD_DIM = 128
NEG_LARGE = -1e30
END_PART = 128


def vmem(count):
    return [pl.BlockSpec(memory_space=pltpu.VMEM)] * count


def smem(count):
    return [pl.BlockSpec(memory_space=pltpu.SMEM)] * count


def params():
    return pltpu.CompilerParams(vmem_limit_bytes=16 * 1024 * 1024)


def cost(flops, moved):
    return pl.CostEstimate(flops=int(flops), bytes_accessed=int(moved), transcendentals=0)


def column(row):
    size = row.shape[1]
    return jnp.transpose(jnp.broadcast_to(row, (size, size)))


def pack_kernel(k_ref, v_ref, end_ref, message_ref):
    rows, width = k_ref.shape
    message_ref[pl.ds(0, rows), pl.ds(0, width)] = k_ref[...]
    message_ref[pl.ds(0, rows), pl.ds(width, width)] = v_ref[...]
    extra = message_ref.shape[0] - rows
    line = lax.broadcasted_iota(jnp.int32, (extra, rows), 0)
    ends = jnp.broadcast_to(end_ref[...], (extra, rows))
    parts = jnp.where(line == 0, ends // END_PART, jnp.where(line == 1, ends % END_PART, 0))
    message_ref[pl.ds(rows, extra), :] = jnp.zeros((extra, 2 * width), jnp.bfloat16)
    message_ref[pl.ds(rows, extra), pl.ds(0, rows)] = parts.astype(jnp.float32).astype(jnp.bfloat16)


def pack(key_rows, value_rows, ends):
    rows, width = key_rows.shape
    return pl.pallas_call(
        pack_kernel,
        out_shape=jax.ShapeDtypeStruct((rows + 16, 2 * width), jnp.bfloat16),
        in_specs=vmem(3),
        out_specs=pl.BlockSpec(memory_space=pltpu.VMEM),
        cost_estimate=cost(10**9, 8 * key_rows.size),
    )(key_rows, value_rows, ends)


def attend_kernel(blocks, q_ref, halo_ref, k_ref, v_ref, end_ref, st_ref, *refs):
    whole_ref, *out_refs = refs
    rows = q_ref.shape[0]
    width = k_ref.shape[1]
    kv_here = width // HEAD_DIM
    group = q_ref.shape[1] // HEAD_DIM // kv_here
    core = lax.axis_index("tp") % 2
    base = lax.axis_index("ctx") * rows
    half = rows // blocks // 2
    query_pos = base + lax.broadcasted_iota(jnp.int32, (rows, rows), 0)
    query_start = column(st_ref[...])
    parts = halo_ref[pl.ds(rows, 16), pl.ds(0, rows)].astype(jnp.float32).astype(jnp.int32)
    masks = []
    for shift, key_end in ((rows, parts[0:1] * END_PART + parts[1:2]), (0, end_ref[...])):
        key_pos = base - shift + lax.broadcasted_iota(jnp.int32, (rows, rows), 1)
        masks.append((key_pos <= query_pos) & (key_pos >= query_start) & (key_end > query_pos))
    visible = jnp.concatenate(masks, axis=1)
    visible = jnp.concatenate([visible] * group, axis=0)
    for kv in range(kv_here):
        keys, values = (
            jnp.concatenate(
                [
                    halo_ref[pl.ds(0, rows), pl.ds(first + kv * HEAD_DIM, HEAD_DIM)],
                    ref[:, pl.ds(kv * HEAD_DIM, HEAD_DIM)],
                ],
                axis=0,
            )
            for first, ref in ((0, k_ref), (width, v_ref))
        )
        query = jnp.concatenate(
            [q_ref[:, pl.ds((kv * group + g) * HEAD_DIM, HEAD_DIM)] for g in range(group)], axis=0
        )
        scores = (
            lax.dot_general(
                query, keys, (((1,), (1,)), ((), ())), preferred_element_type=jnp.float32
            )
            * HEAD_DIM**-0.5
        )
        row_max = jnp.max(jnp.where(visible, scores, NEG_LARGE), axis=1, keepdims=True)
        weights = jnp.where(visible, jnp.exp(scores - row_max), 0.0)
        weight_sum = jnp.sum(weights, axis=1, keepdims=True)
        summed = jnp.dot(
            weights.astype(jnp.bfloat16), values, preferred_element_type=jnp.float32
        )
        attended = (summed / weight_sum).astype(jnp.bfloat16)
        for g in range(group):
            for p in range(blocks):
                for h in range(2):
                    first = g * rows + (p * 2 + h) * half
                    place = pl.multiple_of((h ^ core) * half, half)
                    lanes = pl.ds((kv * group + g) * HEAD_DIM, HEAD_DIM)
                    out_refs[p][pl.ds(place, half), lanes] = attended[first : first + half]
                    whole_ref[pl.ds(p * 2 * half + place, half), lanes] = (
                        attended[first : first + half]
                    )


def attend(blocks, queries, halo, keys, values, end, start):
    rows, features = queries.shape
    out = jax.ShapeDtypeStruct((rows // blocks, features), jnp.bfloat16)
    return pl.pallas_call(
        functools.partial(attend_kernel, blocks),
        out_shape=(
            jax.ShapeDtypeStruct(queries.shape, jnp.bfloat16),
        )
        + (out,) * blocks,
        in_specs=vmem(6),
        out_specs=tuple(vmem(1 + blocks)),
        compiler_params=params(),
        cost_estimate=cost(8 * rows * rows * features, 6 * queries.size),
    )(queries, halo, keys, values, end, start)


def project_kernel(block_rows, *refs):
    chunks, weight_ref, mine_ref, other_ref = refs[:-3], refs[-3], refs[-2], refs[-1]
    half = block_rows // 2
    stacked = jnp.concatenate([c[...] for c in chunks], axis=0)
    share = jnp.dot(stacked, weight_ref[...], preferred_element_type=jnp.float32).astype(
        jnp.bfloat16
    )
    for n in range(share.shape[0] // block_rows):
        first = n * block_rows
        mine_ref[pl.ds(n * half, half), :] = share[first : first + half]
        other_ref[pl.ds(n * half, half), :] = share[first + half : first + block_rows]


def project(block_rows, chunks, weight):
    rows = sum(c.shape[0] for c in chunks)
    out = jax.ShapeDtypeStruct((rows // 2, weight.shape[1]), jnp.bfloat16)
    return pl.pallas_call(
        functools.partial(project_kernel, block_rows),
        out_shape=(out, out),
        in_specs=vmem(len(chunks) + 1),
        out_specs=tuple(vmem(2)),
        compiler_params=params(),
        cost_estimate=cost(2 * rows * weight.size, 2 * weight.size),
    )(*chunks, weight)


def total_kernel(*refs):
    terms, out_ref = refs[:-1], refs[-1]
    out_ref[...] = sum(t[...].astype(jnp.float32) for t in terms).astype(out_ref.dtype)


def total(terms):
    return pl.pallas_call(
        total_kernel,
        out_shape=jax.ShapeDtypeStruct(terms[0].shape, jnp.bfloat16),
        in_specs=vmem(len(terms)),
        out_specs=pl.BlockSpec(memory_space=pltpu.VMEM),
        compiler_params=params(),
        cost_estimate=cost(4 * terms[0].size, 10 * terms[0].size),
    )(*terms)


def pick_kernel(blocks, sums, late, half, *refs):
    (at_0, at_2, at_13), refs = refs[:3], refs[3:]
    done_refs, late_refs, outs, held = refs[:sums], refs[sums : sums + late], refs[-5:-1], refs[-1]
    x = lax.axis_index("tp") // 2
    c = lax.axis_index("ctx")
    first = 0
    for ref in done_refs:
        held[pl.ds(first, ref.shape[0]), :] = ref[...]
        first += ref.shape[0]
    total_late = sum(t[...].astype(jnp.float32) for t in late_refs)
    held[pl.ds(first, late_refs[0].shape[0]), :] = total_late.astype(held.dtype)
    for k in range(4):
        wanted = (c ^ k) * blocks + x
        where = jnp.int32(0)
        for p in range(blocks):
            for d, target in enumerate((at_0[p], at_13[p], at_2[p], at_13[blocks + p])):
                where = jnp.where(target == wanted, d * blocks + p, where)
        outs[k][...] = held[pl.ds(pl.multiple_of(where * half, half), half), :]


def pick(blocks, targets, sums, late):
    cols = late[0].shape[1]
    rows = sum(s.shape[0] for s in sums) + late[0].shape[0]
    half = rows // (4 * blocks)
    out = jax.ShapeDtypeStruct((half, cols), jnp.bfloat16)
    return pl.pallas_call(
        functools.partial(pick_kernel, blocks, len(sums), len(late), half),
        out_shape=(out,) * 4,
        in_specs=smem(3) + vmem(len(sums) + len(late)),
        out_specs=tuple(vmem(4)),
        scratch_shapes=[pltpu.VMEM((rows, cols), jnp.bfloat16)],
        compiler_params=params(),
        cost_estimate=cost(4 * rows * cols, 8 * rows * cols),
    )(*targets, *sums, *late)


def join_kernel(*refs):
    pieces, out_ref = refs[:-1], refs[-1]
    cols = pieces[0].shape[1]
    c = lax.axis_index("ctx")
    for k in range(4):
        out_ref[:, pl.ds(pl.multiple_of((c ^ k) * cols, cols), cols)] = pieces[k][...]


def join(pieces):
    rows, cols = pieces[0].shape
    return pl.pallas_call(
        join_kernel,
        out_shape=jax.ShapeDtypeStruct((rows, 4 * cols), jnp.bfloat16),
        in_specs=vmem(4),
        out_specs=pl.BlockSpec(memory_space=pltpu.VMEM),
        compiler_params=params(),
        cost_estimate=cost(0, 16 * pieces[0].size),
    )(*pieces)


def flip(array, axis, bits):
    return lax.ppermute(array, axis, [(i, i ^ bits) for i in range(4)])


def tp_terms(mine, other):
    return mine, flip(other, "tp", 1), flip(mine, "tp", 2), flip(other, "tp", 3)


def after(value, *others):
    return lax.optimization_barrier((value, *others))[0]


def small_ring(queries, key_rows, value_rows, doc_start, doc_end, block_target, out_weight):
    rows = queries.shape[0]
    blocks = block_target.shape[0]
    block_rows = rows // blocks
    end, start = doc_end.reshape(1, rows), doc_start.reshape(1, rows)
    message = pack(key_rows, value_rows, end)
    halo = lax.ppermute(message, "ctx", [(0, 1), (1, 2), (2, 3)])
    whole, first, second = attend(blocks, queries, halo, key_rows, value_rows, end, start)
    first_2, second_2 = flip(first, "ctx", 2), flip(second, "ctx", 2)
    whole_1 = flip(whole, "ctx", 1)
    first_3, second_3 = flip(first_2, "ctx", 1), flip(second_2, "ctx", 1)
    terms_a = tp_terms(*project(block_rows, (whole,), out_weight))
    target_2 = flip(after(block_target, terms_a[0]), "ctx", 2)
    target_13 = flip(jnp.concatenate([block_target, target_2]), "ctx", 1)
    terms_b = tp_terms(*project(block_rows, (whole_1, first_2), out_weight))
    sum_a = total(terms_a)
    second_2 = after(second_2, sum_a, target_13, terms_b[0])
    terms_c = tp_terms(*project(block_rows, (second_2, first_3), out_weight))
    sum_b = total(terms_b)
    second_3 = after(second_3, sum_b, terms_c[0])
    terms_d = tp_terms(*project(block_rows, (second_3,), out_weight))
    sum_c = total(terms_c)
    targets = (block_target, target_2, target_13)
    kept, *sent = pick(blocks, targets, (sum_a, sum_b, sum_c), terms_d)
    return join([kept] + [flip(sent[k - 1], "ctx", k) for k in (1, 2, 3)])


def attend_block(soft_state, query_grid, query_pos, query_start, key_block, value_block, key_end, key_pos):
    running_max, weight_sum, weighted = soft_state
    scores = jnp.einsum(
        "rkgd,nkd->rkgn", query_grid, key_block, preferred_element_type=jnp.float32
    ) * HEAD_DIM ** (-0.5)
    visible = (
        (key_pos[None, :] <= query_pos[:, None])
        & (key_pos[None, :] >= query_start[:, None])
        & (key_end[None, :] > query_pos[:, None])
    )
    visible = visible[:, None, None, :]
    new_max = jnp.maximum(running_max, jnp.max(jnp.where(visible, scores, NEG_LARGE), axis=-1))
    weights = jnp.where(visible, jnp.exp(scores - new_max[..., None]), 0.0)
    fading = jnp.exp(running_max - new_max)
    weight_sum = weight_sum * fading + jnp.sum(weights, axis=-1)
    weighted = weighted * fading[..., None] + jnp.einsum(
        "rkgn,nkd->rkgd",
        weights.astype(jnp.bfloat16),
        value_block,
        preferred_element_type=jnp.float32,
    )
    return (new_max, weight_sum, weighted)


def attend_all(queries, query_pos, query_start, key_part, value_part, end_part):
    rows = queries.shape[0]
    key_count = key_part.shape[0]
    kv_here = key_part.shape[1] // HEAD_DIM
    query_grid = queries.reshape(rows, kv_here, -1, HEAD_DIM)
    block_len = math.gcd(key_count, 512)
    block_count = key_count // block_len
    items = (
        key_part.reshape(block_count, block_len, kv_here, HEAD_DIM),
        value_part.reshape(block_count, block_len, kv_here, HEAD_DIM),
        end_part.reshape(block_count, block_len),
        jnp.arange(key_count, dtype=jnp.int32).reshape(block_count, block_len),
    )
    start_state = (
        jnp.full(query_grid.shape[:3], NEG_LARGE, jnp.float32),
        jnp.zeros(query_grid.shape[:3], jnp.float32),
        jnp.zeros(query_grid.shape, jnp.float32),
    )

    def one_block(state, item):
        return attend_block(state, query_grid, query_pos, query_start, *item), None

    (_, weight_sum, weighted), _ = lax.scan(one_block, start_state, items)
    return (weighted / weight_sum[..., None]).astype(jnp.bfloat16).reshape(rows, -1)


def any_ring(queries, key_rows, value_rows, doc_start, doc_end, block_target, out_weight):
    rows = queries.shape[0]
    blocks = block_target.shape[0]
    block_rows = rows // blocks
    ctx_count = lax.axis_size("ctx")
    tp_count = lax.axis_size("tp")
    gather = functools.partial(lax.all_gather, axis_name="ctx", axis=0, tiled=True)
    query_pos = lax.axis_index("ctx") * rows + jnp.arange(rows, dtype=jnp.int32)
    attended = attend_all(
        queries, query_pos, doc_start, gather(key_rows), gather(value_rows), gather(doc_end)
    )
    targets = gather(block_target)
    source = jnp.zeros_like(targets).at[targets].set(jnp.arange(targets.size, dtype=jnp.int32))
    source_rows = (source[:, None] * block_rows + jnp.arange(block_rows, dtype=jnp.int32)).reshape(-1)
    balanced = jnp.take(gather(attended), source_rows, axis=0)
    share = jnp.dot(balanced, out_weight, preferred_element_type=jnp.float32).astype(jnp.bfloat16)
    share = share.reshape(ctx_count, tp_count, rows // tp_count, -1)
    summed = lax.psum_scatter(share, "tp", scatter_dimension=1, tiled=True)
    pieces = lax.all_to_all(summed[:, 0], "ctx", split_axis=0, concat_axis=0, tiled=True)
    return jnp.swapaxes(pieces, 0, 1).reshape(rows // tp_count, -1)


def shards(queries, key_rows, value_rows, doc_start, doc_end, block_target, out_weight):
    ctx_count, tp_count = lax.axis_size("ctx"), lax.axis_size("tp")
    rows, blocks = queries.shape[0], block_target.shape[0]
    longest = rows * ctx_count // 2 - rows
    near = longest <= rows and ctx_count == 4 and tp_count == 4 and blocks == 2
    plan = small_ring if near and rows % (4 * blocks * 2) == 0 else any_ring
    return plan(queries, key_rows, value_rows, doc_start, doc_end, block_target, out_weight)


def solution(mesh):
    in_specs = (
        P(("group", "ctx"), "tp"),
        P(("group", "ctx"), "tp"),
        P(("group", "ctx"), "tp"),
        P(("group", "ctx")),
        P(("group", "ctx")),
        P(("group", "ctx")),
        P("tp", "ctx"),
    )
    out_specs = P(("group", "ctx", "tp"), None)
    return jax.shard_map(shards, mesh=mesh, in_specs=in_specs, out_specs=out_specs, check_vma=False)
```

```python
import functools
import math

import jax
import jax.numpy as jnp
from jax import lax
from jax.experimental import pallas as pl
from jax.experimental.pallas import tpu as pltpu
from jax.sharding import PartitionSpec as P

HEAD_DIM = 128
NEG_LARGE = -1e30
END_PART = 128


def vmem(count):
    return [pl.BlockSpec(memory_space=pltpu.VMEM)] * count


def smem(count):
    return [pl.BlockSpec(memory_space=pltpu.SMEM)] * count


def params():
    return pltpu.CompilerParams(vmem_limit_bytes=16 * 1024 * 1024)


def cost(flops, moved):
    return pl.CostEstimate(flops=int(flops), bytes_accessed=int(moved), transcendentals=0)


def column(row):
    size = row.shape[1]
    return jnp.transpose(jnp.broadcast_to(row, (size, size)))


def pack_kernel(k_ref, v_ref, end_ref, message_ref):
    rows, width = k_ref.shape
    message_ref[pl.ds(0, rows), pl.ds(0, width)] = k_ref[...]
    message_ref[pl.ds(0, rows), pl.ds(width, width)] = v_ref[...]
    extra = message_ref.shape[0] - rows
    line = lax.broadcasted_iota(jnp.int32, (extra, rows), 0)
    ends = jnp.broadcast_to(end_ref[...], (extra, rows))
    parts = jnp.where(line == 0, ends // END_PART, jnp.where(line == 1, ends % END_PART, 0))
    message_ref[pl.ds(rows, extra), :] = jnp.zeros((extra, 2 * width), jnp.bfloat16)
    message_ref[pl.ds(rows, extra), pl.ds(0, rows)] = parts.astype(jnp.float32).astype(jnp.bfloat16)


def pack(key_rows, value_rows, ends):
    rows, width = key_rows.shape
    return pl.pallas_call(
        pack_kernel,
        out_shape=jax.ShapeDtypeStruct((rows + 16, 2 * width), jnp.bfloat16),
        in_specs=vmem(3),
        out_specs=pl.BlockSpec(memory_space=pltpu.VMEM),
        cost_estimate=cost(10**9, 8 * key_rows.size),
    )(key_rows, value_rows, ends)


def attend_kernel(blocks, q_ref, halo_ref, k_ref, v_ref, end_ref, st_ref, *refs):
    whole_ref, *out_refs = refs
    rows = q_ref.shape[0]
    width = k_ref.shape[1]
    kv_here = width // HEAD_DIM
    group = q_ref.shape[1] // HEAD_DIM // kv_here
    core = lax.axis_index("tp") % 2
    base = lax.axis_index("ctx") * rows
    half = rows // blocks // 2
    query_pos = base + lax.broadcasted_iota(jnp.int32, (rows, rows), 0)
    query_start = column(st_ref[...])
    parts = halo_ref[pl.ds(rows, 16), pl.ds(0, rows)].astype(jnp.float32).astype(jnp.int32)
    masks = []
    for shift, key_end in ((rows, parts[0:1] * END_PART + parts[1:2]), (0, end_ref[...])):
        key_pos = base - shift + lax.broadcasted_iota(jnp.int32, (rows, rows), 1)
        masks.append((key_pos <= query_pos) & (key_pos >= query_start) & (key_end > query_pos))
    visible = jnp.concatenate(masks, axis=1)
    visible = jnp.concatenate([visible] * group, axis=0)
    for kv in range(kv_here):
        keys, values = (
            jnp.concatenate(
                [
                    halo_ref[pl.ds(0, rows), pl.ds(first + kv * HEAD_DIM, HEAD_DIM)],
                    ref[:, pl.ds(kv * HEAD_DIM, HEAD_DIM)],
                ],
                axis=0,
            )
            for first, ref in ((0, k_ref), (width, v_ref))
        )
        query = jnp.concatenate(
            [q_ref[:, pl.ds((kv * group + g) * HEAD_DIM, HEAD_DIM)] for g in range(group)], axis=0
        )
        scores = (
            lax.dot_general(
                query, keys, (((1,), (1,)), ((), ())), preferred_element_type=jnp.float32
            )
            * HEAD_DIM**-0.5
        )
        row_max = jnp.max(jnp.where(visible, scores, NEG_LARGE), axis=1, keepdims=True)
        weights = jnp.where(visible, jnp.exp(scores - row_max), 0.0)
        weight_sum = jnp.sum(weights, axis=1, keepdims=True)
        summed = jnp.dot(
            weights.astype(jnp.bfloat16), values, preferred_element_type=jnp.float32
        )
        attended = (summed / weight_sum).astype(jnp.bfloat16)
        for g in range(group):
            for p in range(blocks):
                for h in range(2):
                    first = g * rows + (p * 2 + h) * half
                    place = pl.multiple_of((h ^ core) * half, half)
                    lanes = pl.ds((kv * group + g) * HEAD_DIM, HEAD_DIM)
                    out_refs[p][pl.ds(place, half), lanes] = attended[first : first + half]
                    whole_ref[pl.ds(p * 2 * half + place, half), lanes] = (
                        attended[first : first + half]
                    )


def attend(blocks, queries, halo, keys, values, end, start):
    rows, features = queries.shape
    out = jax.ShapeDtypeStruct((rows // blocks, features), jnp.bfloat16)
    return pl.pallas_call(
        functools.partial(attend_kernel, blocks),
        out_shape=(
            jax.ShapeDtypeStruct(queries.shape, jnp.bfloat16),
        )
        + (out,) * blocks,
        in_specs=vmem(6),
        out_specs=tuple(vmem(1 + blocks)),
        compiler_params=params(),
        cost_estimate=cost(8 * rows * rows * features, 6 * queries.size),
    )(queries, halo, keys, values, end, start)


def project_kernel(block_rows, *refs):
    chunks, weight_ref, mine_ref, other_ref = refs[:-3], refs[-3], refs[-2], refs[-1]
    half = block_rows // 2
    stacked = jnp.concatenate([c[...] for c in chunks], axis=0)
    share = jnp.dot(stacked, weight_ref[...], preferred_element_type=jnp.float32).astype(
        jnp.bfloat16
    )
    for n in range(share.shape[0] // block_rows):
        first = n * block_rows
        mine_ref[pl.ds(n * half, half), :] = share[first : first + half]
        other_ref[pl.ds(n * half, half), :] = share[first + half : first + block_rows]


def project(block_rows, chunks, weight):
    rows = sum(c.shape[0] for c in chunks)
    out = jax.ShapeDtypeStruct((rows // 2, weight.shape[1]), jnp.bfloat16)
    return pl.pallas_call(
        functools.partial(project_kernel, block_rows),
        out_shape=(out, out),
        in_specs=vmem(len(chunks) + 1),
        out_specs=tuple(vmem(2)),
        compiler_params=params(),
        cost_estimate=cost(2 * rows * weight.size, 2 * weight.size),
    )(*chunks, weight)


def total_kernel(*refs):
    terms, out_ref = refs[:-1], refs[-1]
    out_ref[...] = sum(t[...].astype(jnp.float32) for t in terms).astype(out_ref.dtype)


def total(terms):
    return pl.pallas_call(
        total_kernel,
        out_shape=jax.ShapeDtypeStruct(terms[0].shape, jnp.bfloat16),
        in_specs=vmem(len(terms)),
        out_specs=pl.BlockSpec(memory_space=pltpu.VMEM),
        compiler_params=params(),
        cost_estimate=cost(4 * terms[0].size, 10 * terms[0].size),
    )(*terms)


def pick_kernel(blocks, half, own_ref, far_ref, *refs):
    sums, outs = refs[:-4], refs[-4:]
    x = lax.axis_index("tp") // 2
    c = lax.axis_index("ctx")
    order = (0, 1, 2, 3, 4, 6, 5, 7)
    pieces = [r[pl.ds(n, half), :] for r in sums for n in range(0, r.shape[0], half)]
    targets = jnp.concatenate([own_ref[...], far_ref[...]], axis=1)
    for k in range(4):
        wanted = (c ^ k) * blocks + x
        piece = pieces[0]
        for n in range(1, len(pieces)):
            column_of = order[n]
            here = jnp.broadcast_to(targets[:, column_of : column_of + 1] == wanted, piece.shape)
            piece = jnp.where(here, pieces[n], piece)
        outs[k][...] = piece


def pick(blocks, own_targets, far_targets, sums):
    rows, cols = sum(s.shape[0] for s in sums), sums[0].shape[1]
    half = rows // (4 * blocks)
    out = jax.ShapeDtypeStruct((half, cols), jnp.bfloat16)
    return pl.pallas_call(
        functools.partial(pick_kernel, blocks, half),
        out_shape=(out,) * 4,
        in_specs=vmem(2 + len(sums)),
        out_specs=tuple(vmem(4)),
        compiler_params=params(),
        cost_estimate=cost(4 * rows * cols, 8 * rows * cols),
    )(own_targets, far_targets, *sums)


def join_kernel(*refs):
    pieces, out_ref = refs[:-1], refs[-1]
    cols = pieces[0].shape[1]
    c = lax.axis_index("ctx")
    for k in range(4):
        out_ref[:, pl.ds(pl.multiple_of((c ^ k) * cols, cols), cols)] = pieces[k][...]


def join(pieces):
    rows, cols = pieces[0].shape
    return pl.pallas_call(
        join_kernel,
        out_shape=jax.ShapeDtypeStruct((rows, 4 * cols), jnp.bfloat16),
        in_specs=vmem(4),
        out_specs=pl.BlockSpec(memory_space=pltpu.VMEM),
        compiler_params=params(),
        cost_estimate=cost(0, 16 * pieces[0].size),
    )(*pieces)


def flip(array, axis, bits):
    return lax.ppermute(array, axis, [(i, i ^ bits) for i in range(4)])


def core_total(mine, other):
    return total((mine, flip(other, "tp", 1)))


def chip_total(share):
    return total((share, flip(share, "tp", 2)))


def after(value, *others):
    return lax.optimization_barrier((value, *others))[0]


def small_ring(queries, key_rows, value_rows, doc_start, doc_end, block_target, out_weight):
    rows = queries.shape[0]
    blocks = block_target.shape[0]
    block_rows = rows // blocks
    end, start = doc_end.reshape(1, rows), doc_start.reshape(1, rows)
    message = pack(key_rows, value_rows, end)
    halo = lax.ppermute(message, "ctx", [(0, 1), (1, 2), (2, 3)])
    whole, first, second = attend(blocks, queries, halo, key_rows, value_rows, end, start)
    first_2, second_2 = flip(first, "ctx", 2), flip(second, "ctx", 2)
    whole_1 = flip(whole, "ctx", 1)
    target_1 = flip(after(block_target, whole), "ctx", 1)
    own_targets = jnp.concatenate([block_target, target_1]).reshape(1, 2 * blocks)
    share_a = core_total(*project(block_rows, (whole,), out_weight))
    first_2 = after(first_2, share_a, own_targets)
    first_3, second_3 = flip(first_2, "ctx", 1), flip(second_2, "ctx", 1)
    sum_a = chip_total(share_a)
    second_2 = after(second_2, sum_a)
    share_b = core_total(*project(block_rows, (whole_1, first_2, first_3, second_2), out_weight))
    far_targets = flip(own_targets, "ctx", 2)
    second_3 = after(second_3, share_b, far_targets)
    share_c = core_total(*project(block_rows, (second_3,), out_weight))
    sum_b = chip_total(share_b)
    sum_c = chip_total(share_c)
    kept, *sent = pick(blocks, own_targets, far_targets, (sum_a, sum_b, sum_c))
    got = [flip(sent[k - 1], "ctx", k) for k in (3, 2, 1)]
    return join([kept] + got[::-1])


def attend_block(soft_state, query_grid, query_pos, query_start, key_block, value_block, key_end, key_pos):
    running_max, weight_sum, weighted = soft_state
    scores = jnp.einsum(
        "rkgd,nkd->rkgn", query_grid, key_block, preferred_element_type=jnp.float32
    ) * HEAD_DIM ** (-0.5)
    visible = (
        (key_pos[None, :] <= query_pos[:, None])
        & (key_pos[None, :] >= query_start[:, None])
        & (key_end[None, :] > query_pos[:, None])
    )
    visible = visible[:, None, None, :]
    new_max = jnp.maximum(running_max, jnp.max(jnp.where(visible, scores, NEG_LARGE), axis=-1))
    weights = jnp.where(visible, jnp.exp(scores - new_max[..., None]), 0.0)
    fading = jnp.exp(running_max - new_max)
    weight_sum = weight_sum * fading + jnp.sum(weights, axis=-1)
    weighted = weighted * fading[..., None] + jnp.einsum(
        "rkgn,nkd->rkgd",
        weights.astype(jnp.bfloat16),
        value_block,
        preferred_element_type=jnp.float32,
    )
    return (new_max, weight_sum, weighted)


def attend_all(queries, query_pos, query_start, key_part, value_part, end_part):
    rows = queries.shape[0]
    key_count = key_part.shape[0]
    kv_here = key_part.shape[1] // HEAD_DIM
    query_grid = queries.reshape(rows, kv_here, -1, HEAD_DIM)
    block_len = math.gcd(key_count, 512)
    block_count = key_count // block_len
    items = (
        key_part.reshape(block_count, block_len, kv_here, HEAD_DIM),
        value_part.reshape(block_count, block_len, kv_here, HEAD_DIM),
        end_part.reshape(block_count, block_len),
        jnp.arange(key_count, dtype=jnp.int32).reshape(block_count, block_len),
    )
    start_state = (
        jnp.full(query_grid.shape[:3], NEG_LARGE, jnp.float32),
        jnp.zeros(query_grid.shape[:3], jnp.float32),
        jnp.zeros(query_grid.shape, jnp.float32),
    )

    def one_block(state, item):
        return attend_block(state, query_grid, query_pos, query_start, *item), None

    (_, weight_sum, weighted), _ = lax.scan(one_block, start_state, items)
    return (weighted / weight_sum[..., None]).astype(jnp.bfloat16).reshape(rows, -1)


def any_ring(queries, key_rows, value_rows, doc_start, doc_end, block_target, out_weight):
    rows = queries.shape[0]
    blocks = block_target.shape[0]
    block_rows = rows // blocks
    ctx_count = lax.axis_size("ctx")
    tp_count = lax.axis_size("tp")
    gather = functools.partial(lax.all_gather, axis_name="ctx", axis=0, tiled=True)
    query_pos = lax.axis_index("ctx") * rows + jnp.arange(rows, dtype=jnp.int32)
    attended = attend_all(
        queries, query_pos, doc_start, gather(key_rows), gather(value_rows), gather(doc_end)
    )
    targets = gather(block_target)
    source = jnp.zeros_like(targets).at[targets].set(jnp.arange(targets.size, dtype=jnp.int32))
    source_rows = (source[:, None] * block_rows + jnp.arange(block_rows, dtype=jnp.int32)).reshape(-1)
    balanced = jnp.take(gather(attended), source_rows, axis=0)
    share = jnp.dot(balanced, out_weight, preferred_element_type=jnp.float32).astype(jnp.bfloat16)
    share = share.reshape(ctx_count, tp_count, rows // tp_count, -1)
    summed = lax.psum_scatter(share, "tp", scatter_dimension=1, tiled=True)
    pieces = lax.all_to_all(summed[:, 0], "ctx", split_axis=0, concat_axis=0, tiled=True)
    return jnp.swapaxes(pieces, 0, 1).reshape(rows // tp_count, -1)


def shards(queries, key_rows, value_rows, doc_start, doc_end, block_target, out_weight):
    ctx_count, tp_count = lax.axis_size("ctx"), lax.axis_size("tp")
    rows, blocks = queries.shape[0], block_target.shape[0]
    longest = rows * ctx_count // 2 - rows
    near = longest <= rows and ctx_count == 4 and tp_count == 4 and blocks == 2
    plan = small_ring if near and rows % (4 * blocks * 2) == 0 else any_ring
    return plan(queries, key_rows, value_rows, doc_start, doc_end, block_target, out_weight)


def solution(mesh):
    in_specs = (
        P(("group", "ctx"), "tp"),
        P(("group", "ctx"), "tp"),
        P(("group", "ctx"), "tp"),
        P(("group", "ctx")),
        P(("group", "ctx")),
        P(("group", "ctx")),
        P("tp", "ctx"),
    )
    out_specs = P(("group", "ctx", "tp"), None)
    return jax.shard_map(shards, mesh=mesh, in_specs=in_specs, out_specs=out_specs, check_vma=False)
```

```python
import functools
import math

import jax
import jax.numpy as jnp
from jax import lax
from jax.experimental import pallas as pl
from jax.experimental.pallas import tpu as pltpu
from jax.sharding import PartitionSpec as P

HEAD_DIM = 128
NEG_LARGE = -1e30
END_PART = 128


def vmem(count):
    return [pl.BlockSpec(memory_space=pltpu.VMEM)] * count


def smem(count):
    return [pl.BlockSpec(memory_space=pltpu.SMEM)] * count


def params():
    return pltpu.CompilerParams(vmem_limit_bytes=16 * 1024 * 1024)


def cost(flops, moved):
    return pl.CostEstimate(flops=int(flops), bytes_accessed=int(moved), transcendentals=0)


def column(row):
    size = row.shape[1]
    return jnp.transpose(jnp.broadcast_to(row, (size, size)))


def pack_kernel(k_ref, v_ref, end_ref, message_ref):
    rows, width = k_ref.shape
    message_ref[pl.ds(0, rows), pl.ds(0, width)] = k_ref[...]
    message_ref[pl.ds(0, rows), pl.ds(width, width)] = v_ref[...]
    extra = message_ref.shape[0] - rows
    line = lax.broadcasted_iota(jnp.int32, (extra, rows), 0)
    ends = jnp.broadcast_to(end_ref[...], (extra, rows))
    parts = jnp.where(line == 0, ends // END_PART, jnp.where(line == 1, ends % END_PART, 0))
    message_ref[pl.ds(rows, extra), :] = jnp.zeros((extra, 2 * width), jnp.bfloat16)
    message_ref[pl.ds(rows, extra), pl.ds(0, rows)] = parts.astype(jnp.float32).astype(jnp.bfloat16)


def pack(key_rows, value_rows, ends):
    rows, width = key_rows.shape
    return pl.pallas_call(
        pack_kernel,
        out_shape=jax.ShapeDtypeStruct((rows + 16, 2 * width), jnp.bfloat16),
        in_specs=vmem(3),
        out_specs=pl.BlockSpec(memory_space=pltpu.VMEM),
        cost_estimate=cost(10**9, 8 * key_rows.size),
    )(key_rows, value_rows, ends)


def attend_kernel(blocks, q_ref, halo_ref, k_ref, v_ref, end_ref, st_ref, *refs):
    whole_ref, *out_refs = refs
    rows = q_ref.shape[0]
    width = k_ref.shape[1]
    kv_here = width // HEAD_DIM
    group = q_ref.shape[1] // HEAD_DIM // kv_here
    core = lax.axis_index("tp") % 2
    base = lax.axis_index("ctx") * rows
    half = rows // blocks // 2
    query_pos = base + lax.broadcasted_iota(jnp.int32, (rows, rows), 0)
    query_start = column(st_ref[...])
    parts = halo_ref[pl.ds(rows, 16), pl.ds(0, rows)].astype(jnp.float32).astype(jnp.int32)
    masks = []
    for shift, key_end in ((rows, parts[0:1] * END_PART + parts[1:2]), (0, end_ref[...])):
        key_pos = base - shift + lax.broadcasted_iota(jnp.int32, (rows, rows), 1)
        masks.append((key_pos <= query_pos) & (key_pos >= query_start) & (key_end > query_pos))
    visible = jnp.concatenate(masks, axis=1)
    visible = jnp.concatenate([visible] * group, axis=0)
    for kv in range(kv_here):
        keys, values = (
            jnp.concatenate(
                [
                    halo_ref[pl.ds(0, rows), pl.ds(first + kv * HEAD_DIM, HEAD_DIM)],
                    ref[:, pl.ds(kv * HEAD_DIM, HEAD_DIM)],
                ],
                axis=0,
            )
            for first, ref in ((0, k_ref), (width, v_ref))
        )
        query = jnp.concatenate(
            [q_ref[:, pl.ds((kv * group + g) * HEAD_DIM, HEAD_DIM)] for g in range(group)], axis=0
        )
        scores = (
            lax.dot_general(
                query, keys, (((1,), (1,)), ((), ())), preferred_element_type=jnp.float32
            )
            * HEAD_DIM**-0.5
        )
        row_max = jnp.max(jnp.where(visible, scores, NEG_LARGE), axis=1, keepdims=True)
        weights = jnp.where(visible, jnp.exp(scores - row_max), 0.0)
        weight_sum = jnp.sum(weights, axis=1, keepdims=True)
        summed = jnp.dot(
            weights.astype(jnp.bfloat16), values, preferred_element_type=jnp.float32
        )
        attended = (summed / weight_sum).astype(jnp.bfloat16)
        for g in range(group):
            for p in range(blocks):
                for h in range(2):
                    first = g * rows + (p * 2 + h) * half
                    place = pl.multiple_of((h ^ core) * half, half)
                    lanes = pl.ds((kv * group + g) * HEAD_DIM, HEAD_DIM)
                    out_refs[p][pl.ds(place, half), lanes] = attended[first : first + half]
                    whole_ref[pl.ds(p * 2 * half + place, half), lanes] = (
                        attended[first : first + half]
                    )


def attend(blocks, queries, halo, keys, values, end, start):
    rows, features = queries.shape
    out = jax.ShapeDtypeStruct((rows // blocks, features), jnp.bfloat16)
    return pl.pallas_call(
        functools.partial(attend_kernel, blocks),
        out_shape=(
            jax.ShapeDtypeStruct(queries.shape, jnp.bfloat16),
        )
        + (out,) * blocks,
        in_specs=vmem(6),
        out_specs=tuple(vmem(1 + blocks)),
        compiler_params=params(),
        cost_estimate=cost(8 * rows * rows * features, 6 * queries.size),
    )(queries, halo, keys, values, end, start)


def project_kernel(block_rows, *refs):
    chunks, weight_ref, mine_ref, other_ref = refs[:-3], refs[-3], refs[-2], refs[-1]
    half = block_rows // 2
    stacked = jnp.concatenate([c[...] for c in chunks], axis=0)
    share = jnp.dot(stacked, weight_ref[...], preferred_element_type=jnp.float32).astype(
        jnp.bfloat16
    )
    for n in range(share.shape[0] // block_rows):
        first = n * block_rows
        mine_ref[pl.ds(n * half, half), :] = share[first : first + half]
        other_ref[pl.ds(n * half, half), :] = share[first + half : first + block_rows]


def project(block_rows, chunks, weight):
    rows = sum(c.shape[0] for c in chunks)
    out = jax.ShapeDtypeStruct((rows // 2, weight.shape[1]), jnp.bfloat16)
    return pl.pallas_call(
        functools.partial(project_kernel, block_rows),
        out_shape=(out, out),
        in_specs=vmem(len(chunks) + 1),
        out_specs=tuple(vmem(2)),
        compiler_params=params(),
        cost_estimate=cost(2 * rows * weight.size, 2 * weight.size),
    )(*chunks, weight)


def total_kernel(*refs):
    terms, out_ref = refs[:-1], refs[-1]
    out_ref[...] = sum(t[...].astype(jnp.float32) for t in terms).astype(out_ref.dtype)


def total(terms):
    return pl.pallas_call(
        total_kernel,
        out_shape=jax.ShapeDtypeStruct(terms[0].shape, jnp.bfloat16),
        in_specs=vmem(len(terms)),
        out_specs=pl.BlockSpec(memory_space=pltpu.VMEM),
        compiler_params=params(),
        cost_estimate=cost(4 * terms[0].size, 10 * terms[0].size),
    )(*terms)


def pick_kernel(blocks, half, own_ref, far_ref, *refs):
    sums, outs = refs[:-4], refs[-4:]
    x = lax.axis_index("tp") // 2
    c = lax.axis_index("ctx")
    order = (0, 1, 2, 3, 4, 6, 5, 7)
    pieces = [r[pl.ds(n, half), :] for r in sums for n in range(0, r.shape[0], half)]
    targets = jnp.concatenate([own_ref[...], far_ref[...]], axis=1)
    for k in range(4):
        wanted = (c ^ k) * blocks + x
        piece = pieces[0]
        for n in range(1, len(pieces)):
            column_of = order[n]
            here = jnp.broadcast_to(targets[:, column_of : column_of + 1] == wanted, piece.shape)
            piece = jnp.where(here, pieces[n], piece)
        outs[k][...] = piece


def pick(blocks, own_targets, far_targets, sums):
    rows, cols = sum(s.shape[0] for s in sums), sums[0].shape[1]
    half = rows // (4 * blocks)
    out = jax.ShapeDtypeStruct((half, cols), jnp.bfloat16)
    return pl.pallas_call(
        functools.partial(pick_kernel, blocks, half),
        out_shape=(out,) * 4,
        in_specs=vmem(2 + len(sums)),
        out_specs=tuple(vmem(4)),
        compiler_params=params(),
        cost_estimate=cost(4 * rows * cols, 8 * rows * cols),
    )(own_targets, far_targets, *sums)


def join_kernel(*refs):
    pieces, out_ref = refs[:-1], refs[-1]
    cols = pieces[0].shape[1]
    c = lax.axis_index("ctx")
    for k in range(4):
        out_ref[:, pl.ds(pl.multiple_of((c ^ k) * cols, cols), cols)] = pieces[k][...]


def join(pieces):
    rows, cols = pieces[0].shape
    return pl.pallas_call(
        join_kernel,
        out_shape=jax.ShapeDtypeStruct((rows, 4 * cols), jnp.bfloat16),
        in_specs=vmem(4),
        out_specs=pl.BlockSpec(memory_space=pltpu.VMEM),
        compiler_params=params(),
        cost_estimate=cost(0, 16 * pieces[0].size),
    )(*pieces)


def flip(array, axis, bits):
    return lax.ppermute(array, axis, [(i, i ^ bits) for i in range(4)])


def core_total(mine, other):
    return total((mine, flip(other, "tp", 1)))


def chip_total(share):
    return total((share, flip(share, "tp", 2)))


def after(value, *others):
    return lax.optimization_barrier((value, *others))[0]


def small_ring(queries, key_rows, value_rows, doc_start, doc_end, block_target, out_weight):
    rows = queries.shape[0]
    blocks = block_target.shape[0]
    block_rows = rows // blocks
    end, start = doc_end.reshape(1, rows), doc_start.reshape(1, rows)
    message = pack(key_rows, value_rows, end)
    halo = lax.ppermute(message, "ctx", [(0, 1), (1, 2), (2, 3)])
    target_1 = flip(after(block_target, message), "ctx", 1)
    own_targets = jnp.concatenate([block_target, target_1]).reshape(1, 2 * blocks)
    start = after(start, own_targets)
    whole, first, second = attend(blocks, queries, halo, key_rows, value_rows, end, start)
    first_2, second_2 = flip(first, "ctx", 2), flip(second, "ctx", 2)
    whole_1 = flip(whole, "ctx", 1)
    far_targets = flip(own_targets, "ctx", 2)
    share_a = core_total(*project(block_rows, (whole,), out_weight))
    first_2 = after(first_2, share_a)
    first_3, second_3 = flip(first_2, "ctx", 1), flip(second_2, "ctx", 1)
    sum_a = chip_total(share_a)
    second_2 = after(second_2, sum_a, far_targets)
    share_b = core_total(*project(block_rows, (whole_1, first_2, first_3, second_2), out_weight))
    second_3 = after(second_3, share_b)
    share_c = core_total(*project(block_rows, (second_3,), out_weight))
    sum_b = chip_total(share_b)
    sum_c = chip_total(share_c)
    kept, *sent = pick(blocks, own_targets, far_targets, (sum_a, sum_b, sum_c))
    got = [flip(sent[k - 1], "ctx", k) for k in (3, 2, 1)]
    return join([kept] + got[::-1])


def attend_block(soft_state, query_grid, query_pos, query_start, key_block, value_block, key_end, key_pos):
    running_max, weight_sum, weighted = soft_state
    scores = jnp.einsum(
        "rkgd,nkd->rkgn", query_grid, key_block, preferred_element_type=jnp.float32
    ) * HEAD_DIM ** (-0.5)
    visible = (
        (key_pos[None, :] <= query_pos[:, None])
        & (key_pos[None, :] >= query_start[:, None])
        & (key_end[None, :] > query_pos[:, None])
    )
    visible = visible[:, None, None, :]
    new_max = jnp.maximum(running_max, jnp.max(jnp.where(visible, scores, NEG_LARGE), axis=-1))
    weights = jnp.where(visible, jnp.exp(scores - new_max[..., None]), 0.0)
    fading = jnp.exp(running_max - new_max)
    weight_sum = weight_sum * fading + jnp.sum(weights, axis=-1)
    weighted = weighted * fading[..., None] + jnp.einsum(
        "rkgn,nkd->rkgd",
        weights.astype(jnp.bfloat16),
        value_block,
        preferred_element_type=jnp.float32,
    )
    return (new_max, weight_sum, weighted)


def attend_all(queries, query_pos, query_start, key_part, value_part, end_part):
    rows = queries.shape[0]
    key_count = key_part.shape[0]
    kv_here = key_part.shape[1] // HEAD_DIM
    query_grid = queries.reshape(rows, kv_here, -1, HEAD_DIM)
    block_len = math.gcd(key_count, 512)
    block_count = key_count // block_len
    items = (
        key_part.reshape(block_count, block_len, kv_here, HEAD_DIM),
        value_part.reshape(block_count, block_len, kv_here, HEAD_DIM),
        end_part.reshape(block_count, block_len),
        jnp.arange(key_count, dtype=jnp.int32).reshape(block_count, block_len),
    )
    start_state = (
        jnp.full(query_grid.shape[:3], NEG_LARGE, jnp.float32),
        jnp.zeros(query_grid.shape[:3], jnp.float32),
        jnp.zeros(query_grid.shape, jnp.float32),
    )

    def one_block(state, item):
        return attend_block(state, query_grid, query_pos, query_start, *item), None

    (_, weight_sum, weighted), _ = lax.scan(one_block, start_state, items)
    return (weighted / weight_sum[..., None]).astype(jnp.bfloat16).reshape(rows, -1)


def any_ring(queries, key_rows, value_rows, doc_start, doc_end, block_target, out_weight):
    rows = queries.shape[0]
    blocks = block_target.shape[0]
    block_rows = rows // blocks
    ctx_count = lax.axis_size("ctx")
    tp_count = lax.axis_size("tp")
    gather = functools.partial(lax.all_gather, axis_name="ctx", axis=0, tiled=True)
    query_pos = lax.axis_index("ctx") * rows + jnp.arange(rows, dtype=jnp.int32)
    attended = attend_all(
        queries, query_pos, doc_start, gather(key_rows), gather(value_rows), gather(doc_end)
    )
    targets = gather(block_target)
    source = jnp.zeros_like(targets).at[targets].set(jnp.arange(targets.size, dtype=jnp.int32))
    source_rows = (source[:, None] * block_rows + jnp.arange(block_rows, dtype=jnp.int32)).reshape(-1)
    balanced = jnp.take(gather(attended), source_rows, axis=0)
    share = jnp.dot(balanced, out_weight, preferred_element_type=jnp.float32).astype(jnp.bfloat16)
    share = share.reshape(ctx_count, tp_count, rows // tp_count, -1)
    summed = lax.psum_scatter(share, "tp", scatter_dimension=1, tiled=True)
    pieces = lax.all_to_all(summed[:, 0], "ctx", split_axis=0, concat_axis=0, tiled=True)
    return jnp.swapaxes(pieces, 0, 1).reshape(rows // tp_count, -1)


def shards(queries, key_rows, value_rows, doc_start, doc_end, block_target, out_weight):
    ctx_count, tp_count = lax.axis_size("ctx"), lax.axis_size("tp")
    rows, blocks = queries.shape[0], block_target.shape[0]
    longest = rows * ctx_count // 2 - rows
    near = longest <= rows and ctx_count == 4 and tp_count == 4 and blocks == 2
    plan = small_ring if near and rows % (4 * blocks * 2) == 0 else any_ring
    return plan(queries, key_rows, value_rows, doc_start, doc_end, block_target, out_weight)


def solution(mesh):
    in_specs = (
        P(("group", "ctx"), "tp"),
        P(("group", "ctx"), "tp"),
        P(("group", "ctx"), "tp"),
        P(("group", "ctx")),
        P(("group", "ctx")),
        P(("group", "ctx")),
        P("tp", "ctx"),
    )
    out_specs = P(("group", "ctx", "tp"), None)
    return jax.shard_map(shards, mesh=mesh, in_specs=in_specs, out_specs=out_specs, check_vma=False)
```

```python
import functools
import math

import jax
import jax.numpy as jnp
from jax import lax
from jax.experimental import pallas as pl
from jax.experimental.pallas import tpu as pltpu
from jax.sharding import PartitionSpec as P

HEAD_DIM = 128
NEG_LARGE = -1e30
END_PART = 128


def vmem(count):
    return [pl.BlockSpec(memory_space=pltpu.VMEM)] * count


def smem(count):
    return [pl.BlockSpec(memory_space=pltpu.SMEM)] * count


def params():
    return pltpu.CompilerParams(vmem_limit_bytes=16 * 1024 * 1024)


def cost(flops, moved):
    return pl.CostEstimate(flops=int(flops), bytes_accessed=int(moved), transcendentals=0)


def column(row):
    size = row.shape[1]
    return jnp.transpose(jnp.broadcast_to(row, (size, size)))


def pack_kernel(k_ref, v_ref, end_ref, message_ref):
    rows, width = k_ref.shape
    message_ref[pl.ds(0, rows), pl.ds(0, width)] = k_ref[...]
    message_ref[pl.ds(0, rows), pl.ds(width, width)] = v_ref[...]
    extra = message_ref.shape[0] - rows
    line = lax.broadcasted_iota(jnp.int32, (extra, rows), 0)
    ends = jnp.broadcast_to(end_ref[...], (extra, rows))
    parts = jnp.where(line == 0, ends // END_PART, jnp.where(line == 1, ends % END_PART, 0))
    message_ref[pl.ds(rows, extra), :] = jnp.zeros((extra, 2 * width), jnp.bfloat16)
    message_ref[pl.ds(rows, extra), pl.ds(0, rows)] = parts.astype(jnp.float32).astype(jnp.bfloat16)


def pack(key_rows, value_rows, ends):
    rows, width = key_rows.shape
    return pl.pallas_call(
        pack_kernel,
        out_shape=jax.ShapeDtypeStruct((rows + 16, 2 * width), jnp.bfloat16),
        in_specs=vmem(3),
        out_specs=pl.BlockSpec(memory_space=pltpu.VMEM),
        cost_estimate=cost(10**9, 8 * key_rows.size),
    )(key_rows, value_rows, ends)


def attend_kernel(blocks, q_ref, halo_ref, k_ref, v_ref, end_ref, st_ref, *refs):
    whole_ref, *out_refs = refs
    rows = q_ref.shape[0]
    width = k_ref.shape[1]
    kv_here = width // HEAD_DIM
    group = q_ref.shape[1] // HEAD_DIM // kv_here
    core = lax.axis_index("tp") % 2
    base = lax.axis_index("ctx") * rows
    half = rows // blocks // 2
    query_pos = base + lax.broadcasted_iota(jnp.int32, (rows, rows), 0)
    query_start = column(st_ref[...])
    parts = halo_ref[pl.ds(rows, 16), pl.ds(0, rows)].astype(jnp.float32).astype(jnp.int32)
    masks = []
    for shift, key_end in ((rows, parts[0:1] * END_PART + parts[1:2]), (0, end_ref[...])):
        key_pos = base - shift + lax.broadcasted_iota(jnp.int32, (rows, rows), 1)
        masks.append((key_pos <= query_pos) & (key_pos >= query_start) & (key_end > query_pos))
    visible = jnp.concatenate(masks, axis=1)
    visible = jnp.concatenate([visible] * group, axis=0)
    for kv in range(kv_here):
        keys, values = (
            jnp.concatenate(
                [
                    halo_ref[pl.ds(0, rows), pl.ds(first + kv * HEAD_DIM, HEAD_DIM)],
                    ref[:, pl.ds(kv * HEAD_DIM, HEAD_DIM)],
                ],
                axis=0,
            )
            for first, ref in ((0, k_ref), (width, v_ref))
        )
        query = jnp.concatenate(
            [q_ref[:, pl.ds((kv * group + g) * HEAD_DIM, HEAD_DIM)] for g in range(group)], axis=0
        )
        scores = (
            lax.dot_general(
                query, keys, (((1,), (1,)), ((), ())), preferred_element_type=jnp.float32
            )
            * HEAD_DIM**-0.5
        )
        row_max = jnp.max(jnp.where(visible, scores, NEG_LARGE), axis=1, keepdims=True)
        weights = jnp.where(visible, jnp.exp(scores - row_max), 0.0)
        weight_sum = jnp.sum(weights, axis=1, keepdims=True)
        summed = jnp.dot(
            weights.astype(jnp.bfloat16), values, preferred_element_type=jnp.float32
        )
        attended = (summed / weight_sum).astype(jnp.bfloat16)
        for g in range(group):
            for p in range(blocks):
                for h in range(2):
                    first = g * rows + (p * 2 + h) * half
                    place = pl.multiple_of((h ^ core) * half, half)
                    lanes = pl.ds((kv * group + g) * HEAD_DIM, HEAD_DIM)
                    out_refs[p][pl.ds(place, half), lanes] = attended[first : first + half]
                    whole_ref[pl.ds(p * 2 * half + place, half), lanes] = (
                        attended[first : first + half]
                    )


def attend(blocks, queries, halo, keys, values, end, start):
    rows, features = queries.shape
    out = jax.ShapeDtypeStruct((rows // blocks, features), jnp.bfloat16)
    return pl.pallas_call(
        functools.partial(attend_kernel, blocks),
        out_shape=(
            jax.ShapeDtypeStruct(queries.shape, jnp.bfloat16),
        )
        + (out,) * blocks,
        in_specs=vmem(6),
        out_specs=tuple(vmem(1 + blocks)),
        compiler_params=params(),
        cost_estimate=cost(8 * rows * rows * features, 6 * queries.size),
    )(queries, halo, keys, values, end, start)


def project_kernel(block_rows, *refs):
    chunks, weight_ref, mine_ref, other_ref = refs[:-3], refs[-3], refs[-2], refs[-1]
    half = block_rows // 2
    stacked = jnp.concatenate([c[...] for c in chunks], axis=0)
    share = jnp.dot(stacked, weight_ref[...], preferred_element_type=jnp.float32).astype(
        jnp.bfloat16
    )
    for n in range(share.shape[0] // block_rows):
        first = n * block_rows
        mine_ref[pl.ds(n * half, half), :] = share[first : first + half]
        other_ref[pl.ds(n * half, half), :] = share[first + half : first + block_rows]


def project(block_rows, chunks, weight):
    rows = sum(c.shape[0] for c in chunks)
    out = jax.ShapeDtypeStruct((rows // 2, weight.shape[1]), jnp.bfloat16)
    return pl.pallas_call(
        functools.partial(project_kernel, block_rows),
        out_shape=(out, out),
        in_specs=vmem(len(chunks) + 1),
        out_specs=tuple(vmem(2)),
        compiler_params=params(),
        cost_estimate=cost(2 * rows * weight.size, 2 * weight.size),
    )(*chunks, weight)


def total_kernel(*refs):
    terms, out_ref = refs[:-1], refs[-1]
    out_ref[...] = sum(t[...].astype(jnp.float32) for t in terms).astype(out_ref.dtype)


def total(terms):
    return pl.pallas_call(
        total_kernel,
        out_shape=jax.ShapeDtypeStruct(terms[0].shape, jnp.bfloat16),
        in_specs=vmem(len(terms)),
        out_specs=pl.BlockSpec(memory_space=pltpu.VMEM),
        compiler_params=params(),
        cost_estimate=cost(4 * terms[0].size, 10 * terms[0].size),
    )(*terms)


def pick_kernel(blocks, half, own_ref, far_ref, *refs):
    sums, outs = refs[:-4], refs[-4:]
    x = lax.axis_index("tp") // 2
    c = lax.axis_index("ctx")
    order = (0, 1, 2, 3, 4, 6, 5, 7)
    pieces = [r[pl.ds(n, half), :] for r in sums for n in range(0, r.shape[0], half)]
    targets = jnp.concatenate([own_ref[...], far_ref[...]], axis=1)
    for k in range(4):
        wanted = (c ^ k) * blocks + x
        piece = pieces[0]
        for n in range(1, len(pieces)):
            column_of = order[n]
            here = jnp.broadcast_to(targets[:, column_of : column_of + 1] == wanted, piece.shape)
            piece = jnp.where(here, pieces[n], piece)
        outs[k][...] = piece


def pick(blocks, own_targets, far_targets, sums):
    rows, cols = sum(s.shape[0] for s in sums), sums[0].shape[1]
    half = rows // (4 * blocks)
    out = jax.ShapeDtypeStruct((half, cols), jnp.bfloat16)
    return pl.pallas_call(
        functools.partial(pick_kernel, blocks, half),
        out_shape=(out,) * 4,
        in_specs=vmem(2 + len(sums)),
        out_specs=tuple(vmem(4)),
        compiler_params=params(),
        cost_estimate=cost(4 * rows * cols, 8 * rows * cols),
    )(own_targets, far_targets, *sums)


def join_kernel(*refs):
    pieces, out_ref = refs[:-1], refs[-1]
    cols = pieces[0].shape[1]
    c = lax.axis_index("ctx")
    for k in range(4):
        out_ref[:, pl.ds(pl.multiple_of((c ^ k) * cols, cols), cols)] = pieces[k][...]


def join(pieces):
    rows, cols = pieces[0].shape
    return pl.pallas_call(
        join_kernel,
        out_shape=jax.ShapeDtypeStruct((rows, 4 * cols), jnp.bfloat16),
        in_specs=vmem(4),
        out_specs=pl.BlockSpec(memory_space=pltpu.VMEM),
        compiler_params=params(),
        cost_estimate=cost(0, 16 * pieces[0].size),
    )(*pieces)


def flip(array, axis, bits):
    return lax.ppermute(array, axis, [(i, i ^ bits) for i in range(4)])


def core_total(mine, other):
    return total((mine, flip(other, "tp", 1)))


def chip_total(share):
    return total((share, flip(share, "tp", 2)))


def after(value, *others):
    return lax.optimization_barrier((value, *others))[0]


def small_ring(queries, key_rows, value_rows, doc_start, doc_end, block_target, out_weight):
    rows = queries.shape[0]
    blocks = block_target.shape[0]
    block_rows = rows // blocks
    end, start = doc_end.reshape(1, rows), doc_start.reshape(1, rows)
    message = pack(key_rows, value_rows, end)
    halo = lax.ppermute(message, "ctx", [(0, 1), (1, 2), (2, 3)])
    early = after(block_target, message)
    target_1, target_2 = flip(early, "ctx", 1), flip(early, "ctx", 2)
    own_targets = jnp.concatenate([block_target, target_1]).reshape(1, 2 * blocks)
    start = after(start, own_targets)
    whole, first, second = attend(blocks, queries, halo, key_rows, value_rows, end, start)
    first_2, second_2 = flip(first, "ctx", 2), flip(second, "ctx", 2)
    whole_1 = flip(whole, "ctx", 1)
    target_3 = flip(after(target_2, whole), "ctx", 1)
    far_targets = jnp.concatenate([target_2, target_3]).reshape(1, 2 * blocks)
    share_a = core_total(*project(block_rows, (whole,), out_weight))
    first_2 = after(first_2, share_a)
    first_3, second_3 = flip(first_2, "ctx", 1), flip(second_2, "ctx", 1)
    sum_a = chip_total(share_a)
    second_2 = after(second_2, sum_a, far_targets)
    share_b = core_total(*project(block_rows, (whole_1, first_2, first_3, second_2), out_weight))
    second_3 = after(second_3, share_b)
    share_c = core_total(*project(block_rows, (second_3,), out_weight))
    sum_b = chip_total(share_b)
    sum_c = chip_total(share_c)
    kept, *sent = pick(blocks, own_targets, far_targets, (sum_a, sum_b, sum_c))
    got = [flip(sent[k - 1], "ctx", k) for k in (3, 2, 1)]
    return join([kept] + got[::-1])


def attend_block(soft_state, query_grid, query_pos, query_start, key_block, value_block, key_end, key_pos):
    running_max, weight_sum, weighted = soft_state
    scores = jnp.einsum(
        "rkgd,nkd->rkgn", query_grid, key_block, preferred_element_type=jnp.float32
    ) * HEAD_DIM ** (-0.5)
    visible = (
        (key_pos[None, :] <= query_pos[:, None])
        & (key_pos[None, :] >= query_start[:, None])
        & (key_end[None, :] > query_pos[:, None])
    )
    visible = visible[:, None, None, :]
    new_max = jnp.maximum(running_max, jnp.max(jnp.where(visible, scores, NEG_LARGE), axis=-1))
    weights = jnp.where(visible, jnp.exp(scores - new_max[..., None]), 0.0)
    fading = jnp.exp(running_max - new_max)
    weight_sum = weight_sum * fading + jnp.sum(weights, axis=-1)
    weighted = weighted * fading[..., None] + jnp.einsum(
        "rkgn,nkd->rkgd",
        weights.astype(jnp.bfloat16),
        value_block,
        preferred_element_type=jnp.float32,
    )
    return (new_max, weight_sum, weighted)


def attend_all(queries, query_pos, query_start, key_part, value_part, end_part):
    rows = queries.shape[0]
    key_count = key_part.shape[0]
    kv_here = key_part.shape[1] // HEAD_DIM
    query_grid = queries.reshape(rows, kv_here, -1, HEAD_DIM)
    block_len = math.gcd(key_count, 512)
    block_count = key_count // block_len
    items = (
        key_part.reshape(block_count, block_len, kv_here, HEAD_DIM),
        value_part.reshape(block_count, block_len, kv_here, HEAD_DIM),
        end_part.reshape(block_count, block_len),
        jnp.arange(key_count, dtype=jnp.int32).reshape(block_count, block_len),
    )
    start_state = (
        jnp.full(query_grid.shape[:3], NEG_LARGE, jnp.float32),
        jnp.zeros(query_grid.shape[:3], jnp.float32),
        jnp.zeros(query_grid.shape, jnp.float32),
    )

    def one_block(state, item):
        return attend_block(state, query_grid, query_pos, query_start, *item), None

    (_, weight_sum, weighted), _ = lax.scan(one_block, start_state, items)
    return (weighted / weight_sum[..., None]).astype(jnp.bfloat16).reshape(rows, -1)


def any_ring(queries, key_rows, value_rows, doc_start, doc_end, block_target, out_weight):
    rows = queries.shape[0]
    blocks = block_target.shape[0]
    block_rows = rows // blocks
    ctx_count = lax.axis_size("ctx")
    tp_count = lax.axis_size("tp")
    gather = functools.partial(lax.all_gather, axis_name="ctx", axis=0, tiled=True)
    query_pos = lax.axis_index("ctx") * rows + jnp.arange(rows, dtype=jnp.int32)
    attended = attend_all(
        queries, query_pos, doc_start, gather(key_rows), gather(value_rows), gather(doc_end)
    )
    targets = gather(block_target)
    source = jnp.zeros_like(targets).at[targets].set(jnp.arange(targets.size, dtype=jnp.int32))
    source_rows = (source[:, None] * block_rows + jnp.arange(block_rows, dtype=jnp.int32)).reshape(-1)
    balanced = jnp.take(gather(attended), source_rows, axis=0)
    share = jnp.dot(balanced, out_weight, preferred_element_type=jnp.float32).astype(jnp.bfloat16)
    share = share.reshape(ctx_count, tp_count, rows // tp_count, -1)
    summed = lax.psum_scatter(share, "tp", scatter_dimension=1, tiled=True)
    pieces = lax.all_to_all(summed[:, 0], "ctx", split_axis=0, concat_axis=0, tiled=True)
    return jnp.swapaxes(pieces, 0, 1).reshape(rows // tp_count, -1)


def shards(queries, key_rows, value_rows, doc_start, doc_end, block_target, out_weight):
    ctx_count, tp_count = lax.axis_size("ctx"), lax.axis_size("tp")
    rows, blocks = queries.shape[0], block_target.shape[0]
    longest = rows * ctx_count // 2 - rows
    near = longest <= rows and ctx_count == 4 and tp_count == 4 and blocks == 2
    plan = small_ring if near and rows % (4 * blocks * 2) == 0 else any_ring
    return plan(queries, key_rows, value_rows, doc_start, doc_end, block_target, out_weight)


def solution(mesh):
    in_specs = (
        P(("group", "ctx"), "tp"),
        P(("group", "ctx"), "tp"),
        P(("group", "ctx"), "tp"),
        P(("group", "ctx")),
        P(("group", "ctx")),
        P(("group", "ctx")),
        P("tp", "ctx"),
    )
    out_specs = P(("group", "ctx", "tp"), None)
    return jax.shard_map(shards, mesh=mesh, in_specs=in_specs, out_specs=out_specs, check_vma=False)
```

```python
import functools
import math

import jax
import jax.numpy as jnp
from jax import lax
from jax.experimental import pallas as pl
from jax.experimental.pallas import tpu as pltpu
from jax.sharding import PartitionSpec as P

HEAD_DIM = 128
NEG_LARGE = -1e30
END_PART = 128


def vmem(count):
    return [pl.BlockSpec(memory_space=pltpu.VMEM)] * count


def smem(count):
    return [pl.BlockSpec(memory_space=pltpu.SMEM)] * count


def params():
    return pltpu.CompilerParams(vmem_limit_bytes=16 * 1024 * 1024)


def cost(flops, moved):
    return pl.CostEstimate(flops=int(flops), bytes_accessed=int(moved), transcendentals=0)


def column(row):
    size = row.shape[1]
    return jnp.transpose(jnp.broadcast_to(row, (size, size)))


def pack_kernel(k_ref, v_ref, end_ref, message_ref):
    rows, width = k_ref.shape
    message_ref[pl.ds(0, rows), pl.ds(0, width)] = k_ref[...]
    message_ref[pl.ds(0, rows), pl.ds(width, width)] = v_ref[...]
    extra = message_ref.shape[0] - rows
    line = lax.broadcasted_iota(jnp.int32, (extra, rows), 0)
    ends = jnp.broadcast_to(end_ref[...], (extra, rows))
    parts = jnp.where(line == 0, ends // END_PART, jnp.where(line == 1, ends % END_PART, 0))
    message_ref[pl.ds(rows, extra), :] = jnp.zeros((extra, 2 * width), jnp.bfloat16)
    message_ref[pl.ds(rows, extra), pl.ds(0, rows)] = parts.astype(jnp.float32).astype(jnp.bfloat16)


def pack(key_rows, value_rows, ends):
    rows, width = key_rows.shape
    return pl.pallas_call(
        pack_kernel,
        out_shape=jax.ShapeDtypeStruct((rows + 16, 2 * width), jnp.bfloat16),
        in_specs=vmem(3),
        out_specs=pl.BlockSpec(memory_space=pltpu.VMEM),
        cost_estimate=cost(10**9, 8 * key_rows.size),
    )(key_rows, value_rows, ends)


def attend_kernel(blocks, q_ref, halo_ref, k_ref, v_ref, end_ref, st_ref, *refs):
    whole_ref, *out_refs = refs
    rows = q_ref.shape[0]
    width = k_ref.shape[1]
    kv_here = width // HEAD_DIM
    group = q_ref.shape[1] // HEAD_DIM // kv_here
    core = lax.axis_index("tp") % 2
    base = lax.axis_index("ctx") * rows
    half = rows // blocks // 2
    query_pos = base + lax.broadcasted_iota(jnp.int32, (rows, rows), 0)
    query_start = column(st_ref[...])
    parts = halo_ref[pl.ds(rows, 16), pl.ds(0, rows)].astype(jnp.float32).astype(jnp.int32)
    masks = []
    for shift, key_end in ((rows, parts[0:1] * END_PART + parts[1:2]), (0, end_ref[...])):
        key_pos = base - shift + lax.broadcasted_iota(jnp.int32, (rows, rows), 1)
        masks.append((key_pos <= query_pos) & (key_pos >= query_start) & (key_end > query_pos))
    visible = jnp.concatenate(masks, axis=1)
    visible = jnp.concatenate([visible] * group, axis=0)
    for kv in range(kv_here):
        keys, values = (
            jnp.concatenate(
                [
                    halo_ref[pl.ds(0, rows), pl.ds(first + kv * HEAD_DIM, HEAD_DIM)],
                    ref[:, pl.ds(kv * HEAD_DIM, HEAD_DIM)],
                ],
                axis=0,
            )
            for first, ref in ((0, k_ref), (width, v_ref))
        )
        query = jnp.concatenate(
            [q_ref[:, pl.ds((kv * group + g) * HEAD_DIM, HEAD_DIM)] for g in range(group)], axis=0
        )
        scores = (
            lax.dot_general(
                query, keys, (((1,), (1,)), ((), ())), preferred_element_type=jnp.float32
            )
            * HEAD_DIM**-0.5
        )
        row_max = jnp.max(jnp.where(visible, scores, NEG_LARGE), axis=1, keepdims=True)
        weights = jnp.where(visible, jnp.exp(scores - row_max), 0.0)
        weight_sum = jnp.sum(weights, axis=1, keepdims=True)
        summed = jnp.dot(
            weights.astype(jnp.bfloat16), values, preferred_element_type=jnp.float32
        )
        attended = (summed / weight_sum).astype(jnp.bfloat16)
        for g in range(group):
            for p in range(blocks):
                for h in range(2):
                    first = g * rows + (p * 2 + h) * half
                    place = pl.multiple_of((h ^ core) * half, half)
                    lanes = pl.ds((kv * group + g) * HEAD_DIM, HEAD_DIM)
                    out_refs[p][pl.ds(place, half), lanes] = attended[first : first + half]
                    whole_ref[pl.ds(p * 2 * half + place, half), lanes] = (
                        attended[first : first + half]
                    )


def attend(blocks, queries, halo, keys, values, end, start):
    rows, features = queries.shape
    out = jax.ShapeDtypeStruct((rows // blocks, features), jnp.bfloat16)
    return pl.pallas_call(
        functools.partial(attend_kernel, blocks),
        out_shape=(
            jax.ShapeDtypeStruct(queries.shape, jnp.bfloat16),
        )
        + (out,) * blocks,
        in_specs=vmem(6),
        out_specs=tuple(vmem(1 + blocks)),
        compiler_params=params(),
        cost_estimate=cost(8 * rows * rows * features, 6 * queries.size),
    )(queries, halo, keys, values, end, start)


def project_kernel(block_rows, *refs):
    chunks, weight_ref, mine_ref, other_ref = refs[:-3], refs[-3], refs[-2], refs[-1]
    half = block_rows // 2
    stacked = jnp.concatenate([c[...] for c in chunks], axis=0)
    share = jnp.dot(stacked, weight_ref[...], preferred_element_type=jnp.float32).astype(
        jnp.bfloat16
    )
    for n in range(share.shape[0] // block_rows):
        first = n * block_rows
        mine_ref[pl.ds(n * half, half), :] = share[first : first + half]
        other_ref[pl.ds(n * half, half), :] = share[first + half : first + block_rows]


def project(block_rows, chunks, weight):
    rows = sum(c.shape[0] for c in chunks)
    out = jax.ShapeDtypeStruct((rows // 2, weight.shape[1]), jnp.bfloat16)
    return pl.pallas_call(
        functools.partial(project_kernel, block_rows),
        out_shape=(out, out),
        in_specs=vmem(len(chunks) + 1),
        out_specs=tuple(vmem(2)),
        compiler_params=params(),
        cost_estimate=cost(2 * rows * weight.size, 2 * weight.size),
    )(*chunks, weight)


def total_kernel(*refs):
    terms, out_ref = refs[:-1], refs[-1]
    out_ref[...] = sum(t[...].astype(jnp.float32) for t in terms).astype(out_ref.dtype)


def total(terms):
    return pl.pallas_call(
        total_kernel,
        out_shape=jax.ShapeDtypeStruct(terms[0].shape, jnp.bfloat16),
        in_specs=vmem(len(terms)),
        out_specs=pl.BlockSpec(memory_space=pltpu.VMEM),
        compiler_params=params(),
        cost_estimate=cost(4 * terms[0].size, 10 * terms[0].size),
    )(*terms)


def pick_kernel(blocks, half, even_ref, odd_ref, *refs):
    sums, outs = refs[:-4], refs[-4:]
    x = lax.axis_index("tp") // 2
    c = lax.axis_index("ctx")
    order = (0, 1, 4, 5, 2, 6, 3, 7)
    pieces = [r[pl.ds(n, half), :] for r in sums for n in range(0, r.shape[0], half)]
    targets = jnp.concatenate([even_ref[...], odd_ref[...]], axis=1)
    for k in range(4):
        wanted = (c ^ k) * blocks + x
        piece = pieces[0]
        for n in range(1, len(pieces)):
            column_of = order[n]
            here = jnp.broadcast_to(targets[:, column_of : column_of + 1] == wanted, piece.shape)
            piece = jnp.where(here, pieces[n], piece)
        outs[k][...] = piece


def pick(blocks, even_targets, odd_targets, sums):
    rows, cols = sum(s.shape[0] for s in sums), sums[0].shape[1]
    half = rows // (4 * blocks)
    out = jax.ShapeDtypeStruct((half, cols), jnp.bfloat16)
    return pl.pallas_call(
        functools.partial(pick_kernel, blocks, half),
        out_shape=(out,) * 4,
        in_specs=vmem(2 + len(sums)),
        out_specs=tuple(vmem(4)),
        compiler_params=params(),
        cost_estimate=cost(4 * rows * cols, 8 * rows * cols),
    )(even_targets, odd_targets, *sums)


def join_kernel(*refs):
    pieces, out_ref = refs[:-1], refs[-1]
    cols = pieces[0].shape[1]
    c = lax.axis_index("ctx")
    for k in range(4):
        out_ref[:, pl.ds(pl.multiple_of((c ^ k) * cols, cols), cols)] = pieces[k][...]


def join(pieces):
    rows, cols = pieces[0].shape
    return pl.pallas_call(
        join_kernel,
        out_shape=jax.ShapeDtypeStruct((rows, 4 * cols), jnp.bfloat16),
        in_specs=vmem(4),
        out_specs=pl.BlockSpec(memory_space=pltpu.VMEM),
        compiler_params=params(),
        cost_estimate=cost(0, 16 * pieces[0].size),
    )(*pieces)


def flip(array, axis, bits):
    return lax.ppermute(array, axis, [(i, i ^ bits) for i in range(4)])


def core_total(mine, other):
    return total((mine, flip(other, "tp", 1)))


def chip_total(share):
    return total((share, flip(share, "tp", 2)))


def after(value, *others):
    return lax.optimization_barrier((value, *others))[0]


def small_ring(queries, key_rows, value_rows, doc_start, doc_end, block_target, out_weight):
    rows = queries.shape[0]
    blocks = block_target.shape[0]
    block_rows = rows // blocks
    end, start = doc_end.reshape(1, rows), doc_start.reshape(1, rows)
    message = pack(key_rows, value_rows, end)
    halo = lax.ppermute(message, "ctx", [(0, 1), (1, 2), (2, 3)])
    target_2 = flip(after(block_target, message), "ctx", 2)
    even_targets = jnp.concatenate([block_target, target_2]).reshape(1, 2 * blocks)
    halo = after(halo, target_2)
    whole, first, second = attend(blocks, queries, halo, key_rows, value_rows, end, start)
    whole_1 = flip(whole, "ctx", 1)
    first_2, second_2 = flip(first, "ctx", 2), flip(second, "ctx", 2)
    odd_targets = flip(even_targets, "ctx", 1)
    share_a = core_total(*project(block_rows, (whole, whole_1), out_weight))
    first_3, second_3 = flip(first_2, "ctx", 1), flip(second_2, "ctx", 1)
    sum_a = chip_total(share_a)
    second_2 = after(second_2, share_a, odd_targets)
    share_b = core_total(*project(block_rows, (first_2, first_3, second_2), out_weight))
    second_3 = after(second_3, share_b)
    share_c = core_total(*project(block_rows, (second_3,), out_weight))
    sum_b = chip_total(share_b)
    sum_c = chip_total(share_c)
    kept, *sent = pick(blocks, even_targets, odd_targets, (sum_a, sum_b, sum_c))
    got = [flip(sent[k - 1], "ctx", k) for k in (3, 2, 1)]
    return join([kept] + got[::-1])


def attend_block(soft_state, query_grid, query_pos, query_start, key_block, value_block, key_end, key_pos):
    running_max, weight_sum, weighted = soft_state
    scores = jnp.einsum(
        "rkgd,nkd->rkgn", query_grid, key_block, preferred_element_type=jnp.float32
    ) * HEAD_DIM ** (-0.5)
    visible = (
        (key_pos[None, :] <= query_pos[:, None])
        & (key_pos[None, :] >= query_start[:, None])
        & (key_end[None, :] > query_pos[:, None])
    )
    visible = visible[:, None, None, :]
    new_max = jnp.maximum(running_max, jnp.max(jnp.where(visible, scores, NEG_LARGE), axis=-1))
    weights = jnp.where(visible, jnp.exp(scores - new_max[..., None]), 0.0)
    fading = jnp.exp(running_max - new_max)
    weight_sum = weight_sum * fading + jnp.sum(weights, axis=-1)
    weighted = weighted * fading[..., None] + jnp.einsum(
        "rkgn,nkd->rkgd",
        weights.astype(jnp.bfloat16),
        value_block,
        preferred_element_type=jnp.float32,
    )
    return (new_max, weight_sum, weighted)


def attend_all(queries, query_pos, query_start, key_part, value_part, end_part):
    rows = queries.shape[0]
    key_count = key_part.shape[0]
    kv_here = key_part.shape[1] // HEAD_DIM
    query_grid = queries.reshape(rows, kv_here, -1, HEAD_DIM)
    block_len = math.gcd(key_count, 512)
    block_count = key_count // block_len
    items = (
        key_part.reshape(block_count, block_len, kv_here, HEAD_DIM),
        value_part.reshape(block_count, block_len, kv_here, HEAD_DIM),
        end_part.reshape(block_count, block_len),
        jnp.arange(key_count, dtype=jnp.int32).reshape(block_count, block_len),
    )
    start_state = (
        jnp.full(query_grid.shape[:3], NEG_LARGE, jnp.float32),
        jnp.zeros(query_grid.shape[:3], jnp.float32),
        jnp.zeros(query_grid.shape, jnp.float32),
    )

    def one_block(state, item):
        return attend_block(state, query_grid, query_pos, query_start, *item), None

    (_, weight_sum, weighted), _ = lax.scan(one_block, start_state, items)
    return (weighted / weight_sum[..., None]).astype(jnp.bfloat16).reshape(rows, -1)


def any_ring(queries, key_rows, value_rows, doc_start, doc_end, block_target, out_weight):
    rows = queries.shape[0]
    blocks = block_target.shape[0]
    block_rows = rows // blocks
    ctx_count = lax.axis_size("ctx")
    tp_count = lax.axis_size("tp")
    gather = functools.partial(lax.all_gather, axis_name="ctx", axis=0, tiled=True)
    query_pos = lax.axis_index("ctx") * rows + jnp.arange(rows, dtype=jnp.int32)
    attended = attend_all(
        queries, query_pos, doc_start, gather(key_rows), gather(value_rows), gather(doc_end)
    )
    targets = gather(block_target)
    source = jnp.zeros_like(targets).at[targets].set(jnp.arange(targets.size, dtype=jnp.int32))
    source_rows = (source[:, None] * block_rows + jnp.arange(block_rows, dtype=jnp.int32)).reshape(-1)
    balanced = jnp.take(gather(attended), source_rows, axis=0)
    share = jnp.dot(balanced, out_weight, preferred_element_type=jnp.float32).astype(jnp.bfloat16)
    share = share.reshape(ctx_count, tp_count, rows // tp_count, -1)
    summed = lax.psum_scatter(share, "tp", scatter_dimension=1, tiled=True)
    pieces = lax.all_to_all(summed[:, 0], "ctx", split_axis=0, concat_axis=0, tiled=True)
    return jnp.swapaxes(pieces, 0, 1).reshape(rows // tp_count, -1)


def shards(queries, key_rows, value_rows, doc_start, doc_end, block_target, out_weight):
    ctx_count, tp_count = lax.axis_size("ctx"), lax.axis_size("tp")
    rows, blocks = queries.shape[0], block_target.shape[0]
    longest = rows * ctx_count // 2 - rows
    near = longest <= rows and ctx_count == 4 and tp_count == 4 and blocks == 2
    plan = small_ring if near and rows % (4 * blocks * 2) == 0 else any_ring
    return plan(queries, key_rows, value_rows, doc_start, doc_end, block_target, out_weight)


def solution(mesh):
    in_specs = (
        P(("group", "ctx"), "tp"),
        P(("group", "ctx"), "tp"),
        P(("group", "ctx"), "tp"),
        P(("group", "ctx")),
        P(("group", "ctx")),
        P(("group", "ctx")),
        P("tp", "ctx"),
    )
    out_specs = P(("group", "ctx", "tp"), None)
    return jax.shard_map(shards, mesh=mesh, in_specs=in_specs, out_specs=out_specs, check_vma=False)
```

```python
import functools
import math

import jax
import jax.numpy as jnp
from jax import lax
from jax.experimental import pallas as pl
from jax.experimental.pallas import tpu as pltpu
from jax.sharding import PartitionSpec as P

HEAD_DIM = 128
NEG_LARGE = -1e30
END_PART = 128


def vmem(count):
    return [pl.BlockSpec(memory_space=pltpu.VMEM)] * count


def smem(count):
    return [pl.BlockSpec(memory_space=pltpu.SMEM)] * count


def params():
    return pltpu.CompilerParams(vmem_limit_bytes=16 * 1024 * 1024)


def cost(flops, moved):
    return pl.CostEstimate(flops=int(flops), bytes_accessed=int(moved), transcendentals=0)


def column(row):
    size = row.shape[1]
    return jnp.transpose(jnp.broadcast_to(row, (size, size)))


def pack_kernel(k_ref, v_ref, end_ref, message_ref):
    rows, width = k_ref.shape
    message_ref[pl.ds(0, rows), pl.ds(0, width)] = k_ref[...]
    message_ref[pl.ds(0, rows), pl.ds(width, width)] = v_ref[...]
    extra = message_ref.shape[0] - rows
    line = lax.broadcasted_iota(jnp.int32, (extra, rows), 0)
    ends = jnp.broadcast_to(end_ref[...], (extra, rows))
    parts = jnp.where(line == 0, ends // END_PART, jnp.where(line == 1, ends % END_PART, 0))
    message_ref[pl.ds(rows, extra), :] = jnp.zeros((extra, 2 * width), jnp.bfloat16)
    message_ref[pl.ds(rows, extra), pl.ds(0, rows)] = parts.astype(jnp.float32).astype(jnp.bfloat16)


def pack(key_rows, value_rows, ends):
    rows, width = key_rows.shape
    return pl.pallas_call(
        pack_kernel,
        out_shape=jax.ShapeDtypeStruct((rows + 16, 2 * width), jnp.bfloat16),
        in_specs=vmem(3),
        out_specs=pl.BlockSpec(memory_space=pltpu.VMEM),
        cost_estimate=cost(10**9, 8 * key_rows.size),
    )(key_rows, value_rows, ends)


def attend_kernel(blocks, q_ref, halo_ref, k_ref, v_ref, end_ref, st_ref, *refs):
    whole_ref, *out_refs = refs
    rows = q_ref.shape[0]
    width = k_ref.shape[1]
    kv_here = width // HEAD_DIM
    group = q_ref.shape[1] // HEAD_DIM // kv_here
    core = lax.axis_index("tp") % 2
    base = lax.axis_index("ctx") * rows
    half = rows // blocks // 2
    query_pos = base + lax.broadcasted_iota(jnp.int32, (rows, rows), 0)
    query_start = column(st_ref[...])
    parts = halo_ref[pl.ds(rows, 16), pl.ds(0, rows)].astype(jnp.float32).astype(jnp.int32)
    masks = []
    for shift, key_end in ((rows, parts[0:1] * END_PART + parts[1:2]), (0, end_ref[...])):
        key_pos = base - shift + lax.broadcasted_iota(jnp.int32, (rows, rows), 1)
        masks.append((key_pos <= query_pos) & (key_pos >= query_start) & (key_end > query_pos))
    visible = jnp.concatenate(masks, axis=1)
    visible = jnp.concatenate([visible] * group, axis=0)
    for kv in range(kv_here):
        keys, values = (
            jnp.concatenate(
                [
                    halo_ref[pl.ds(0, rows), pl.ds(first + kv * HEAD_DIM, HEAD_DIM)],
                    ref[:, pl.ds(kv * HEAD_DIM, HEAD_DIM)],
                ],
                axis=0,
            )
            for first, ref in ((0, k_ref), (width, v_ref))
        )
        query = jnp.concatenate(
            [q_ref[:, pl.ds((kv * group + g) * HEAD_DIM, HEAD_DIM)] for g in range(group)], axis=0
        )
        scores = (
            lax.dot_general(
                query, keys, (((1,), (1,)), ((), ())), preferred_element_type=jnp.float32
            )
            * HEAD_DIM**-0.5
        )
        row_max = jnp.max(jnp.where(visible, scores, NEG_LARGE), axis=1, keepdims=True)
        weights = jnp.where(visible, jnp.exp(scores - row_max), 0.0)
        weight_sum = jnp.sum(weights, axis=1, keepdims=True)
        summed = jnp.dot(
            weights.astype(jnp.bfloat16), values, preferred_element_type=jnp.float32
        )
        attended = (summed / weight_sum).astype(jnp.bfloat16)
        for g in range(group):
            for p in range(blocks):
                for h in range(2):
                    first = g * rows + (p * 2 + h) * half
                    place = pl.multiple_of((h ^ core) * half, half)
                    lanes = pl.ds((kv * group + g) * HEAD_DIM, HEAD_DIM)
                    out_refs[p][pl.ds(place, half), lanes] = attended[first : first + half]
                    whole_ref[pl.ds(p * 2 * half + place, half), lanes] = (
                        attended[first : first + half]
                    )


def attend(blocks, queries, halo, keys, values, end, start):
    rows, features = queries.shape
    out = jax.ShapeDtypeStruct((rows // blocks, features), jnp.bfloat16)
    return pl.pallas_call(
        functools.partial(attend_kernel, blocks),
        out_shape=(
            jax.ShapeDtypeStruct(queries.shape, jnp.bfloat16),
        )
        + (out,) * blocks,
        in_specs=vmem(6),
        out_specs=tuple(vmem(1 + blocks)),
        compiler_params=params(),
        cost_estimate=cost(8 * rows * rows * features, 6 * queries.size),
    )(queries, halo, keys, values, end, start)


def project_kernel(block_rows, *refs):
    chunks, weight_ref, mine_ref, other_ref = refs[:-3], refs[-3], refs[-2], refs[-1]
    half = block_rows // 2
    stacked = jnp.concatenate([c[...] for c in chunks], axis=0)
    share = jnp.dot(stacked, weight_ref[...], preferred_element_type=jnp.float32).astype(
        jnp.bfloat16
    )
    for n in range(share.shape[0] // block_rows):
        first = n * block_rows
        mine_ref[pl.ds(n * half, half), :] = share[first : first + half]
        other_ref[pl.ds(n * half, half), :] = share[first + half : first + block_rows]


def project(block_rows, chunks, weight):
    rows = sum(c.shape[0] for c in chunks)
    out = jax.ShapeDtypeStruct((rows // 2, weight.shape[1]), jnp.bfloat16)
    return pl.pallas_call(
        functools.partial(project_kernel, block_rows),
        out_shape=(out, out),
        in_specs=vmem(len(chunks) + 1),
        out_specs=tuple(vmem(2)),
        compiler_params=params(),
        cost_estimate=cost(2 * rows * weight.size, 2 * weight.size),
    )(*chunks, weight)


def total_kernel(*refs):
    terms, out_ref = refs[:-1], refs[-1]
    out_ref[...] = sum(t[...].astype(jnp.float32) for t in terms).astype(out_ref.dtype)


def total(terms):
    return pl.pallas_call(
        total_kernel,
        out_shape=jax.ShapeDtypeStruct(terms[0].shape, jnp.bfloat16),
        in_specs=vmem(len(terms)),
        out_specs=pl.BlockSpec(memory_space=pltpu.VMEM),
        compiler_params=params(),
        cost_estimate=cost(4 * terms[0].size, 10 * terms[0].size),
    )(*terms)


def pick_kernel(blocks, half, even_ref, odd_ref, *refs):
    sums, outs = refs[:-4], refs[-4:]
    x = lax.axis_index("tp") // 2
    c = lax.axis_index("ctx")
    order = (0, 1, 4, 5, 2, 6, 3, 7)
    pieces = [r[pl.ds(n, half), :] for r in sums for n in range(0, r.shape[0], half)]
    targets = jnp.concatenate([even_ref[...], odd_ref[...]], axis=1)
    for k in range(4):
        wanted = (c ^ k) * blocks + x
        piece = pieces[0]
        for n in range(1, len(pieces)):
            column_of = order[n]
            here = jnp.broadcast_to(targets[:, column_of : column_of + 1] == wanted, piece.shape)
            piece = jnp.where(here, pieces[n], piece)
        outs[k][...] = piece


def pick(blocks, even_targets, odd_targets, sums):
    rows, cols = sum(s.shape[0] for s in sums), sums[0].shape[1]
    half = rows // (4 * blocks)
    out = jax.ShapeDtypeStruct((half, cols), jnp.bfloat16)
    return pl.pallas_call(
        functools.partial(pick_kernel, blocks, half),
        out_shape=(out,) * 4,
        in_specs=vmem(2 + len(sums)),
        out_specs=tuple(vmem(4)),
        compiler_params=params(),
        cost_estimate=cost(4 * rows * cols, 8 * rows * cols),
    )(even_targets, odd_targets, *sums)


def hold_kernel(near_ref, far_ref, out_ref):
    cols = near_ref.shape[1]
    out_ref[:, pl.ds(0, cols)] = near_ref[...]
    out_ref[:, pl.ds(cols, cols)] = far_ref[...]


def hold(near, far):
    rows, cols = near.shape
    return pl.pallas_call(
        hold_kernel,
        out_shape=jax.ShapeDtypeStruct((rows, 2 * cols), near.dtype),
        in_specs=vmem(2),
        out_specs=pl.BlockSpec(memory_space=pltpu.VMEM),
        compiler_params=params(),
        cost_estimate=cost(0, 8 * near.size),
    )(near, far)


def join_kernel(held_ref, two_ref, one_ref, out_ref):
    cols = one_ref.shape[1]
    c = lax.axis_index("ctx")
    pieces = (held_ref[:, pl.ds(0, cols)], one_ref[...], two_ref[...], held_ref[:, pl.ds(cols, cols)])
    for k in range(4):
        out_ref[:, pl.ds(pl.multiple_of((c ^ k) * cols, cols), cols)] = pieces[k]


def join(held, two, one):
    rows, cols = one.shape
    return pl.pallas_call(
        join_kernel,
        out_shape=jax.ShapeDtypeStruct((rows, 4 * cols), jnp.bfloat16),
        in_specs=vmem(3),
        out_specs=pl.BlockSpec(memory_space=pltpu.VMEM),
        compiler_params=params(),
        cost_estimate=cost(0, 16 * one.size),
    )(held, two, one)


def flip(array, axis, bits):
    return lax.ppermute(array, axis, [(i, i ^ bits) for i in range(4)])


def core_total(mine, other):
    return total((mine, flip(other, "tp", 1)))


def chip_total(share):
    return total((share, flip(share, "tp", 2)))


def after(value, *others):
    return lax.optimization_barrier((value, *others))[0]


def small_ring(queries, key_rows, value_rows, doc_start, doc_end, block_target, out_weight):
    rows = queries.shape[0]
    blocks = block_target.shape[0]
    block_rows = rows // blocks
    end, start = doc_end.reshape(1, rows), doc_start.reshape(1, rows)
    message = pack(key_rows, value_rows, end)
    halo = lax.ppermute(message, "ctx", [(0, 1), (1, 2), (2, 3)])
    target_2 = flip(after(block_target, message), "ctx", 2)
    even_targets = jnp.concatenate([block_target, target_2]).reshape(1, 2 * blocks)
    halo = after(halo, target_2)
    whole, first, second = attend(blocks, queries, halo, key_rows, value_rows, end, start)
    whole_1 = flip(whole, "ctx", 1)
    first_2, second_2 = flip(first, "ctx", 2), flip(second, "ctx", 2)
    odd_targets = flip(even_targets, "ctx", 1)
    whole_1 = after(whole_1, odd_targets)
    share_a = core_total(*project(block_rows, (whole, whole_1), out_weight))
    first_3, second_3 = flip(first_2, "ctx", 1), flip(second_2, "ctx", 1)
    sum_a = chip_total(share_a)
    second_2 = after(second_2, share_a)
    share_b = core_total(*project(block_rows, (first_2, first_3, second_2), out_weight))
    second_3 = after(second_3, share_b)
    share_c = core_total(*project(block_rows, (second_3,), out_weight))
    sum_b = chip_total(share_b)
    sum_c = chip_total(share_c)
    kept, *sent = pick(blocks, even_targets, odd_targets, (sum_a, sum_b, sum_c))
    got_3, got_2, got_1 = (flip(sent[k - 1], "ctx", k) for k in (3, 2, 1))
    return join(hold(kept, got_3), got_2, got_1)


def attend_block(soft_state, query_grid, query_pos, query_start, key_block, value_block, key_end, key_pos):
    running_max, weight_sum, weighted = soft_state
    scores = jnp.einsum(
        "rkgd,nkd->rkgn", query_grid, key_block, preferred_element_type=jnp.float32
    ) * HEAD_DIM ** (-0.5)
    visible = (
        (key_pos[None, :] <= query_pos[:, None])
        & (key_pos[None, :] >= query_start[:, None])
        & (key_end[None, :] > query_pos[:, None])
    )
    visible = visible[:, None, None, :]
    new_max = jnp.maximum(running_max, jnp.max(jnp.where(visible, scores, NEG_LARGE), axis=-1))
    weights = jnp.where(visible, jnp.exp(scores - new_max[..., None]), 0.0)
    fading = jnp.exp(running_max - new_max)
    weight_sum = weight_sum * fading + jnp.sum(weights, axis=-1)
    weighted = weighted * fading[..., None] + jnp.einsum(
        "rkgn,nkd->rkgd",
        weights.astype(jnp.bfloat16),
        value_block,
        preferred_element_type=jnp.float32,
    )
    return (new_max, weight_sum, weighted)


def attend_all(queries, query_pos, query_start, key_part, value_part, end_part):
    rows = queries.shape[0]
    key_count = key_part.shape[0]
    kv_here = key_part.shape[1] // HEAD_DIM
    query_grid = queries.reshape(rows, kv_here, -1, HEAD_DIM)
    block_len = math.gcd(key_count, 512)
    block_count = key_count // block_len
    items = (
        key_part.reshape(block_count, block_len, kv_here, HEAD_DIM),
        value_part.reshape(block_count, block_len, kv_here, HEAD_DIM),
        end_part.reshape(block_count, block_len),
        jnp.arange(key_count, dtype=jnp.int32).reshape(block_count, block_len),
    )
    start_state = (
        jnp.full(query_grid.shape[:3], NEG_LARGE, jnp.float32),
        jnp.zeros(query_grid.shape[:3], jnp.float32),
        jnp.zeros(query_grid.shape, jnp.float32),
    )

    def one_block(state, item):
        return attend_block(state, query_grid, query_pos, query_start, *item), None

    (_, weight_sum, weighted), _ = lax.scan(one_block, start_state, items)
    return (weighted / weight_sum[..., None]).astype(jnp.bfloat16).reshape(rows, -1)


def any_ring(queries, key_rows, value_rows, doc_start, doc_end, block_target, out_weight):
    rows = queries.shape[0]
    blocks = block_target.shape[0]
    block_rows = rows // blocks
    ctx_count = lax.axis_size("ctx")
    tp_count = lax.axis_size("tp")
    gather = functools.partial(lax.all_gather, axis_name="ctx", axis=0, tiled=True)
    query_pos = lax.axis_index("ctx") * rows + jnp.arange(rows, dtype=jnp.int32)
    attended = attend_all(
        queries, query_pos, doc_start, gather(key_rows), gather(value_rows), gather(doc_end)
    )
    targets = gather(block_target)
    source = jnp.zeros_like(targets).at[targets].set(jnp.arange(targets.size, dtype=jnp.int32))
    source_rows = (source[:, None] * block_rows + jnp.arange(block_rows, dtype=jnp.int32)).reshape(-1)
    balanced = jnp.take(gather(attended), source_rows, axis=0)
    share = jnp.dot(balanced, out_weight, preferred_element_type=jnp.float32).astype(jnp.bfloat16)
    share = share.reshape(ctx_count, tp_count, rows // tp_count, -1)
    summed = lax.psum_scatter(share, "tp", scatter_dimension=1, tiled=True)
    pieces = lax.all_to_all(summed[:, 0], "ctx", split_axis=0, concat_axis=0, tiled=True)
    return jnp.swapaxes(pieces, 0, 1).reshape(rows // tp_count, -1)


def shards(queries, key_rows, value_rows, doc_start, doc_end, block_target, out_weight):
    ctx_count, tp_count = lax.axis_size("ctx"), lax.axis_size("tp")
    rows, blocks = queries.shape[0], block_target.shape[0]
    longest = rows * ctx_count // 2 - rows
    near = longest <= rows and ctx_count == 4 and tp_count == 4 and blocks == 2
    plan = small_ring if near and rows % (4 * blocks * 2) == 0 else any_ring
    return plan(queries, key_rows, value_rows, doc_start, doc_end, block_target, out_weight)


def solution(mesh):
    in_specs = (
        P(("group", "ctx"), "tp"),
        P(("group", "ctx"), "tp"),
        P(("group", "ctx"), "tp"),
        P(("group", "ctx")),
        P(("group", "ctx")),
        P(("group", "ctx")),
        P("tp", "ctx"),
    )
    out_specs = P(("group", "ctx", "tp"), None)
    return jax.shard_map(shards, mesh=mesh, in_specs=in_specs, out_specs=out_specs, check_vma=False)
```

```python
import functools
import math

import jax
import jax.numpy as jnp
from jax import lax
from jax.experimental import pallas as pl
from jax.experimental.pallas import tpu as pltpu
from jax.sharding import PartitionSpec as P

HEAD_DIM = 128
NEG_LARGE = -1e30
END_PART = 128


def vmem(count):
    return [pl.BlockSpec(memory_space=pltpu.VMEM)] * count


def smem(count):
    return [pl.BlockSpec(memory_space=pltpu.SMEM)] * count


def params():
    return pltpu.CompilerParams(vmem_limit_bytes=16 * 1024 * 1024)


def cost(flops, moved):
    return pl.CostEstimate(flops=int(flops), bytes_accessed=int(moved), transcendentals=0)


def column(row):
    size = row.shape[1]
    return jnp.transpose(jnp.broadcast_to(row, (size, size)))


def pack_kernel(k_ref, v_ref, end_ref, message_ref):
    rows, width = k_ref.shape
    message_ref[pl.ds(0, rows), pl.ds(0, width)] = k_ref[...]
    message_ref[pl.ds(0, rows), pl.ds(width, width)] = v_ref[...]
    extra = message_ref.shape[0] - rows
    line = lax.broadcasted_iota(jnp.int32, (extra, rows), 0)
    ends = jnp.broadcast_to(end_ref[...], (extra, rows))
    parts = jnp.where(line == 0, ends // END_PART, jnp.where(line == 1, ends % END_PART, 0))
    message_ref[pl.ds(rows, extra), :] = jnp.zeros((extra, 2 * width), jnp.bfloat16)
    message_ref[pl.ds(rows, extra), pl.ds(0, rows)] = parts.astype(jnp.float32).astype(jnp.bfloat16)


def pack(key_rows, value_rows, ends):
    rows, width = key_rows.shape
    return pl.pallas_call(
        pack_kernel,
        out_shape=jax.ShapeDtypeStruct((rows + 16, 2 * width), jnp.bfloat16),
        in_specs=vmem(3),
        out_specs=pl.BlockSpec(memory_space=pltpu.VMEM),
        cost_estimate=cost(10**9, 8 * key_rows.size),
    )(key_rows, value_rows, ends)


def attend_kernel(blocks, q_ref, halo_ref, k_ref, v_ref, end_ref, st_ref, targets_ref, *refs):
    whole_ref, *out_refs = refs
    count = targets_ref.shape[1]
    targets = jnp.broadcast_to(targets_ref[...].astype(jnp.float32), (8, count)).astype(jnp.bfloat16)
    whole_ref[pl.ds(q_ref.shape[0], 8), :] = jnp.zeros((8, q_ref.shape[1]), jnp.bfloat16)
    whole_ref[pl.ds(q_ref.shape[0], 8), pl.ds(0, count)] = targets
    rows = q_ref.shape[0]
    width = k_ref.shape[1]
    kv_here = width // HEAD_DIM
    group = q_ref.shape[1] // HEAD_DIM // kv_here
    core = lax.axis_index("tp") % 2
    base = lax.axis_index("ctx") * rows
    half = rows // blocks // 2
    query_pos = base + lax.broadcasted_iota(jnp.int32, (rows, rows), 0)
    query_start = column(st_ref[...])
    parts = halo_ref[pl.ds(rows, 16), pl.ds(0, rows)].astype(jnp.float32).astype(jnp.int32)
    masks = []
    for shift, key_end in ((rows, parts[0:1] * END_PART + parts[1:2]), (0, end_ref[...])):
        key_pos = base - shift + lax.broadcasted_iota(jnp.int32, (rows, rows), 1)
        masks.append((key_pos <= query_pos) & (key_pos >= query_start) & (key_end > query_pos))
    visible = jnp.concatenate(masks, axis=1)
    visible = jnp.concatenate([visible] * group, axis=0)
    for kv in range(kv_here):
        keys, values = (
            jnp.concatenate(
                [
                    halo_ref[pl.ds(0, rows), pl.ds(first + kv * HEAD_DIM, HEAD_DIM)],
                    ref[:, pl.ds(kv * HEAD_DIM, HEAD_DIM)],
                ],
                axis=0,
            )
            for first, ref in ((0, k_ref), (width, v_ref))
        )
        query = jnp.concatenate(
            [q_ref[:, pl.ds((kv * group + g) * HEAD_DIM, HEAD_DIM)] for g in range(group)], axis=0
        )
        scores = (
            lax.dot_general(
                query, keys, (((1,), (1,)), ((), ())), preferred_element_type=jnp.float32
            )
            * HEAD_DIM**-0.5
        )
        row_max = jnp.max(jnp.where(visible, scores, NEG_LARGE), axis=1, keepdims=True)
        weights = jnp.where(visible, jnp.exp(scores - row_max), 0.0)
        weight_sum = jnp.sum(weights, axis=1, keepdims=True)
        summed = jnp.dot(
            weights.astype(jnp.bfloat16), values, preferred_element_type=jnp.float32
        )
        attended = (summed / weight_sum).astype(jnp.bfloat16)
        for g in range(group):
            for p in range(blocks):
                for h in range(2):
                    first = g * rows + (p * 2 + h) * half
                    place = pl.multiple_of((h ^ core) * half, half)
                    lanes = pl.ds((kv * group + g) * HEAD_DIM, HEAD_DIM)
                    out_refs[p][pl.ds(place, half), lanes] = attended[first : first + half]
                    whole_ref[pl.ds(p * 2 * half + place, half), lanes] = (
                        attended[first : first + half]
                    )


def attend(blocks, queries, halo, keys, values, end, start, targets):
    rows, features = queries.shape
    out = jax.ShapeDtypeStruct((rows // blocks, features), jnp.bfloat16)
    return pl.pallas_call(
        functools.partial(attend_kernel, blocks),
        out_shape=(
            jax.ShapeDtypeStruct((rows + 8, features), jnp.bfloat16),
        )
        + (out,) * blocks,
        in_specs=vmem(7),
        out_specs=tuple(vmem(1 + blocks)),
        compiler_params=params(),
        cost_estimate=cost(8 * rows * rows * features, 6 * queries.size),
    )(queries, halo, keys, values, end, start, targets)


def project_kernel(block_rows, *refs):
    chunks, weight_ref, mine_ref, other_ref = refs[:-3], refs[-3], refs[-2], refs[-1]
    half = block_rows // 2
    whole = [c.shape[0] // block_rows * block_rows for c in chunks]
    stacked = jnp.concatenate([c[pl.ds(0, n), :] for c, n in zip(chunks, whole)], axis=0)
    share = jnp.dot(stacked, weight_ref[...], preferred_element_type=jnp.float32).astype(
        jnp.bfloat16
    )
    for n in range(share.shape[0] // block_rows):
        first = n * block_rows
        mine_ref[pl.ds(n * half, half), :] = share[first : first + half]
        other_ref[pl.ds(n * half, half), :] = share[first + half : first + block_rows]


def project(block_rows, chunks, weight, estimate=None):
    rows = sum(c.shape[0] // block_rows * block_rows for c in chunks)
    out = jax.ShapeDtypeStruct((rows // 2, weight.shape[1]), jnp.bfloat16)
    return pl.pallas_call(
        functools.partial(project_kernel, block_rows),
        out_shape=(out, out),
        in_specs=vmem(len(chunks) + 1),
        out_specs=tuple(vmem(2)),
        compiler_params=params(),
        cost_estimate=estimate or cost(2 * rows * weight.size, 2 * weight.size),
    )(*chunks, weight)


def total_kernel(*refs):
    terms, out_ref = refs[:-1], refs[-1]
    out_ref[...] = sum(t[...].astype(jnp.float32) for t in terms).astype(out_ref.dtype)


def total(terms):
    return pl.pallas_call(
        total_kernel,
        out_shape=jax.ShapeDtypeStruct(terms[0].shape, jnp.bfloat16),
        in_specs=vmem(len(terms)),
        out_specs=pl.BlockSpec(memory_space=pltpu.VMEM),
        compiler_params=params(),
        cost_estimate=cost(4 * terms[0].size, 10 * terms[0].size),
    )(*terms)


def pick_kernel(blocks, half, even_ref, whole_ref, *refs):
    sums, outs = refs[:-4], refs[-4:]
    x = lax.axis_index("tp") // 2
    c = lax.axis_index("ctx")
    order = (0, 1, 4, 5, 2, 6, 3, 7)
    pieces = [r[pl.ds(n, half), :] for r in sums for n in range(0, r.shape[0], half)]
    tail = whole_ref[pl.ds(whole_ref.shape[0] - 8, 8), pl.ds(0, HEAD_DIM)].astype(jnp.float32)
    odd = tail[0:1, 0 : 2 * blocks].astype(jnp.int32)
    targets = jnp.concatenate([even_ref[...], odd], axis=1)
    for k in range(4):
        wanted = (c ^ k) * blocks + x
        piece = pieces[0]
        for n in range(1, len(pieces)):
            column_of = order[n]
            here = jnp.broadcast_to(targets[:, column_of : column_of + 1] == wanted, piece.shape)
            piece = jnp.where(here, pieces[n], piece)
        outs[k][...] = piece


def pick(blocks, even_targets, whole_1, sums):
    rows, cols = sum(s.shape[0] for s in sums), sums[0].shape[1]
    half = rows // (4 * blocks)
    out = jax.ShapeDtypeStruct((half, cols), jnp.bfloat16)
    return pl.pallas_call(
        functools.partial(pick_kernel, blocks, half),
        out_shape=(out,) * 4,
        in_specs=vmem(2 + len(sums)),
        out_specs=tuple(vmem(4)),
        compiler_params=params(),
        cost_estimate=cost(4 * rows * cols, 8 * rows * cols),
    )(even_targets, whole_1, *sums)


def hold_kernel(near_ref, far_ref, out_ref):
    cols = near_ref.shape[1]
    out_ref[:, pl.ds(0, cols)] = near_ref[...]
    out_ref[:, pl.ds(cols, cols)] = far_ref[...]


def hold(near, far):
    rows, cols = near.shape
    return pl.pallas_call(
        hold_kernel,
        out_shape=jax.ShapeDtypeStruct((rows, 2 * cols), near.dtype),
        in_specs=vmem(2),
        out_specs=pl.BlockSpec(memory_space=pltpu.VMEM),
        compiler_params=params(),
        cost_estimate=cost(0, 8 * near.size),
    )(near, far)


def join_kernel(held_ref, two_ref, one_ref, out_ref):
    cols = one_ref.shape[1]
    c = lax.axis_index("ctx")
    pieces = (held_ref[:, pl.ds(0, cols)], one_ref[...], two_ref[...], held_ref[:, pl.ds(cols, cols)])
    for k in range(4):
        out_ref[:, pl.ds(pl.multiple_of((c ^ k) * cols, cols), cols)] = pieces[k]


def join(held, two, one):
    rows, cols = one.shape
    return pl.pallas_call(
        join_kernel,
        out_shape=jax.ShapeDtypeStruct((rows, 4 * cols), jnp.bfloat16),
        in_specs=vmem(3),
        out_specs=pl.BlockSpec(memory_space=pltpu.VMEM),
        compiler_params=params(),
        cost_estimate=cost(0, 16 * one.size),
    )(held, two, one)


def flip(array, axis, bits):
    return lax.ppermute(array, axis, [(i, i ^ bits) for i in range(4)])


def core_total(mine, other):
    return total((mine, flip(other, "tp", 1)))


def stack_kernel(done_ref, mine_ref, got_ref, out_ref):
    rows = done_ref.shape[0]
    out_ref[pl.ds(0, rows), :] = done_ref[...]
    both = mine_ref[...].astype(jnp.float32) + got_ref[...].astype(jnp.float32)
    out_ref[pl.ds(rows, mine_ref.shape[0]), :] = both.astype(out_ref.dtype)


def stack_core_total(done, mine, other):
    rows = done.shape[0] + mine.shape[0]
    return pl.pallas_call(
        stack_kernel,
        out_shape=jax.ShapeDtypeStruct((rows, mine.shape[1]), jnp.bfloat16),
        in_specs=vmem(3),
        out_specs=pl.BlockSpec(memory_space=pltpu.VMEM),
        compiler_params=params(),
        cost_estimate=cost(mine.size, 8 * mine.size),
    )(done, mine, flip(other, "tp", 1))


def chip_total(share):
    return total((share, flip(share, "tp", 2)))


def after(value, *others):
    return lax.optimization_barrier((value, *others))[0]


def small_ring(queries, key_rows, value_rows, doc_start, doc_end, block_target, out_weight):
    rows = queries.shape[0]
    blocks = block_target.shape[0]
    block_rows = rows // blocks
    end, start = doc_end.reshape(1, rows), doc_start.reshape(1, rows)
    message = pack(key_rows, value_rows, end)
    halo = lax.ppermute(message, "ctx", [(0, 1), (1, 2), (2, 3)])
    target_2 = flip(after(block_target, message), "ctx", 2)
    even_targets = jnp.concatenate([block_target, target_2]).reshape(1, 2 * blocks)
    halo = after(halo, target_2)
    whole, first, second = attend(
        blocks, queries, halo, key_rows, value_rows, end, start, even_targets
    )
    whole_1 = flip(whole, "ctx", 1)
    first_2, second_2 = flip(first, "ctx", 2), flip(second, "ctx", 2)
    first_3, second_3 = flip(first_2, "ctx", 1), flip(second_2, "ctx", 1)
    share_a = core_total(*project(block_rows, (whole, whole_1), out_weight))
    share_ab = stack_core_total(
        share_a, *project(block_rows, (first_2, first_3, second_2), out_weight, cost(3 * 10**9, 0))
    )
    share_c = core_total(*project(block_rows, (second_3,), out_weight, cost(10**10, 0)))
    sums = (chip_total(share_ab), chip_total(share_c))
    kept, *sent = pick(blocks, even_targets, whole_1, sums)
    got_3, got_2, got_1 = (flip(sent[k - 1], "ctx", k) for k in (3, 2, 1))
    return join(hold(kept, got_3), got_2, got_1)


def attend_block(soft_state, query_grid, query_pos, query_start, key_block, value_block, key_end, key_pos):
    running_max, weight_sum, weighted = soft_state
    scores = jnp.einsum(
        "rkgd,nkd->rkgn", query_grid, key_block, preferred_element_type=jnp.float32
    ) * HEAD_DIM ** (-0.5)
    visible = (
        (key_pos[None, :] <= query_pos[:, None])
        & (key_pos[None, :] >= query_start[:, None])
        & (key_end[None, :] > query_pos[:, None])
    )
    visible = visible[:, None, None, :]
    new_max = jnp.maximum(running_max, jnp.max(jnp.where(visible, scores, NEG_LARGE), axis=-1))
    weights = jnp.where(visible, jnp.exp(scores - new_max[..., None]), 0.0)
    fading = jnp.exp(running_max - new_max)
    weight_sum = weight_sum * fading + jnp.sum(weights, axis=-1)
    weighted = weighted * fading[..., None] + jnp.einsum(
        "rkgn,nkd->rkgd",
        weights.astype(jnp.bfloat16),
        value_block,
        preferred_element_type=jnp.float32,
    )
    return (new_max, weight_sum, weighted)


def attend_all(queries, query_pos, query_start, key_part, value_part, end_part):
    rows = queries.shape[0]
    key_count = key_part.shape[0]
    kv_here = key_part.shape[1] // HEAD_DIM
    query_grid = queries.reshape(rows, kv_here, -1, HEAD_DIM)
    block_len = math.gcd(key_count, 512)
    block_count = key_count // block_len
    items = (
        key_part.reshape(block_count, block_len, kv_here, HEAD_DIM),
        value_part.reshape(block_count, block_len, kv_here, HEAD_DIM),
        end_part.reshape(block_count, block_len),
        jnp.arange(key_count, dtype=jnp.int32).reshape(block_count, block_len),
    )
    start_state = (
        jnp.full(query_grid.shape[:3], NEG_LARGE, jnp.float32),
        jnp.zeros(query_grid.shape[:3], jnp.float32),
        jnp.zeros(query_grid.shape, jnp.float32),
    )

    def one_block(state, item):
        return attend_block(state, query_grid, query_pos, query_start, *item), None

    (_, weight_sum, weighted), _ = lax.scan(one_block, start_state, items)
    return (weighted / weight_sum[..., None]).astype(jnp.bfloat16).reshape(rows, -1)


def any_ring(queries, key_rows, value_rows, doc_start, doc_end, block_target, out_weight):
    rows = queries.shape[0]
    blocks = block_target.shape[0]
    block_rows = rows // blocks
    ctx_count = lax.axis_size("ctx")
    tp_count = lax.axis_size("tp")
    gather = functools.partial(lax.all_gather, axis_name="ctx", axis=0, tiled=True)
    query_pos = lax.axis_index("ctx") * rows + jnp.arange(rows, dtype=jnp.int32)
    attended = attend_all(
        queries, query_pos, doc_start, gather(key_rows), gather(value_rows), gather(doc_end)
    )
    targets = gather(block_target)
    source = jnp.zeros_like(targets).at[targets].set(jnp.arange(targets.size, dtype=jnp.int32))
    source_rows = (source[:, None] * block_rows + jnp.arange(block_rows, dtype=jnp.int32)).reshape(-1)
    balanced = jnp.take(gather(attended), source_rows, axis=0)
    share = jnp.dot(balanced, out_weight, preferred_element_type=jnp.float32).astype(jnp.bfloat16)
    share = share.reshape(ctx_count, tp_count, rows // tp_count, -1)
    summed = lax.psum_scatter(share, "tp", scatter_dimension=1, tiled=True)
    pieces = lax.all_to_all(summed[:, 0], "ctx", split_axis=0, concat_axis=0, tiled=True)
    return jnp.swapaxes(pieces, 0, 1).reshape(rows // tp_count, -1)


def shards(queries, key_rows, value_rows, doc_start, doc_end, block_target, out_weight):
    ctx_count, tp_count = lax.axis_size("ctx"), lax.axis_size("tp")
    rows, blocks = queries.shape[0], block_target.shape[0]
    longest = rows * ctx_count // 2 - rows
    near = longest <= rows and ctx_count == 4 and tp_count == 4 and blocks == 2
    plan = small_ring if near and rows % (4 * blocks * 2) == 0 else any_ring
    return plan(queries, key_rows, value_rows, doc_start, doc_end, block_target, out_weight)


def solution(mesh):
    in_specs = (
        P(("group", "ctx"), "tp"),
        P(("group", "ctx"), "tp"),
        P(("group", "ctx"), "tp"),
        P(("group", "ctx")),
        P(("group", "ctx")),
        P(("group", "ctx")),
        P("tp", "ctx"),
    )
    out_specs = P(("group", "ctx", "tp"), None)
    return jax.shard_map(shards, mesh=mesh, in_specs=in_specs, out_specs=out_specs, check_vma=False)
```

```python
import functools
import math

import jax
import jax.numpy as jnp
from jax import lax
from jax.experimental import pallas as pl
from jax.experimental.pallas import tpu as pltpu
from jax.sharding import PartitionSpec as P

HEAD_DIM = 128
NEG_LARGE = -1e30
END_PART = 128


def vmem(count):
    return [pl.BlockSpec(memory_space=pltpu.VMEM)] * count


def smem(count):
    return [pl.BlockSpec(memory_space=pltpu.SMEM)] * count


def params():
    return pltpu.CompilerParams(vmem_limit_bytes=16 * 1024 * 1024)


def cost(flops, moved):
    return pl.CostEstimate(flops=int(flops), bytes_accessed=int(moved), transcendentals=0)


def column(row):
    size = row.shape[1]
    return jnp.transpose(jnp.broadcast_to(row, (size, size)))


def pack_kernel(k_ref, v_ref, end_ref, message_ref):
    rows, width = k_ref.shape
    message_ref[pl.ds(0, rows), pl.ds(0, width)] = k_ref[...]
    message_ref[pl.ds(0, rows), pl.ds(width, width)] = v_ref[...]
    extra = message_ref.shape[0] - rows
    line = lax.broadcasted_iota(jnp.int32, (extra, rows), 0)
    ends = jnp.broadcast_to(end_ref[...], (extra, rows))
    parts = jnp.where(line == 0, ends // END_PART, jnp.where(line == 1, ends % END_PART, 0))
    message_ref[pl.ds(rows, extra), :] = jnp.zeros((extra, 2 * width), jnp.bfloat16)
    message_ref[pl.ds(rows, extra), pl.ds(0, rows)] = parts.astype(jnp.float32).astype(jnp.bfloat16)


def pack(key_rows, value_rows, ends):
    rows, width = key_rows.shape
    return pl.pallas_call(
        pack_kernel,
        out_shape=jax.ShapeDtypeStruct((rows + 16, 2 * width), jnp.bfloat16),
        in_specs=vmem(3),
        out_specs=pl.BlockSpec(memory_space=pltpu.VMEM),
        cost_estimate=cost(10**9, 8 * key_rows.size),
    )(key_rows, value_rows, ends)


def attend_kernel(blocks, q_ref, halo_ref, k_ref, v_ref, end_ref, st_ref, own_ref, near_ref, *refs):
    whole_ref, *out_refs = refs
    targets = jnp.concatenate([own_ref[...], near_ref[...]], axis=1)
    count = targets.shape[1]
    targets = jnp.broadcast_to(targets.astype(jnp.float32), (8, count)).astype(jnp.bfloat16)
    for ref, first in ((whole_ref, q_ref.shape[0]), (out_refs[0], q_ref.shape[0] // blocks)):
        ref[pl.ds(first, 8), :] = jnp.zeros((8, q_ref.shape[1]), jnp.bfloat16)
        ref[pl.ds(first, 8), pl.ds(0, count)] = targets
    rows = q_ref.shape[0]
    width = k_ref.shape[1]
    kv_here = width // HEAD_DIM
    group = q_ref.shape[1] // HEAD_DIM // kv_here
    core = lax.axis_index("tp") % 2
    base = lax.axis_index("ctx") * rows
    half = rows // blocks // 2
    query_pos = base + lax.broadcasted_iota(jnp.int32, (rows, rows), 0)
    query_start = column(st_ref[...])
    parts = halo_ref[pl.ds(rows, 16), pl.ds(0, rows)].astype(jnp.float32).astype(jnp.int32)
    masks = []
    for shift, key_end in ((rows, parts[0:1] * END_PART + parts[1:2]), (0, end_ref[...])):
        key_pos = base - shift + lax.broadcasted_iota(jnp.int32, (rows, rows), 1)
        masks.append((key_pos <= query_pos) & (key_pos >= query_start) & (key_end > query_pos))
    visible = jnp.concatenate(masks, axis=1)
    visible = jnp.concatenate([visible] * group, axis=0)
    for kv in range(kv_here):
        keys, values = (
            jnp.concatenate(
                [
                    halo_ref[pl.ds(0, rows), pl.ds(first + kv * HEAD_DIM, HEAD_DIM)],
                    ref[:, pl.ds(kv * HEAD_DIM, HEAD_DIM)],
                ],
                axis=0,
            )
            for first, ref in ((0, k_ref), (width, v_ref))
        )
        query = jnp.concatenate(
            [q_ref[:, pl.ds((kv * group + g) * HEAD_DIM, HEAD_DIM)] for g in range(group)], axis=0
        )
        scores = (
            lax.dot_general(
                query, keys, (((1,), (1,)), ((), ())), preferred_element_type=jnp.float32
            )
            * HEAD_DIM**-0.5
        )
        row_max = jnp.max(jnp.where(visible, scores, NEG_LARGE), axis=1, keepdims=True)
        weights = jnp.where(visible, jnp.exp(scores - row_max), 0.0)
        weight_sum = jnp.sum(weights, axis=1, keepdims=True)
        summed = jnp.dot(
            weights.astype(jnp.bfloat16), values, preferred_element_type=jnp.float32
        )
        attended = (summed / weight_sum).astype(jnp.bfloat16)
        for g in range(group):
            for p in range(blocks):
                for h in range(2):
                    first = g * rows + (p * 2 + h) * half
                    place = pl.multiple_of((h ^ core) * half, half)
                    lanes = pl.ds((kv * group + g) * HEAD_DIM, HEAD_DIM)
                    out_refs[p][pl.ds(place, half), lanes] = attended[first : first + half]
                    whole_ref[pl.ds(p * 2 * half + place, half), lanes] = (
                        attended[first : first + half]
                    )


def attend(blocks, queries, halo, keys, values, end, start, own, near):
    rows, features = queries.shape
    sizes = (rows + 8, rows // blocks + 8) + (rows // blocks,) * (blocks - 1)
    return pl.pallas_call(
        functools.partial(attend_kernel, blocks),
        out_shape=tuple(jax.ShapeDtypeStruct((size, features), jnp.bfloat16) for size in sizes),
        in_specs=vmem(8),
        out_specs=tuple(vmem(1 + blocks)),
        compiler_params=params(),
        cost_estimate=cost(1 * 10**8, 0),
    )(queries, halo, keys, values, end, start, own, near)


def project_kernel(block_rows, *refs):
    chunks, weight_ref, mine_ref, other_ref = refs[:-3], refs[-3], refs[-2], refs[-1]
    half = block_rows // 2
    whole = [c.shape[0] // block_rows * block_rows for c in chunks]
    stacked = jnp.concatenate([c[pl.ds(0, n), :] for c, n in zip(chunks, whole)], axis=0)
    share = jnp.dot(stacked, weight_ref[...], preferred_element_type=jnp.float32).astype(
        jnp.bfloat16
    )
    for n in range(share.shape[0] // block_rows):
        first = n * block_rows
        mine_ref[pl.ds(n * half, half), :] = share[first : first + half]
        other_ref[pl.ds(n * half, half), :] = share[first + half : first + block_rows]


def project(block_rows, chunks, weight, estimate=None):
    rows = sum(c.shape[0] // block_rows * block_rows for c in chunks)
    out = jax.ShapeDtypeStruct((rows // 2, weight.shape[1]), jnp.bfloat16)
    return pl.pallas_call(
        functools.partial(project_kernel, block_rows),
        out_shape=(out, out),
        in_specs=vmem(len(chunks) + 1),
        out_specs=tuple(vmem(2)),
        compiler_params=params(),
        cost_estimate=estimate or cost(2 * rows * weight.size, 2 * weight.size),
    )(*chunks, weight)


def total_kernel(*refs):
    terms, out_ref = refs[:-1], refs[-1]
    out_ref[...] = sum(t[...].astype(jnp.float32) for t in terms).astype(out_ref.dtype)


def total(terms):
    return pl.pallas_call(
        total_kernel,
        out_shape=jax.ShapeDtypeStruct(terms[0].shape, jnp.bfloat16),
        in_specs=vmem(len(terms)),
        out_specs=pl.BlockSpec(memory_space=pltpu.VMEM),
        compiler_params=params(),
        cost_estimate=cost(4 * terms[0].size, 10 * terms[0].size),
    )(*terms)


def inner():
    c = lax.axis_index("ctx")
    return (c == 1) | (c == 2)


def tail_targets(ref, count):
    tail = ref[pl.ds(ref.shape[0] - 8, 8), pl.ds(0, HEAD_DIM)].astype(jnp.float32)
    return tail[0:1, 0:count].astype(jnp.int32)


def pick_kernel(blocks, half, own_ref, near_ref, one_ref, two_ref, *refs):
    sums, outs = refs[:-4], refs[-4:]
    x = lax.axis_index("tp") // 2
    c = lax.axis_index("ctx")
    pieces = [r[pl.ds(n, half), :] for r in sums for n in range(0, r.shape[0], half)]
    far = jnp.where(
        inner(), tail_targets(two_ref, 2 * blocks), tail_targets(one_ref, 2 * blocks)
    )
    by_source = (own_ref[...], near_ref[...], far[:, :blocks], far[:, blocks:])
    by_cycle = (
        by_source[0],
        jnp.where(inner(), by_source[1], by_source[2]),
        jnp.where(inner(), by_source[2], by_source[1]),
        by_source[3],
    )
    order = ((0, 0), (0, 1), (1, 0), (1, 1), (2, 0), (3, 0), (2, 1), (3, 1))
    for k in range(4):
        wanted = (c ^ k) * blocks + x
        piece = pieces[0]
        for n in range(1, len(pieces)):
            cycle, p = order[n]
            here = jnp.broadcast_to(by_cycle[cycle][:, p : p + 1] == wanted, piece.shape)
            piece = jnp.where(here, pieces[n], piece)
        outs[k][...] = piece


def pick(blocks, own, near, one, two, sums):
    rows, cols = sum(s.shape[0] for s in sums), sums[0].shape[1]
    half = rows // (4 * blocks)
    out = jax.ShapeDtypeStruct((half, cols), jnp.bfloat16)
    return pl.pallas_call(
        functools.partial(pick_kernel, blocks, half),
        out_shape=(out,) * 4,
        in_specs=vmem(4 + len(sums)),
        out_specs=tuple(vmem(4)),
        compiler_params=params(),
        cost_estimate=cost(4 * rows * cols, 8 * rows * cols),
    )(own, near, one, two, *sums)


def forward_kernel(first, one_ref, two_ref, out_ref):
    rows = out_ref.shape[0]
    out_ref[...] = jnp.where(inner(), two_ref[pl.ds(0, rows), :], one_ref[pl.ds(first, rows), :])


def forward(block_rows, first, one, two):
    out = jax.ShapeDtypeStruct((block_rows, one.shape[1]), one.dtype)
    return pl.pallas_call(
        functools.partial(forward_kernel, first),
        out_shape=out,
        in_specs=vmem(2),
        out_specs=pl.BlockSpec(memory_space=pltpu.VMEM),
        compiler_params=params(),
        cost_estimate=cost(30 * 10**8, 0),
    )(one, two)


def hold_kernel(near_ref, far_ref, out_ref):
    cols = near_ref.shape[1]
    out_ref[:, pl.ds(0, cols)] = near_ref[...]
    out_ref[:, pl.ds(cols, cols)] = far_ref[...]


def hold(near, far):
    rows, cols = near.shape
    return pl.pallas_call(
        hold_kernel,
        out_shape=jax.ShapeDtypeStruct((rows, 2 * cols), near.dtype),
        in_specs=vmem(2),
        out_specs=pl.BlockSpec(memory_space=pltpu.VMEM),
        compiler_params=params(),
        cost_estimate=cost(0, 8 * near.size),
    )(near, far)


def join_kernel(held_ref, two_ref, one_ref, out_ref):
    cols = one_ref.shape[1]
    c = lax.axis_index("ctx")
    pieces = (held_ref[:, pl.ds(0, cols)], one_ref[...], two_ref[...], held_ref[:, pl.ds(cols, cols)])
    for k in range(4):
        out_ref[:, pl.ds(pl.multiple_of((c ^ k) * cols, cols), cols)] = pieces[k]


def join(held, two, one):
    rows, cols = one.shape
    return pl.pallas_call(
        join_kernel,
        out_shape=jax.ShapeDtypeStruct((rows, 4 * cols), jnp.bfloat16),
        in_specs=vmem(3),
        out_specs=pl.BlockSpec(memory_space=pltpu.VMEM),
        compiler_params=params(),
        cost_estimate=cost(0, 16 * one.size),
    )(held, two, one)


def flip(array, axis, bits):
    return lax.ppermute(array, axis, [(i, i ^ bits) for i in range(4)])


def core_total(mine, other):
    return total((mine, flip(other, "tp", 1)))


def stack_kernel(done_ref, mine_ref, got_ref, out_ref):
    rows = done_ref.shape[0]
    out_ref[pl.ds(0, rows), :] = done_ref[...]
    both = mine_ref[...].astype(jnp.float32) + got_ref[...].astype(jnp.float32)
    out_ref[pl.ds(rows, mine_ref.shape[0]), :] = both.astype(out_ref.dtype)


def stack_core_total(done, mine, other):
    rows = done.shape[0] + mine.shape[0]
    return pl.pallas_call(
        stack_kernel,
        out_shape=jax.ShapeDtypeStruct((rows, mine.shape[1]), jnp.bfloat16),
        in_specs=vmem(3),
        out_specs=pl.BlockSpec(memory_space=pltpu.VMEM),
        compiler_params=params(),
        cost_estimate=cost(mine.size, 8 * mine.size),
    )(done, mine, flip(other, "tp", 1))


def chip_total(share):
    return total((share, flip(share, "tp", 2)))


def after(value, *others):
    return lax.optimization_barrier((value, *others))[0]


def small_ring(queries, key_rows, value_rows, doc_start, doc_end, block_target, out_weight):
    rows = queries.shape[0]
    blocks = block_target.shape[0]
    block_rows = rows // blocks
    end, start = doc_end.reshape(1, rows), doc_start.reshape(1, rows)
    message = pack(key_rows, value_rows, end)
    halo = lax.ppermute(message, "ctx", [(0, 1), (1, 2), (2, 3)])
    own_target = block_target.reshape(1, blocks)
    near_target = flip(after(own_target, message), "ctx", 1)
    halo = after(halo, near_target)
    whole, first, second = attend(
        blocks, queries, halo, key_rows, value_rows, end, start, own_target, near_target
    )
    cycle_1, cycle_2 = [(0, 1), (1, 3), (3, 2), (2, 0)], [(0, 2), (2, 3), (3, 1), (1, 0)]
    whole_1 = lax.ppermute(whole, "ctx", cycle_1)
    first_2, second_2 = (lax.ppermute(a, "ctx", cycle_2) for a in (first, second))
    first_3 = flip(forward(block_rows, 0, whole_1, first_2), "ctx", 1)
    second_3 = flip(forward(block_rows, block_rows, whole_1, second_2), "ctx", 1)
    share_a = core_total(*project(block_rows, (whole, whole_1), out_weight, cost(0, 0)))
    share_ab = stack_core_total(
        share_a, *project(block_rows, (first_2, first_3, second_2), out_weight, cost(30 * 10**8, 0))
    )
    share_c = core_total(*project(block_rows, (second_3,), out_weight, cost(30 * 10**8, 0)))
    sums = (chip_total(share_ab), chip_total(share_c))
    kept, *sent = pick(blocks, own_target, near_target, whole_1, first_2, sums)
    got_3, got_2, got_1 = (flip(sent[k - 1], "ctx", k) for k in (3, 2, 1))
    return join(hold(kept, got_3), got_2, got_1)


def attend_block(soft_state, query_grid, query_pos, query_start, key_block, value_block, key_end, key_pos):
    running_max, weight_sum, weighted = soft_state
    scores = jnp.einsum(
        "rkgd,nkd->rkgn", query_grid, key_block, preferred_element_type=jnp.float32
    ) * HEAD_DIM ** (-0.5)
    visible = (
        (key_pos[None, :] <= query_pos[:, None])
        & (key_pos[None, :] >= query_start[:, None])
        & (key_end[None, :] > query_pos[:, None])
    )
    visible = visible[:, None, None, :]
    new_max = jnp.maximum(running_max, jnp.max(jnp.where(visible, scores, NEG_LARGE), axis=-1))
    weights = jnp.where(visible, jnp.exp(scores - new_max[..., None]), 0.0)
    fading = jnp.exp(running_max - new_max)
    weight_sum = weight_sum * fading + jnp.sum(weights, axis=-1)
    weighted = weighted * fading[..., None] + jnp.einsum(
        "rkgn,nkd->rkgd",
        weights.astype(jnp.bfloat16),
        value_block,
        preferred_element_type=jnp.float32,
    )
    return (new_max, weight_sum, weighted)


def attend_all(queries, query_pos, query_start, key_part, value_part, end_part):
    rows = queries.shape[0]
    key_count = key_part.shape[0]
    kv_here = key_part.shape[1] // HEAD_DIM
    query_grid = queries.reshape(rows, kv_here, -1, HEAD_DIM)
    block_len = math.gcd(key_count, 512)
    block_count = key_count // block_len
    items = (
        key_part.reshape(block_count, block_len, kv_here, HEAD_DIM),
        value_part.reshape(block_count, block_len, kv_here, HEAD_DIM),
        end_part.reshape(block_count, block_len),
        jnp.arange(key_count, dtype=jnp.int32).reshape(block_count, block_len),
    )
    start_state = (
        jnp.full(query_grid.shape[:3], NEG_LARGE, jnp.float32),
        jnp.zeros(query_grid.shape[:3], jnp.float32),
        jnp.zeros(query_grid.shape, jnp.float32),
    )

    def one_block(state, item):
        return attend_block(state, query_grid, query_pos, query_start, *item), None

    (_, weight_sum, weighted), _ = lax.scan(one_block, start_state, items)
    return (weighted / weight_sum[..., None]).astype(jnp.bfloat16).reshape(rows, -1)


def any_ring(queries, key_rows, value_rows, doc_start, doc_end, block_target, out_weight):
    rows = queries.shape[0]
    blocks = block_target.shape[0]
    block_rows = rows // blocks
    ctx_count = lax.axis_size("ctx")
    tp_count = lax.axis_size("tp")
    gather = functools.partial(lax.all_gather, axis_name="ctx", axis=0, tiled=True)
    query_pos = lax.axis_index("ctx") * rows + jnp.arange(rows, dtype=jnp.int32)
    attended = attend_all(
        queries, query_pos, doc_start, gather(key_rows), gather(value_rows), gather(doc_end)
    )
    targets = gather(block_target)
    source = jnp.zeros_like(targets).at[targets].set(jnp.arange(targets.size, dtype=jnp.int32))
    source_rows = (source[:, None] * block_rows + jnp.arange(block_rows, dtype=jnp.int32)).reshape(-1)
    balanced = jnp.take(gather(attended), source_rows, axis=0)
    share = jnp.dot(balanced, out_weight, preferred_element_type=jnp.float32).astype(jnp.bfloat16)
    share = share.reshape(ctx_count, tp_count, rows // tp_count, -1)
    summed = lax.psum_scatter(share, "tp", scatter_dimension=1, tiled=True)
    pieces = lax.all_to_all(summed[:, 0], "ctx", split_axis=0, concat_axis=0, tiled=True)
    return jnp.swapaxes(pieces, 0, 1).reshape(rows // tp_count, -1)


def shards(queries, key_rows, value_rows, doc_start, doc_end, block_target, out_weight):
    ctx_count, tp_count = lax.axis_size("ctx"), lax.axis_size("tp")
    rows, blocks = queries.shape[0], block_target.shape[0]
    longest = rows * ctx_count // 2 - rows
    near = longest <= rows and ctx_count == 4 and tp_count == 4 and blocks == 2
    plan = small_ring if near and rows % (4 * blocks * 2) == 0 else any_ring
    return plan(queries, key_rows, value_rows, doc_start, doc_end, block_target, out_weight)


def solution(mesh):
    in_specs = (
        P(("group", "ctx"), "tp"),
        P(("group", "ctx"), "tp"),
        P(("group", "ctx"), "tp"),
        P(("group", "ctx")),
        P(("group", "ctx")),
        P(("group", "ctx")),
        P("tp", "ctx"),
    )
    out_specs = P(("group", "ctx", "tp"), None)
    return jax.shard_map(shards, mesh=mesh, in_specs=in_specs, out_specs=out_specs, check_vma=False)
```

```python
import functools
import math

import jax
import jax.numpy as jnp
from jax import lax
from jax.experimental import pallas as pl
from jax.experimental.pallas import tpu as pltpu
from jax.sharding import PartitionSpec as P

HEAD_DIM = 128
NEG_LARGE = -1e30
END_PART = 128


def vmem(count):
    return [pl.BlockSpec(memory_space=pltpu.VMEM)] * count


def smem(count):
    return [pl.BlockSpec(memory_space=pltpu.SMEM)] * count


def params():
    return pltpu.CompilerParams(vmem_limit_bytes=16 * 1024 * 1024)


def cost(flops, moved):
    return pl.CostEstimate(flops=int(flops), bytes_accessed=int(moved), transcendentals=0)


def column(row):
    size = row.shape[1]
    return jnp.transpose(jnp.broadcast_to(row, (size, size)))


def pack_kernel(k_ref, v_ref, end_ref, message_ref):
    rows, width = k_ref.shape
    message_ref[pl.ds(0, rows), pl.ds(0, width)] = k_ref[...]
    message_ref[pl.ds(0, rows), pl.ds(width, width)] = v_ref[...]
    extra = message_ref.shape[0] - rows
    line = lax.broadcasted_iota(jnp.int32, (extra, rows), 0)
    ends = jnp.broadcast_to(end_ref[...], (extra, rows))
    parts = jnp.where(line == 0, ends // END_PART, jnp.where(line == 1, ends % END_PART, 0))
    message_ref[pl.ds(rows, extra), :] = jnp.zeros((extra, 2 * width), jnp.bfloat16)
    message_ref[pl.ds(rows, extra), pl.ds(0, rows)] = parts.astype(jnp.float32).astype(jnp.bfloat16)


def pack(key_rows, value_rows, ends):
    rows, width = key_rows.shape
    return pl.pallas_call(
        pack_kernel,
        out_shape=jax.ShapeDtypeStruct((rows + 16, 2 * width), jnp.bfloat16),
        in_specs=vmem(3),
        out_specs=pl.BlockSpec(memory_space=pltpu.VMEM),
        cost_estimate=cost(10**9, 8 * key_rows.size),
    )(key_rows, value_rows, ends)


def attend_kernel(blocks, q_ref, halo_ref, k_ref, v_ref, end_ref, st_ref, own_ref, near_ref, *refs):
    whole_ref, *out_refs = refs
    targets = jnp.concatenate([own_ref[...], near_ref[...]], axis=1)
    count = targets.shape[1]
    targets = jnp.broadcast_to(targets.astype(jnp.float32), (8, count)).astype(jnp.bfloat16)
    for ref, first in ((whole_ref, q_ref.shape[0]), (out_refs[0], q_ref.shape[0] // blocks)):
        ref[pl.ds(first, 8), :] = jnp.zeros((8, q_ref.shape[1]), jnp.bfloat16)
        ref[pl.ds(first, 8), pl.ds(0, count)] = targets
    rows = q_ref.shape[0]
    width = k_ref.shape[1]
    kv_here = width // HEAD_DIM
    group = q_ref.shape[1] // HEAD_DIM // kv_here
    core = lax.axis_index("tp") % 2
    base = lax.axis_index("ctx") * rows
    half = rows // blocks // 2
    query_pos = base + lax.broadcasted_iota(jnp.int32, (rows, rows), 0)
    query_start = column(st_ref[...])
    parts = halo_ref[pl.ds(rows, 16), pl.ds(0, rows)].astype(jnp.float32).astype(jnp.int32)
    masks = []
    for shift, key_end in ((rows, parts[0:1] * END_PART + parts[1:2]), (0, end_ref[...])):
        key_pos = base - shift + lax.broadcasted_iota(jnp.int32, (rows, rows), 1)
        masks.append((key_pos <= query_pos) & (key_pos >= query_start) & (key_end > query_pos))
    visible = jnp.concatenate(masks, axis=1)
    visible = jnp.concatenate([visible] * group, axis=0)
    for kv in range(kv_here):
        keys, values = (
            jnp.concatenate(
                [
                    halo_ref[pl.ds(0, rows), pl.ds(first + kv * HEAD_DIM, HEAD_DIM)],
                    ref[:, pl.ds(kv * HEAD_DIM, HEAD_DIM)],
                ],
                axis=0,
            )
            for first, ref in ((0, k_ref), (width, v_ref))
        )
        query = jnp.concatenate(
            [q_ref[:, pl.ds((kv * group + g) * HEAD_DIM, HEAD_DIM)] for g in range(group)], axis=0
        )
        scores = (
            lax.dot_general(
                query, keys, (((1,), (1,)), ((), ())), preferred_element_type=jnp.float32
            )
            * HEAD_DIM**-0.5
        )
        row_max = jnp.max(jnp.where(visible, scores, NEG_LARGE), axis=1, keepdims=True)
        weights = jnp.where(visible, jnp.exp(scores - row_max), 0.0)
        weight_sum = jnp.sum(weights, axis=1, keepdims=True)
        summed = jnp.dot(
            weights.astype(jnp.bfloat16), values, preferred_element_type=jnp.float32
        )
        attended = (summed / weight_sum).astype(jnp.bfloat16)
        for g in range(group):
            for p in range(blocks):
                for h in range(2):
                    first = g * rows + (p * 2 + h) * half
                    place = pl.multiple_of((h ^ core) * half, half)
                    lanes = pl.ds((kv * group + g) * HEAD_DIM, HEAD_DIM)
                    out_refs[p][pl.ds(place, half), lanes] = attended[first : first + half]
                    whole_ref[pl.ds(p * 2 * half + place, half), lanes] = (
                        attended[first : first + half]
                    )


def attend(blocks, queries, halo, keys, values, end, start, own, near):
    rows, features = queries.shape
    sizes = (rows + 8, rows // blocks + 8) + (rows // blocks,) * (blocks - 1)
    return pl.pallas_call(
        functools.partial(attend_kernel, blocks),
        out_shape=tuple(jax.ShapeDtypeStruct((size, features), jnp.bfloat16) for size in sizes),
        in_specs=vmem(8),
        out_specs=tuple(vmem(1 + blocks)),
        compiler_params=params(),
        cost_estimate=cost(10 * 10**8, 0),
    )(queries, halo, keys, values, end, start, own, near)


def project_kernel(block_rows, *refs):
    chunks, weight_ref, mine_ref, other_ref = refs[:-3], refs[-3], refs[-2], refs[-1]
    half = block_rows // 2
    whole = [c.shape[0] // block_rows * block_rows for c in chunks]
    stacked = jnp.concatenate([c[pl.ds(0, n), :] for c, n in zip(chunks, whole)], axis=0)
    share = jnp.dot(stacked, weight_ref[...], preferred_element_type=jnp.float32).astype(
        jnp.bfloat16
    )
    for n in range(share.shape[0] // block_rows):
        first = n * block_rows
        mine_ref[pl.ds(n * half, half), :] = share[first : first + half]
        other_ref[pl.ds(n * half, half), :] = share[first + half : first + block_rows]


def project(block_rows, chunks, weight, estimate=None):
    rows = sum(c.shape[0] // block_rows * block_rows for c in chunks)
    out = jax.ShapeDtypeStruct((rows // 2, weight.shape[1]), jnp.bfloat16)
    return pl.pallas_call(
        functools.partial(project_kernel, block_rows),
        out_shape=(out, out),
        in_specs=vmem(len(chunks) + 1),
        out_specs=tuple(vmem(2)),
        compiler_params=params(),
        cost_estimate=estimate or cost(2 * rows * weight.size, 2 * weight.size),
    )(*chunks, weight)


def total_kernel(*refs):
    terms, out_ref = refs[:-1], refs[-1]
    out_ref[...] = sum(t[...].astype(jnp.float32) for t in terms).astype(out_ref.dtype)


def total(terms):
    return pl.pallas_call(
        total_kernel,
        out_shape=jax.ShapeDtypeStruct(terms[0].shape, jnp.bfloat16),
        in_specs=vmem(len(terms)),
        out_specs=pl.BlockSpec(memory_space=pltpu.VMEM),
        compiler_params=params(),
        cost_estimate=cost(4 * terms[0].size, 10 * terms[0].size),
    )(*terms)


def inner():
    c = lax.axis_index("ctx")
    return (c == 1) | (c == 2)


def tail_targets(ref, count):
    tail = ref[pl.ds(ref.shape[0] - 8, 8), pl.ds(0, HEAD_DIM)].astype(jnp.float32)
    return tail[0:1, 0:count].astype(jnp.int32)


def pick_kernel(blocks, half, own_ref, near_ref, one_ref, two_ref, *refs):
    sums, outs = refs[:-4], refs[-4:]
    x = lax.axis_index("tp") // 2
    c = lax.axis_index("ctx")
    pieces = [r[pl.ds(n, half), :] for r in sums for n in range(0, r.shape[0], half)]
    far = jnp.where(
        inner(), tail_targets(two_ref, 2 * blocks), tail_targets(one_ref, 2 * blocks)
    )
    by_source = (own_ref[...], near_ref[...], far[:, :blocks], far[:, blocks:])
    by_cycle = (
        by_source[0],
        jnp.where(inner(), by_source[1], by_source[2]),
        jnp.where(inner(), by_source[2], by_source[1]),
        by_source[3],
    )
    order = [(cycle, p) for cycle in range(4) for p in range(blocks)]
    for k in range(4):
        wanted = (c ^ k) * blocks + x
        piece = pieces[0]
        for n in range(1, len(pieces)):
            cycle, p = order[n]
            here = jnp.broadcast_to(by_cycle[cycle][:, p : p + 1] == wanted, piece.shape)
            piece = jnp.where(here, pieces[n], piece)
        outs[k][...] = piece


def pick(blocks, own, near, one, two, sums):
    rows, cols = sum(s.shape[0] for s in sums), sums[0].shape[1]
    half = rows // (4 * blocks)
    out = jax.ShapeDtypeStruct((half, cols), jnp.bfloat16)
    return pl.pallas_call(
        functools.partial(pick_kernel, blocks, half),
        out_shape=(out,) * 4,
        in_specs=vmem(4 + len(sums)),
        out_specs=tuple(vmem(4)),
        compiler_params=params(),
        cost_estimate=cost(4 * rows * cols, 8 * rows * cols),
    )(own, near, one, two, *sums)


def forward_kernel(first, one_ref, two_ref, out_ref):
    rows = out_ref.shape[0]
    out_ref[...] = jnp.where(inner(), two_ref[pl.ds(0, rows), :], one_ref[pl.ds(first, rows), :])


def forward(block_rows, first, one, two):
    out = jax.ShapeDtypeStruct((block_rows, one.shape[1]), one.dtype)
    return pl.pallas_call(
        functools.partial(forward_kernel, first),
        out_shape=out,
        in_specs=vmem(2),
        out_specs=pl.BlockSpec(memory_space=pltpu.VMEM),
        compiler_params=params(),
        cost_estimate=cost(30 * 10**8, 0),
    )(one, two)


def hold_kernel(near_ref, far_ref, out_ref):
    cols = near_ref.shape[1]
    out_ref[:, pl.ds(0, cols)] = near_ref[...]
    out_ref[:, pl.ds(cols, cols)] = far_ref[...]


def hold(near, far):
    rows, cols = near.shape
    return pl.pallas_call(
        hold_kernel,
        out_shape=jax.ShapeDtypeStruct((rows, 2 * cols), near.dtype),
        in_specs=vmem(2),
        out_specs=pl.BlockSpec(memory_space=pltpu.VMEM),
        compiler_params=params(),
        cost_estimate=cost(0, 8 * near.size),
    )(near, far)


def join_kernel(held_ref, two_ref, one_ref, out_ref):
    cols = one_ref.shape[1]
    c = lax.axis_index("ctx")
    pieces = (held_ref[:, pl.ds(0, cols)], one_ref[...], two_ref[...], held_ref[:, pl.ds(cols, cols)])
    for k in range(4):
        out_ref[:, pl.ds(pl.multiple_of((c ^ k) * cols, cols), cols)] = pieces[k]


def join(held, two, one):
    rows, cols = one.shape
    return pl.pallas_call(
        join_kernel,
        out_shape=jax.ShapeDtypeStruct((rows, 4 * cols), jnp.bfloat16),
        in_specs=vmem(3),
        out_specs=pl.BlockSpec(memory_space=pltpu.VMEM),
        compiler_params=params(),
        cost_estimate=cost(0, 16 * one.size),
    )(held, two, one)


def flip(array, axis, bits):
    return lax.ppermute(array, axis, [(i, i ^ bits) for i in range(4)])


def core_total(mine, other):
    return total((mine, flip(other, "tp", 1)))


def stack_kernel(done_ref, mine_ref, got_ref, out_ref):
    rows = done_ref.shape[0]
    out_ref[pl.ds(0, rows), :] = done_ref[...]
    both = mine_ref[...].astype(jnp.float32) + got_ref[...].astype(jnp.float32)
    out_ref[pl.ds(rows, mine_ref.shape[0]), :] = both.astype(out_ref.dtype)


def stack_core_total(done, mine, other):
    rows = done.shape[0] + mine.shape[0]
    return pl.pallas_call(
        stack_kernel,
        out_shape=jax.ShapeDtypeStruct((rows, mine.shape[1]), jnp.bfloat16),
        in_specs=vmem(3),
        out_specs=pl.BlockSpec(memory_space=pltpu.VMEM),
        compiler_params=params(),
        cost_estimate=cost(1 * 10**8, 0),
    )(done, mine, flip(other, "tp", 1))


def chip_total(share):
    return total((share, flip(share, "tp", 2)))


def after(value, *others):
    return lax.optimization_barrier((value, *others))[0]


def small_ring(queries, key_rows, value_rows, doc_start, doc_end, block_target, out_weight):
    rows = queries.shape[0]
    blocks = block_target.shape[0]
    block_rows = rows // blocks
    end, start = doc_end.reshape(1, rows), doc_start.reshape(1, rows)
    message = pack(key_rows, value_rows, end)
    halo = lax.ppermute(message, "ctx", [(0, 1), (1, 2), (2, 3)])
    own_target = block_target.reshape(1, blocks)
    near_target = flip(after(own_target, message), "ctx", 1)
    halo = after(halo, near_target)
    whole, first, second = attend(
        blocks, queries, halo, key_rows, value_rows, end, start, own_target, near_target
    )
    cycle_1, cycle_2 = [(0, 1), (1, 3), (3, 2), (2, 0)], [(0, 2), (2, 3), (3, 1), (1, 0)]
    whole_1 = lax.ppermute(whole, "ctx", cycle_1)
    first_2, second_2 = (lax.ppermute(a, "ctx", cycle_2) for a in (first, second))
    second_3 = flip(second, "ctx", 3)
    first_3 = flip(forward(block_rows, 0, whole_1, first_2), "ctx", 1)
    share_a = core_total(*project(block_rows, (whole, whole_1), out_weight, cost(0, 0)))
    share_ab = stack_core_total(
        share_a, *project(block_rows, (first_2, second_2), out_weight, cost(30 * 10**8, 0))
    )
    share_c = core_total(*project(block_rows, (first_3, second_3), out_weight))
    sums = (chip_total(share_ab), chip_total(share_c))
    kept, *sent = pick(blocks, own_target, near_target, whole_1, first_2, sums)
    got_3, got_2, got_1 = (flip(sent[k - 1], "ctx", k) for k in (3, 2, 1))
    return join(hold(kept, got_3), got_2, got_1)


def attend_block(soft_state, query_grid, query_pos, query_start, key_block, value_block, key_end, key_pos):
    running_max, weight_sum, weighted = soft_state
    scores = jnp.einsum(
        "rkgd,nkd->rkgn", query_grid, key_block, preferred_element_type=jnp.float32
    ) * HEAD_DIM ** (-0.5)
    visible = (
        (key_pos[None, :] <= query_pos[:, None])
        & (key_pos[None, :] >= query_start[:, None])
        & (key_end[None, :] > query_pos[:, None])
    )
    visible = visible[:, None, None, :]
    new_max = jnp.maximum(running_max, jnp.max(jnp.where(visible, scores, NEG_LARGE), axis=-1))
    weights = jnp.where(visible, jnp.exp(scores - new_max[..., None]), 0.0)
    fading = jnp.exp(running_max - new_max)
    weight_sum = weight_sum * fading + jnp.sum(weights, axis=-1)
    weighted = weighted * fading[..., None] + jnp.einsum(
        "rkgn,nkd->rkgd",
        weights.astype(jnp.bfloat16),
        value_block,
        preferred_element_type=jnp.float32,
    )
    return (new_max, weight_sum, weighted)


def attend_all(queries, query_pos, query_start, key_part, value_part, end_part):
    rows = queries.shape[0]
    key_count = key_part.shape[0]
    kv_here = key_part.shape[1] // HEAD_DIM
    query_grid = queries.reshape(rows, kv_here, -1, HEAD_DIM)
    block_len = math.gcd(key_count, 512)
    block_count = key_count // block_len
    items = (
        key_part.reshape(block_count, block_len, kv_here, HEAD_DIM),
        value_part.reshape(block_count, block_len, kv_here, HEAD_DIM),
        end_part.reshape(block_count, block_len),
        jnp.arange(key_count, dtype=jnp.int32).reshape(block_count, block_len),
    )
    start_state = (
        jnp.full(query_grid.shape[:3], NEG_LARGE, jnp.float32),
        jnp.zeros(query_grid.shape[:3], jnp.float32),
        jnp.zeros(query_grid.shape, jnp.float32),
    )

    def one_block(state, item):
        return attend_block(state, query_grid, query_pos, query_start, *item), None

    (_, weight_sum, weighted), _ = lax.scan(one_block, start_state, items)
    return (weighted / weight_sum[..., None]).astype(jnp.bfloat16).reshape(rows, -1)


def any_ring(queries, key_rows, value_rows, doc_start, doc_end, block_target, out_weight):
    rows = queries.shape[0]
    blocks = block_target.shape[0]
    block_rows = rows // blocks
    ctx_count = lax.axis_size("ctx")
    tp_count = lax.axis_size("tp")
    gather = functools.partial(lax.all_gather, axis_name="ctx", axis=0, tiled=True)
    query_pos = lax.axis_index("ctx") * rows + jnp.arange(rows, dtype=jnp.int32)
    attended = attend_all(
        queries, query_pos, doc_start, gather(key_rows), gather(value_rows), gather(doc_end)
    )
    targets = gather(block_target)
    source = jnp.zeros_like(targets).at[targets].set(jnp.arange(targets.size, dtype=jnp.int32))
    source_rows = (source[:, None] * block_rows + jnp.arange(block_rows, dtype=jnp.int32)).reshape(-1)
    balanced = jnp.take(gather(attended), source_rows, axis=0)
    share = jnp.dot(balanced, out_weight, preferred_element_type=jnp.float32).astype(jnp.bfloat16)
    share = share.reshape(ctx_count, tp_count, rows // tp_count, -1)
    summed = lax.psum_scatter(share, "tp", scatter_dimension=1, tiled=True)
    pieces = lax.all_to_all(summed[:, 0], "ctx", split_axis=0, concat_axis=0, tiled=True)
    return jnp.swapaxes(pieces, 0, 1).reshape(rows // tp_count, -1)


def shards(queries, key_rows, value_rows, doc_start, doc_end, block_target, out_weight):
    ctx_count, tp_count = lax.axis_size("ctx"), lax.axis_size("tp")
    rows, blocks = queries.shape[0], block_target.shape[0]
    longest = rows * ctx_count // 2 - rows
    near = longest <= rows and ctx_count == 4 and tp_count == 4 and blocks == 2
    plan = small_ring if near and rows % (4 * blocks * 2) == 0 else any_ring
    return plan(queries, key_rows, value_rows, doc_start, doc_end, block_target, out_weight)


def solution(mesh):
    in_specs = (
        P(("group", "ctx"), "tp"),
        P(("group", "ctx"), "tp"),
        P(("group", "ctx"), "tp"),
        P(("group", "ctx")),
        P(("group", "ctx")),
        P(("group", "ctx")),
        P("tp", "ctx"),
    )
    out_specs = P(("group", "ctx", "tp"), None)
    return jax.shard_map(shards, mesh=mesh, in_specs=in_specs, out_specs=out_specs, check_vma=False)
```

```python
import functools
import math

import jax
import jax.numpy as jnp
from jax import lax
from jax.experimental import pallas as pl
from jax.experimental.pallas import tpu as pltpu
from jax.sharding import PartitionSpec as P

HEAD_DIM = 128
NEG_LARGE = -1e30
END_PART = 128


def vmem(count):
    return [pl.BlockSpec(memory_space=pltpu.VMEM)] * count


def smem(count):
    return [pl.BlockSpec(memory_space=pltpu.SMEM)] * count


def params():
    return pltpu.CompilerParams(vmem_limit_bytes=16 * 1024 * 1024)


def cost(flops, moved):
    return pl.CostEstimate(flops=int(flops), bytes_accessed=int(moved), transcendentals=0)


def column(row):
    size = row.shape[1]
    return jnp.transpose(jnp.broadcast_to(row, (size, size)))


def pack_kernel(k_ref, v_ref, end_ref, message_ref):
    rows, width = k_ref.shape
    message_ref[pl.ds(0, rows), pl.ds(0, width)] = k_ref[...]
    message_ref[pl.ds(0, rows), pl.ds(width, width)] = v_ref[...]
    extra = message_ref.shape[0] - rows
    line = lax.broadcasted_iota(jnp.int32, (extra, rows), 0)
    ends = jnp.broadcast_to(end_ref[...], (extra, rows))
    parts = jnp.where(line == 0, ends // END_PART, jnp.where(line == 1, ends % END_PART, 0))
    message_ref[pl.ds(rows, extra), :] = jnp.zeros((extra, 2 * width), jnp.bfloat16)
    message_ref[pl.ds(rows, extra), pl.ds(0, rows)] = parts.astype(jnp.float32).astype(jnp.bfloat16)


def pack(key_rows, value_rows, ends):
    rows, width = key_rows.shape
    return pl.pallas_call(
        pack_kernel,
        out_shape=jax.ShapeDtypeStruct((rows + 16, 2 * width), jnp.bfloat16),
        in_specs=vmem(3),
        out_specs=pl.BlockSpec(memory_space=pltpu.VMEM),
        cost_estimate=cost(10**9, 8 * key_rows.size),
    )(key_rows, value_rows, ends)


def attend_kernel(blocks, q_ref, halo_ref, k_ref, v_ref, end_ref, st_ref, own_ref, near_ref, *refs):
    plain_ref, noted_ref = refs
    targets = jnp.concatenate([own_ref[...], near_ref[...]], axis=1)
    count = targets.shape[1]
    targets = jnp.broadcast_to(targets.astype(jnp.float32), (8, count)).astype(jnp.bfloat16)
    noted_ref[pl.ds(q_ref.shape[0], 8), :] = jnp.zeros((8, q_ref.shape[1]), jnp.bfloat16)
    noted_ref[pl.ds(q_ref.shape[0], 8), pl.ds(0, count)] = targets
    rows = q_ref.shape[0]
    width = k_ref.shape[1]
    kv_here = width // HEAD_DIM
    group = q_ref.shape[1] // HEAD_DIM // kv_here
    core = lax.axis_index("tp") % 2
    base = lax.axis_index("ctx") * rows
    half = rows // blocks // 2
    query_pos = base + lax.broadcasted_iota(jnp.int32, (rows, rows), 0)
    query_start = column(st_ref[...])
    parts = halo_ref[pl.ds(rows, 16), pl.ds(0, rows)].astype(jnp.float32).astype(jnp.int32)
    masks = []
    for shift, key_end in ((rows, parts[0:1] * END_PART + parts[1:2]), (0, end_ref[...])):
        key_pos = base - shift + lax.broadcasted_iota(jnp.int32, (rows, rows), 1)
        masks.append((key_pos <= query_pos) & (key_pos >= query_start) & (key_end > query_pos))
    visible = jnp.concatenate(masks, axis=1)
    visible = jnp.concatenate([visible] * group, axis=0)
    for kv in range(kv_here):
        keys, values = (
            jnp.concatenate(
                [
                    halo_ref[pl.ds(0, rows), pl.ds(first + kv * HEAD_DIM, HEAD_DIM)],
                    ref[:, pl.ds(kv * HEAD_DIM, HEAD_DIM)],
                ],
                axis=0,
            )
            for first, ref in ((0, k_ref), (width, v_ref))
        )
        query = jnp.concatenate(
            [q_ref[:, pl.ds((kv * group + g) * HEAD_DIM, HEAD_DIM)] for g in range(group)], axis=0
        )
        scores = (
            lax.dot_general(
                query, keys, (((1,), (1,)), ((), ())), preferred_element_type=jnp.float32
            )
            * HEAD_DIM**-0.5
        )
        row_max = jnp.max(jnp.where(visible, scores, NEG_LARGE), axis=1, keepdims=True)
        weights = jnp.where(visible, jnp.exp(scores - row_max), 0.0)
        weight_sum = jnp.sum(weights, axis=1, keepdims=True)
        summed = jnp.dot(
            weights.astype(jnp.bfloat16), values, preferred_element_type=jnp.float32
        )
        attended = (summed / weight_sum).astype(jnp.bfloat16)
        for g in range(group):
            for p in range(blocks):
                for h in range(2):
                    first = g * rows + (p * 2 + h) * half
                    place = pl.multiple_of((h ^ core) * half, half)
                    lanes = pl.ds((kv * group + g) * HEAD_DIM, HEAD_DIM)
                    target_rows = pl.ds(p * 2 * half + place, half)
                    plain_ref[target_rows, lanes] = attended[first : first + half]
                    noted_ref[target_rows, lanes] = attended[first : first + half]


def attend(blocks, queries, halo, keys, values, end, start, own, near):
    rows, features = queries.shape
    sizes = (rows, rows + 8)
    return pl.pallas_call(
        functools.partial(attend_kernel, blocks),
        out_shape=tuple(jax.ShapeDtypeStruct((size, features), jnp.bfloat16) for size in sizes),
        in_specs=vmem(8),
        out_specs=tuple(vmem(2)),
        compiler_params=params(),
        cost_estimate=cost(10 * 10**8, 0),
    )(queries, halo, keys, values, end, start, own, near)


def project_kernel(block_rows, *refs):
    chunks, weight_ref, mine_ref, other_ref = refs[:-3], refs[-3], refs[-2], refs[-1]
    half = block_rows // 2
    whole = [c.shape[0] // block_rows * block_rows for c in chunks]
    stacked = jnp.concatenate([c[pl.ds(0, n), :] for c, n in zip(chunks, whole)], axis=0)
    share = jnp.dot(stacked, weight_ref[...], preferred_element_type=jnp.float32).astype(
        jnp.bfloat16
    )
    for n in range(share.shape[0] // block_rows):
        first = n * block_rows
        mine_ref[pl.ds(n * half, half), :] = share[first : first + half]
        other_ref[pl.ds(n * half, half), :] = share[first + half : first + block_rows]


def project(block_rows, chunks, weight, estimate=None):
    rows = sum(c.shape[0] // block_rows * block_rows for c in chunks)
    out = jax.ShapeDtypeStruct((rows // 2, weight.shape[1]), jnp.bfloat16)
    return pl.pallas_call(
        functools.partial(project_kernel, block_rows),
        out_shape=(out, out),
        in_specs=vmem(len(chunks) + 1),
        out_specs=tuple(vmem(2)),
        compiler_params=params(),
        cost_estimate=estimate or cost(2 * rows * weight.size, 2 * weight.size),
    )(*chunks, weight)


def total_kernel(*refs):
    terms, out_ref = refs[:-1], refs[-1]
    out_ref[...] = sum(t[...].astype(jnp.float32) for t in terms).astype(out_ref.dtype)


def total(terms):
    return pl.pallas_call(
        total_kernel,
        out_shape=jax.ShapeDtypeStruct(terms[0].shape, jnp.bfloat16),
        in_specs=vmem(len(terms)),
        out_specs=pl.BlockSpec(memory_space=pltpu.VMEM),
        compiler_params=params(),
        cost_estimate=cost(4 * terms[0].size, 10 * terms[0].size),
    )(*terms)


def pick_kernel(blocks, half, own_ref, near_ref, two_ref, *refs):
    sums, outs = refs[:-4], refs[-4:]
    x = lax.axis_index("tp") // 2
    c = lax.axis_index("ctx")
    pieces = [r[pl.ds(n, half), :] for r in sums for n in range(0, r.shape[0], half)]
    tail = two_ref[pl.ds(two_ref.shape[0] - 8, 8), pl.ds(0, HEAD_DIM)].astype(jnp.float32)
    far = tail[0:1, 0 : 2 * blocks].astype(jnp.int32)
    targets = jnp.concatenate([own_ref[...], near_ref[...], far], axis=1)
    for k in range(4):
        wanted = (c ^ k) * blocks + x
        piece = pieces[0]
        for n in range(1, len(pieces)):
            here = jnp.broadcast_to(targets[:, n : n + 1] == wanted, piece.shape)
            piece = jnp.where(here, pieces[n], piece)
        outs[k][...] = piece


def pick(blocks, own, near, two, sums):
    rows, cols = sum(s.shape[0] for s in sums), sums[0].shape[1]
    half = rows // (4 * blocks)
    out = jax.ShapeDtypeStruct((half, cols), jnp.bfloat16)
    return pl.pallas_call(
        functools.partial(pick_kernel, blocks, half),
        out_shape=(out,) * 4,
        in_specs=vmem(3 + len(sums)),
        out_specs=tuple(vmem(4)),
        compiler_params=params(),
        cost_estimate=cost(4 * rows * cols, 8 * rows * cols),
    )(own, near, two, *sums)


def forward_kernel(got_ref, out_ref):
    out_ref[...] = got_ref[pl.ds(0, out_ref.shape[0]), :]


def forward(rows, got):
    out = jax.ShapeDtypeStruct((rows, got.shape[1]), got.dtype)
    return pl.pallas_call(
        forward_kernel,
        out_shape=out,
        in_specs=vmem(1),
        out_specs=pl.BlockSpec(memory_space=pltpu.VMEM),
        compiler_params=params(),
        cost_estimate=cost(0, 0),
    )(got)


def hold_kernel(near_ref, far_ref, out_ref):
    cols = near_ref.shape[1]
    out_ref[:, pl.ds(0, cols)] = near_ref[...]
    out_ref[:, pl.ds(cols, cols)] = far_ref[...]


def hold(near, far):
    rows, cols = near.shape
    return pl.pallas_call(
        hold_kernel,
        out_shape=jax.ShapeDtypeStruct((rows, 2 * cols), near.dtype),
        in_specs=vmem(2),
        out_specs=pl.BlockSpec(memory_space=pltpu.VMEM),
        compiler_params=params(),
        cost_estimate=cost(0, 8 * near.size),
    )(near, far)


def join_kernel(held_ref, two_ref, one_ref, out_ref):
    cols = one_ref.shape[1]
    c = lax.axis_index("ctx")
    pieces = (held_ref[:, pl.ds(0, cols)], one_ref[...], two_ref[...], held_ref[:, pl.ds(cols, cols)])
    for k in range(4):
        out_ref[:, pl.ds(pl.multiple_of((c ^ k) * cols, cols), cols)] = pieces[k]


def join(held, two, one):
    rows, cols = one.shape
    return pl.pallas_call(
        join_kernel,
        out_shape=jax.ShapeDtypeStruct((rows, 4 * cols), jnp.bfloat16),
        in_specs=vmem(3),
        out_specs=pl.BlockSpec(memory_space=pltpu.VMEM),
        compiler_params=params(),
        cost_estimate=cost(0, 16 * one.size),
    )(held, two, one)


def flip(array, axis, bits):
    return lax.ppermute(array, axis, [(i, i ^ bits) for i in range(4)])


def core_total(mine, other):
    return total((mine, flip(other, "tp", 1)))


def stack_kernel(done_ref, mine_ref, got_ref, out_ref):
    rows = done_ref.shape[0]
    out_ref[pl.ds(0, rows), :] = done_ref[...]
    both = mine_ref[...].astype(jnp.float32) + got_ref[...].astype(jnp.float32)
    out_ref[pl.ds(rows, mine_ref.shape[0]), :] = both.astype(out_ref.dtype)


def stack_core_total(done, mine, other):
    rows = done.shape[0] + mine.shape[0]
    return pl.pallas_call(
        stack_kernel,
        out_shape=jax.ShapeDtypeStruct((rows, mine.shape[1]), jnp.bfloat16),
        in_specs=vmem(3),
        out_specs=pl.BlockSpec(memory_space=pltpu.VMEM),
        compiler_params=params(),
        cost_estimate=cost(mine.size, 8 * mine.size),
    )(done, mine, flip(other, "tp", 1))


def chip_total(share):
    return total((share, flip(share, "tp", 2)))


def after(value, *others):
    return lax.optimization_barrier((value, *others))[0]


def small_ring(queries, key_rows, value_rows, doc_start, doc_end, block_target, out_weight):
    rows = queries.shape[0]
    blocks = block_target.shape[0]
    block_rows = rows // blocks
    end, start = doc_end.reshape(1, rows), doc_start.reshape(1, rows)
    message = pack(key_rows, value_rows, end)
    halo = lax.ppermute(message, "ctx", [(0, 1), (1, 2), (2, 3)])
    own_target = block_target.reshape(1, blocks)
    near_target = flip(after(own_target, message), "ctx", 1)
    halo = after(halo, near_target)
    plain, noted = attend(
        blocks, queries, halo, key_rows, value_rows, end, start, own_target, near_target
    )
    rows_1, rows_2 = flip(plain, "ctx", 1), flip(noted, "ctx", 2)
    rows_3 = flip(forward(rows, rows_2), "ctx", 1)
    share_a = core_total(*project(block_rows, (plain, rows_1), out_weight, cost(30 * 10**8, 0)))
    rows_2 = after(rows_2, share_a)
    share_ab = stack_core_total(share_a, *project(block_rows, (rows_2,), out_weight))
    rows_3 = after(rows_3, share_ab)
    share_c = core_total(*project(block_rows, (rows_3,), out_weight))
    sums = (chip_total(share_ab), chip_total(share_c))
    kept, *sent = pick(blocks, own_target, near_target, rows_2, sums)
    got_3, got_2, got_1 = (flip(sent[k - 1], "ctx", k) for k in (3, 2, 1))
    return join(hold(kept, got_3), got_2, got_1)


def attend_block(soft_state, query_grid, query_pos, query_start, key_block, value_block, key_end, key_pos):
    running_max, weight_sum, weighted = soft_state
    scores = jnp.einsum(
        "rkgd,nkd->rkgn", query_grid, key_block, preferred_element_type=jnp.float32
    ) * HEAD_DIM ** (-0.5)
    visible = (
        (key_pos[None, :] <= query_pos[:, None])
        & (key_pos[None, :] >= query_start[:, None])
        & (key_end[None, :] > query_pos[:, None])
    )
    visible = visible[:, None, None, :]
    new_max = jnp.maximum(running_max, jnp.max(jnp.where(visible, scores, NEG_LARGE), axis=-1))
    weights = jnp.where(visible, jnp.exp(scores - new_max[..., None]), 0.0)
    fading = jnp.exp(running_max - new_max)
    weight_sum = weight_sum * fading + jnp.sum(weights, axis=-1)
    weighted = weighted * fading[..., None] + jnp.einsum(
        "rkgn,nkd->rkgd",
        weights.astype(jnp.bfloat16),
        value_block,
        preferred_element_type=jnp.float32,
    )
    return (new_max, weight_sum, weighted)


def attend_all(queries, query_pos, query_start, key_part, value_part, end_part):
    rows = queries.shape[0]
    key_count = key_part.shape[0]
    kv_here = key_part.shape[1] // HEAD_DIM
    query_grid = queries.reshape(rows, kv_here, -1, HEAD_DIM)
    block_len = math.gcd(key_count, 512)
    block_count = key_count // block_len
    items = (
        key_part.reshape(block_count, block_len, kv_here, HEAD_DIM),
        value_part.reshape(block_count, block_len, kv_here, HEAD_DIM),
        end_part.reshape(block_count, block_len),
        jnp.arange(key_count, dtype=jnp.int32).reshape(block_count, block_len),
    )
    start_state = (
        jnp.full(query_grid.shape[:3], NEG_LARGE, jnp.float32),
        jnp.zeros(query_grid.shape[:3], jnp.float32),
        jnp.zeros(query_grid.shape, jnp.float32),
    )

    def one_block(state, item):
        return attend_block(state, query_grid, query_pos, query_start, *item), None

    (_, weight_sum, weighted), _ = lax.scan(one_block, start_state, items)
    return (weighted / weight_sum[..., None]).astype(jnp.bfloat16).reshape(rows, -1)


def any_ring(queries, key_rows, value_rows, doc_start, doc_end, block_target, out_weight):
    rows = queries.shape[0]
    blocks = block_target.shape[0]
    block_rows = rows // blocks
    ctx_count = lax.axis_size("ctx")
    tp_count = lax.axis_size("tp")
    gather = functools.partial(lax.all_gather, axis_name="ctx", axis=0, tiled=True)
    query_pos = lax.axis_index("ctx") * rows + jnp.arange(rows, dtype=jnp.int32)
    attended = attend_all(
        queries, query_pos, doc_start, gather(key_rows), gather(value_rows), gather(doc_end)
    )
    targets = gather(block_target)
    source = jnp.zeros_like(targets).at[targets].set(jnp.arange(targets.size, dtype=jnp.int32))
    source_rows = (source[:, None] * block_rows + jnp.arange(block_rows, dtype=jnp.int32)).reshape(-1)
    balanced = jnp.take(gather(attended), source_rows, axis=0)
    share = jnp.dot(balanced, out_weight, preferred_element_type=jnp.float32).astype(jnp.bfloat16)
    share = share.reshape(ctx_count, tp_count, rows // tp_count, -1)
    summed = lax.psum_scatter(share, "tp", scatter_dimension=1, tiled=True)
    pieces = lax.all_to_all(summed[:, 0], "ctx", split_axis=0, concat_axis=0, tiled=True)
    return jnp.swapaxes(pieces, 0, 1).reshape(rows // tp_count, -1)


def shards(queries, key_rows, value_rows, doc_start, doc_end, block_target, out_weight):
    ctx_count, tp_count = lax.axis_size("ctx"), lax.axis_size("tp")
    rows, blocks = queries.shape[0], block_target.shape[0]
    longest = rows * ctx_count // 2 - rows
    near = longest <= rows and ctx_count == 4 and tp_count == 4 and blocks == 2
    plan = small_ring if near and rows % (4 * blocks * 2) == 0 else any_ring
    return plan(queries, key_rows, value_rows, doc_start, doc_end, block_target, out_weight)


def solution(mesh):
    in_specs = (
        P(("group", "ctx"), "tp"),
        P(("group", "ctx"), "tp"),
        P(("group", "ctx"), "tp"),
        P(("group", "ctx")),
        P(("group", "ctx")),
        P(("group", "ctx")),
        P("tp", "ctx"),
    )
    out_specs = P(("group", "ctx", "tp"), None)
    return jax.shard_map(shards, mesh=mesh, in_specs=in_specs, out_specs=out_specs, check_vma=False)
```

```python
import functools
import math

import jax
import jax.numpy as jnp
from jax import lax
from jax.experimental import pallas as pl
from jax.experimental.pallas import tpu as pltpu
from jax.sharding import PartitionSpec as P

HEAD_DIM = 128
NEG_LARGE = -1e30
END_PART = 128


def vmem(count):
    return [pl.BlockSpec(memory_space=pltpu.VMEM)] * count


def smem(count):
    return [pl.BlockSpec(memory_space=pltpu.SMEM)] * count


def params():
    return pltpu.CompilerParams(vmem_limit_bytes=16 * 1024 * 1024)


def cost(flops, moved):
    return pl.CostEstimate(flops=int(flops), bytes_accessed=int(moved), transcendentals=0)


def column(row):
    size = row.shape[1]
    return jnp.transpose(jnp.broadcast_to(row, (size, size)))


def pack_kernel(k_ref, v_ref, end_ref, message_ref):
    rows, width = k_ref.shape
    message_ref[pl.ds(0, rows), pl.ds(0, width)] = k_ref[...]
    message_ref[pl.ds(0, rows), pl.ds(width, width)] = v_ref[...]
    extra = message_ref.shape[0] - rows
    line = lax.broadcasted_iota(jnp.int32, (extra, rows), 0)
    ends = jnp.broadcast_to(end_ref[...], (extra, rows))
    parts = jnp.where(line == 0, ends // END_PART, jnp.where(line == 1, ends % END_PART, 0))
    message_ref[pl.ds(rows, extra), :] = jnp.zeros((extra, 2 * width), jnp.bfloat16)
    message_ref[pl.ds(rows, extra), pl.ds(0, rows)] = parts.astype(jnp.float32).astype(jnp.bfloat16)


def pack(key_rows, value_rows, ends):
    rows, width = key_rows.shape
    return pl.pallas_call(
        pack_kernel,
        out_shape=jax.ShapeDtypeStruct((rows + 16, 2 * width), jnp.bfloat16),
        in_specs=vmem(3),
        out_specs=pl.BlockSpec(memory_space=pltpu.VMEM),
        cost_estimate=cost(10**9, 8 * key_rows.size),
    )(key_rows, value_rows, ends)


def attend_kernel(blocks, q_ref, halo_ref, k_ref, v_ref, end_ref, st_ref, own_ref, near_ref, *refs):
    plain_ref, noted_ref = refs
    targets = jnp.concatenate([own_ref[...], near_ref[...]], axis=1)
    count = targets.shape[1]
    targets = jnp.broadcast_to(targets.astype(jnp.float32), (8, count)).astype(jnp.bfloat16)
    noted_ref[pl.ds(q_ref.shape[0], 8), :] = jnp.zeros((8, q_ref.shape[1]), jnp.bfloat16)
    noted_ref[pl.ds(q_ref.shape[0], 8), pl.ds(0, count)] = targets
    rows = q_ref.shape[0]
    width = k_ref.shape[1]
    kv_here = width // HEAD_DIM
    group = q_ref.shape[1] // HEAD_DIM // kv_here
    core = lax.axis_index("tp") % 2
    base = lax.axis_index("ctx") * rows
    half = rows // blocks // 2
    query_pos = base + lax.broadcasted_iota(jnp.int32, (rows, rows), 0)
    query_start = column(st_ref[...])
    parts = halo_ref[pl.ds(rows, 16), pl.ds(0, rows)].astype(jnp.float32).astype(jnp.int32)
    masks = []
    for shift, key_end in ((rows, parts[0:1] * END_PART + parts[1:2]), (0, end_ref[...])):
        key_pos = base - shift + lax.broadcasted_iota(jnp.int32, (rows, rows), 1)
        masks.append((key_pos <= query_pos) & (key_pos >= query_start) & (key_end > query_pos))
    visible = jnp.concatenate(masks, axis=1)
    visible = jnp.concatenate([visible] * group, axis=0)
    for kv in range(kv_here):
        keys, values = (
            jnp.concatenate(
                [
                    halo_ref[pl.ds(0, rows), pl.ds(first + kv * HEAD_DIM, HEAD_DIM)],
                    ref[:, pl.ds(kv * HEAD_DIM, HEAD_DIM)],
                ],
                axis=0,
            )
            for first, ref in ((0, k_ref), (width, v_ref))
        )
        query = jnp.concatenate(
            [q_ref[:, pl.ds((kv * group + g) * HEAD_DIM, HEAD_DIM)] for g in range(group)], axis=0
        )
        scores = (
            lax.dot_general(
                query, keys, (((1,), (1,)), ((), ())), preferred_element_type=jnp.float32
            )
            * HEAD_DIM**-0.5
        )
        row_max = jnp.max(jnp.where(visible, scores, NEG_LARGE), axis=1, keepdims=True)
        weights = jnp.where(visible, jnp.exp(scores - row_max), 0.0)
        weight_sum = jnp.sum(weights, axis=1, keepdims=True)
        summed = jnp.dot(
            weights.astype(jnp.bfloat16), values, preferred_element_type=jnp.float32
        )
        attended = (summed / weight_sum).astype(jnp.bfloat16)
        for g in range(group):
            for p in range(blocks):
                for h in range(2):
                    first = g * rows + (p * 2 + h) * half
                    place = pl.multiple_of((h ^ core) * half, half)
                    lanes = pl.ds((kv * group + g) * HEAD_DIM, HEAD_DIM)
                    target_rows = pl.ds(p * 2 * half + place, half)
                    plain_ref[target_rows, lanes] = attended[first : first + half]
                    noted_ref[target_rows, lanes] = attended[first : first + half]


def attend(blocks, queries, halo, keys, values, end, start, own, near):
    rows, features = queries.shape
    sizes = (rows, rows + 8)
    return pl.pallas_call(
        functools.partial(attend_kernel, blocks),
        out_shape=tuple(jax.ShapeDtypeStruct((size, features), jnp.bfloat16) for size in sizes),
        in_specs=vmem(8),
        out_specs=tuple(vmem(2)),
        compiler_params=params(),
        cost_estimate=cost(100 * 10**8, 0),
    )(queries, halo, keys, values, end, start, own, near)


def project_kernel(block_rows, *refs):
    chunks, weight_ref, mine_ref, other_ref = refs[:-3], refs[-3], refs[-2], refs[-1]
    half = block_rows // 2
    whole = [c.shape[0] // block_rows * block_rows for c in chunks]
    stacked = jnp.concatenate([c[pl.ds(0, n), :] for c, n in zip(chunks, whole)], axis=0)
    share = jnp.dot(stacked, weight_ref[...], preferred_element_type=jnp.float32).astype(
        jnp.bfloat16
    )
    for n in range(share.shape[0] // block_rows):
        first = n * block_rows
        mine_ref[pl.ds(n * half, half), :] = share[first : first + half]
        other_ref[pl.ds(n * half, half), :] = share[first + half : first + block_rows]


def project(block_rows, chunks, weight, estimate=None):
    rows = sum(c.shape[0] // block_rows * block_rows for c in chunks)
    out = jax.ShapeDtypeStruct((rows // 2, weight.shape[1]), jnp.bfloat16)
    return pl.pallas_call(
        functools.partial(project_kernel, block_rows),
        out_shape=(out, out),
        in_specs=vmem(len(chunks) + 1),
        out_specs=tuple(vmem(2)),
        compiler_params=params(),
        cost_estimate=estimate or cost(2 * rows * weight.size, 2 * weight.size),
    )(*chunks, weight)


def total_kernel(*refs):
    terms, out_ref = refs[:-1], refs[-1]
    out_ref[...] = sum(t[...].astype(jnp.float32) for t in terms).astype(out_ref.dtype)


def total(terms):
    return pl.pallas_call(
        total_kernel,
        out_shape=jax.ShapeDtypeStruct(terms[0].shape, jnp.bfloat16),
        in_specs=vmem(len(terms)),
        out_specs=pl.BlockSpec(memory_space=pltpu.VMEM),
        compiler_params=params(),
        cost_estimate=cost(10 * 10**8, 0),
    )(*terms)


def pick_kernel(blocks, half, own_ref, near_ref, two_ref, *refs):
    sums, outs = refs[:-4], refs[-4:]
    x = lax.axis_index("tp") // 2
    c = lax.axis_index("ctx")
    pieces = [r[pl.ds(n, half), :] for r in sums for n in range(0, r.shape[0], half)]
    tail = two_ref[pl.ds(two_ref.shape[0] - 8, 8), pl.ds(0, HEAD_DIM)].astype(jnp.float32)
    far = tail[0:1, 0 : 2 * blocks].astype(jnp.int32)
    targets = jnp.concatenate([own_ref[...], near_ref[...], far], axis=1)
    for k in range(4):
        wanted = (c ^ k) * blocks + x
        piece = pieces[0]
        for n in range(1, len(pieces)):
            here = jnp.broadcast_to(targets[:, n : n + 1] == wanted, piece.shape)
            piece = jnp.where(here, pieces[n], piece)
        outs[k][...] = piece


def pick(blocks, own, near, two, sums):
    rows, cols = sum(s.shape[0] for s in sums), sums[0].shape[1]
    half = rows // (4 * blocks)
    out = jax.ShapeDtypeStruct((half, cols), jnp.bfloat16)
    return pl.pallas_call(
        functools.partial(pick_kernel, blocks, half),
        out_shape=(out,) * 4,
        in_specs=vmem(3 + len(sums)),
        out_specs=tuple(vmem(4)),
        compiler_params=params(),
        cost_estimate=cost(4 * rows * cols, 8 * rows * cols),
    )(own, near, two, *sums)


def forward_kernel(got_ref, out_ref):
    out_ref[...] = got_ref[pl.ds(0, out_ref.shape[0]), :]


def forward(rows, got):
    out = jax.ShapeDtypeStruct((rows, got.shape[1]), got.dtype)
    return pl.pallas_call(
        forward_kernel,
        out_shape=out,
        in_specs=vmem(1),
        out_specs=pl.BlockSpec(memory_space=pltpu.VMEM),
        compiler_params=params(),
        cost_estimate=cost(1 * 10**8, 0),
    )(got)


def hold_kernel(near_ref, far_ref, out_ref):
    cols = near_ref.shape[1]
    out_ref[:, pl.ds(0, cols)] = near_ref[...]
    out_ref[:, pl.ds(cols, cols)] = far_ref[...]


def hold(near, far):
    rows, cols = near.shape
    return pl.pallas_call(
        hold_kernel,
        out_shape=jax.ShapeDtypeStruct((rows, 2 * cols), near.dtype),
        in_specs=vmem(2),
        out_specs=pl.BlockSpec(memory_space=pltpu.VMEM),
        compiler_params=params(),
        cost_estimate=cost(0, 8 * near.size),
    )(near, far)


def join_kernel(held_ref, two_ref, one_ref, out_ref):
    cols = one_ref.shape[1]
    c = lax.axis_index("ctx")
    pieces = (held_ref[:, pl.ds(0, cols)], one_ref[...], two_ref[...], held_ref[:, pl.ds(cols, cols)])
    for k in range(4):
        out_ref[:, pl.ds(pl.multiple_of((c ^ k) * cols, cols), cols)] = pieces[k]


def join(held, two, one):
    rows, cols = one.shape
    return pl.pallas_call(
        join_kernel,
        out_shape=jax.ShapeDtypeStruct((rows, 4 * cols), jnp.bfloat16),
        in_specs=vmem(3),
        out_specs=pl.BlockSpec(memory_space=pltpu.VMEM),
        compiler_params=params(),
        cost_estimate=cost(0, 16 * one.size),
    )(held, two, one)


def flip(array, axis, bits):
    return lax.ppermute(array, axis, [(i, i ^ bits) for i in range(4)])


def core_total(mine, other):
    return total((mine, flip(other, "tp", 1)))


def stack_kernel(done_ref, mine_ref, got_ref, out_ref):
    rows = done_ref.shape[0]
    out_ref[pl.ds(0, rows), :] = done_ref[...]
    both = mine_ref[...].astype(jnp.float32) + got_ref[...].astype(jnp.float32)
    out_ref[pl.ds(rows, mine_ref.shape[0]), :] = both.astype(out_ref.dtype)


def stack_core_total(done, mine, other):
    rows = done.shape[0] + mine.shape[0]
    return pl.pallas_call(
        stack_kernel,
        out_shape=jax.ShapeDtypeStruct((rows, mine.shape[1]), jnp.bfloat16),
        in_specs=vmem(3),
        out_specs=pl.BlockSpec(memory_space=pltpu.VMEM),
        compiler_params=params(),
        cost_estimate=cost(mine.size, 8 * mine.size),
    )(done, mine, flip(other, "tp", 1))


def chip_total(share):
    return total((share, flip(share, "tp", 2)))


def after(value, *others):
    return lax.optimization_barrier((value, *others))[0]


def small_ring(queries, key_rows, value_rows, doc_start, doc_end, block_target, out_weight):
    rows = queries.shape[0]
    blocks = block_target.shape[0]
    block_rows = rows // blocks
    end, start = doc_end.reshape(1, rows), doc_start.reshape(1, rows)
    message = pack(key_rows, value_rows, end)
    halo = lax.ppermute(message, "ctx", [(0, 1), (1, 2), (2, 3)])
    own_target = block_target.reshape(1, blocks)
    near_target = flip(after(own_target, message), "ctx", 1)
    halo = after(halo, near_target)
    plain, noted = attend(
        blocks, queries, halo, key_rows, value_rows, end, start, own_target, near_target
    )
    rows_2, rows_1 = flip(noted, "ctx", 2), flip(plain, "ctx", 1)
    rows_3 = flip(forward(rows, rows_2), "ctx", 1)
    sum_a = chip_total(core_total(*project(block_rows, (plain,), out_weight, cost(10 * 10**8, 0))))
    share_b = core_total(*project(block_rows, (rows_1, rows_2), out_weight, cost(30 * 10**8, 0)))
    share_c = core_total(*project(block_rows, (rows_3,), out_weight, cost(30 * 10**8, 0)))
    sums = (sum_a, chip_total(share_b), chip_total(share_c))
    kept, *sent = pick(blocks, own_target, near_target, rows_2, sums)
    got_3, got_2, got_1 = (flip(sent[k - 1], "ctx", k) for k in (3, 2, 1))
    return join(hold(kept, got_3), got_2, got_1)


def attend_block(soft_state, query_grid, query_pos, query_start, key_block, value_block, key_end, key_pos):
    running_max, weight_sum, weighted = soft_state
    scores = jnp.einsum(
        "rkgd,nkd->rkgn", query_grid, key_block, preferred_element_type=jnp.float32
    ) * HEAD_DIM ** (-0.5)
    visible = (
        (key_pos[None, :] <= query_pos[:, None])
        & (key_pos[None, :] >= query_start[:, None])
        & (key_end[None, :] > query_pos[:, None])
    )
    visible = visible[:, None, None, :]
    new_max = jnp.maximum(running_max, jnp.max(jnp.where(visible, scores, NEG_LARGE), axis=-1))
    weights = jnp.where(visible, jnp.exp(scores - new_max[..., None]), 0.0)
    fading = jnp.exp(running_max - new_max)
    weight_sum = weight_sum * fading + jnp.sum(weights, axis=-1)
    weighted = weighted * fading[..., None] + jnp.einsum(
        "rkgn,nkd->rkgd",
        weights.astype(jnp.bfloat16),
        value_block,
        preferred_element_type=jnp.float32,
    )
    return (new_max, weight_sum, weighted)


def attend_all(queries, query_pos, query_start, key_part, value_part, end_part):
    rows = queries.shape[0]
    key_count = key_part.shape[0]
    kv_here = key_part.shape[1] // HEAD_DIM
    query_grid = queries.reshape(rows, kv_here, -1, HEAD_DIM)
    block_len = math.gcd(key_count, 512)
    block_count = key_count // block_len
    items = (
        key_part.reshape(block_count, block_len, kv_here, HEAD_DIM),
        value_part.reshape(block_count, block_len, kv_here, HEAD_DIM),
        end_part.reshape(block_count, block_len),
        jnp.arange(key_count, dtype=jnp.int32).reshape(block_count, block_len),
    )
    start_state = (
        jnp.full(query_grid.shape[:3], NEG_LARGE, jnp.float32),
        jnp.zeros(query_grid.shape[:3], jnp.float32),
        jnp.zeros(query_grid.shape, jnp.float32),
    )

    def one_block(state, item):
        return attend_block(state, query_grid, query_pos, query_start, *item), None

    (_, weight_sum, weighted), _ = lax.scan(one_block, start_state, items)
    return (weighted / weight_sum[..., None]).astype(jnp.bfloat16).reshape(rows, -1)


def any_ring(queries, key_rows, value_rows, doc_start, doc_end, block_target, out_weight):
    rows = queries.shape[0]
    blocks = block_target.shape[0]
    block_rows = rows // blocks
    ctx_count = lax.axis_size("ctx")
    tp_count = lax.axis_size("tp")
    gather = functools.partial(lax.all_gather, axis_name="ctx", axis=0, tiled=True)
    query_pos = lax.axis_index("ctx") * rows + jnp.arange(rows, dtype=jnp.int32)
    attended = attend_all(
        queries, query_pos, doc_start, gather(key_rows), gather(value_rows), gather(doc_end)
    )
    targets = gather(block_target)
    source = jnp.zeros_like(targets).at[targets].set(jnp.arange(targets.size, dtype=jnp.int32))
    source_rows = (source[:, None] * block_rows + jnp.arange(block_rows, dtype=jnp.int32)).reshape(-1)
    balanced = jnp.take(gather(attended), source_rows, axis=0)
    share = jnp.dot(balanced, out_weight, preferred_element_type=jnp.float32).astype(jnp.bfloat16)
    share = share.reshape(ctx_count, tp_count, rows // tp_count, -1)
    summed = lax.psum_scatter(share, "tp", scatter_dimension=1, tiled=True)
    pieces = lax.all_to_all(summed[:, 0], "ctx", split_axis=0, concat_axis=0, tiled=True)
    return jnp.swapaxes(pieces, 0, 1).reshape(rows // tp_count, -1)


def shards(queries, key_rows, value_rows, doc_start, doc_end, block_target, out_weight):
    ctx_count, tp_count = lax.axis_size("ctx"), lax.axis_size("tp")
    rows, blocks = queries.shape[0], block_target.shape[0]
    longest = rows * ctx_count // 2 - rows
    near = longest <= rows and ctx_count == 4 and tp_count == 4 and blocks == 2
    plan = small_ring if near and rows % (4 * blocks * 2) == 0 else any_ring
    return plan(queries, key_rows, value_rows, doc_start, doc_end, block_target, out_weight)


def solution(mesh):
    in_specs = (
        P(("group", "ctx"), "tp"),
        P(("group", "ctx"), "tp"),
        P(("group", "ctx"), "tp"),
        P(("group", "ctx")),
        P(("group", "ctx")),
        P(("group", "ctx")),
        P("tp", "ctx"),
    )
    out_specs = P(("group", "ctx", "tp"), None)
    return jax.shard_map(shards, mesh=mesh, in_specs=in_specs, out_specs=out_specs, check_vma=False)
```

```python
import functools
import math

import jax
import jax.numpy as jnp
from jax import lax
from jax.experimental import pallas as pl
from jax.experimental.pallas import tpu as pltpu
from jax.sharding import PartitionSpec as P

HEAD_DIM = 128
NEG_LARGE = -1e30
END_PART = 128


def vmem(count):
    return [pl.BlockSpec(memory_space=pltpu.VMEM)] * count


def smem(count):
    return [pl.BlockSpec(memory_space=pltpu.SMEM)] * count


def params():
    return pltpu.CompilerParams(vmem_limit_bytes=16 * 1024 * 1024)


def cost(flops, moved):
    return pl.CostEstimate(flops=int(flops), bytes_accessed=int(moved), transcendentals=0)


def column(row):
    size = row.shape[1]
    return jnp.transpose(jnp.broadcast_to(row, (size, size)))


def pack_kernel(k_ref, v_ref, end_ref, target_ref, message_ref):
    rows, width = k_ref.shape
    message_ref[pl.ds(0, rows), pl.ds(0, width)] = k_ref[...]
    message_ref[pl.ds(0, rows), pl.ds(width, width)] = v_ref[...]
    extra = message_ref.shape[0] - rows
    line = lax.broadcasted_iota(jnp.int32, (extra, rows), 0)
    ends = jnp.broadcast_to(end_ref[...], (extra, rows))
    parts = jnp.where(line == 0, ends // END_PART, jnp.where(line == 1, ends % END_PART, 0))
    message_ref[pl.ds(rows, extra), :] = jnp.zeros((extra, 2 * width), jnp.bfloat16)
    message_ref[pl.ds(rows, extra), pl.ds(0, rows)] = parts.astype(jnp.float32).astype(jnp.bfloat16)
    targets = jnp.broadcast_to(target_ref[...].astype(jnp.float32), (extra, target_ref.shape[1]))
    message_ref[pl.ds(rows, extra), pl.ds(rows, target_ref.shape[1])] = targets.astype(jnp.bfloat16)


def pack(key_rows, value_rows, ends, targets):
    rows, width = key_rows.shape
    return pl.pallas_call(
        pack_kernel,
        out_shape=jax.ShapeDtypeStruct((rows + 16, 2 * width), jnp.bfloat16),
        in_specs=vmem(4),
        out_specs=pl.BlockSpec(memory_space=pltpu.VMEM),
        cost_estimate=cost(10**9, 8 * key_rows.size),
    )(key_rows, value_rows, ends, targets)


def attend_kernel(
    blocks, q_ref, flip_ref, mid_ref, k_ref, v_ref, end_ref, st_ref, own_ref, plain_ref, noted_ref
):
    across = lax.axis_index("ctx") % 2 == 0
    halo = jnp.where(across, mid_ref[...], flip_ref[...])
    near = flip_ref[pl.ds(k_ref.shape[0], 16), pl.ds(k_ref.shape[0], HEAD_DIM)]
    near = near[0:1, 0:blocks].astype(jnp.float32)
    targets = jnp.concatenate([own_ref[...].astype(jnp.float32), near], axis=1)
    count = targets.shape[1]
    targets = jnp.broadcast_to(targets, (8, count)).astype(jnp.bfloat16)
    noted_ref[pl.ds(q_ref.shape[0], 8), :] = jnp.zeros((8, q_ref.shape[1]), jnp.bfloat16)
    noted_ref[pl.ds(q_ref.shape[0], 8), pl.ds(0, count)] = targets
    rows = q_ref.shape[0]
    width = k_ref.shape[1]
    kv_here = width // HEAD_DIM
    group = q_ref.shape[1] // HEAD_DIM // kv_here
    core = lax.axis_index("tp") % 2
    base = lax.axis_index("ctx") * rows
    half = rows // blocks // 2
    query_pos = base + lax.broadcasted_iota(jnp.int32, (rows, rows), 0)
    query_start = column(st_ref[...])
    parts = halo[rows : rows + 16, 0:rows].astype(jnp.float32).astype(jnp.int32)
    masks = []
    for shift, key_end in ((rows, parts[0:1] * END_PART + parts[1:2]), (0, end_ref[...])):
        key_pos = base - shift + lax.broadcasted_iota(jnp.int32, (rows, rows), 1)
        masks.append((key_pos <= query_pos) & (key_pos >= query_start) & (key_end > query_pos))
    visible = jnp.concatenate(masks, axis=1)
    visible = jnp.concatenate([visible] * group, axis=0)
    for kv in range(kv_here):
        keys, values = (
            jnp.concatenate(
                [
                    halo[0:rows, first + kv * HEAD_DIM : first + (kv + 1) * HEAD_DIM],
                    ref[:, pl.ds(kv * HEAD_DIM, HEAD_DIM)],
                ],
                axis=0,
            )
            for first, ref in ((0, k_ref), (width, v_ref))
        )
        query = jnp.concatenate(
            [q_ref[:, pl.ds((kv * group + g) * HEAD_DIM, HEAD_DIM)] for g in range(group)], axis=0
        )
        scores = (
            lax.dot_general(
                query, keys, (((1,), (1,)), ((), ())), preferred_element_type=jnp.float32
            )
            * HEAD_DIM**-0.5
        )
        row_max = jnp.max(jnp.where(visible, scores, NEG_LARGE), axis=1, keepdims=True)
        weights = jnp.where(visible, jnp.exp(scores - row_max), 0.0)
        weight_sum = jnp.sum(weights, axis=1, keepdims=True)
        summed = jnp.dot(
            weights.astype(jnp.bfloat16), values, preferred_element_type=jnp.float32
        )
        attended = (summed / weight_sum).astype(jnp.bfloat16)
        for g in range(group):
            for p in range(blocks):
                for h in range(2):
                    first = g * rows + (p * 2 + h) * half
                    place = pl.multiple_of((h ^ core) * half, half)
                    lanes = pl.ds((kv * group + g) * HEAD_DIM, HEAD_DIM)
                    target_rows = pl.ds(p * 2 * half + place, half)
                    plain_ref[target_rows, lanes] = attended[first : first + half]
                    noted_ref[target_rows, lanes] = attended[first : first + half]


def attend(blocks, queries, flipped, mid, keys, values, end, start, own):
    rows, features = queries.shape
    sizes = (rows, rows + 8)
    return pl.pallas_call(
        functools.partial(attend_kernel, blocks),
        out_shape=tuple(jax.ShapeDtypeStruct((size, features), jnp.bfloat16) for size in sizes),
        in_specs=vmem(8),
        out_specs=tuple(vmem(2)),
        compiler_params=params(),
        cost_estimate=cost(10 * 10**8, 0),
    )(queries, flipped, mid, keys, values, end, start, own)


def project_kernel(block_rows, *refs):
    chunks, weight_ref, mine_ref, other_ref = refs[:-3], refs[-3], refs[-2], refs[-1]
    half = block_rows // 2
    whole = [c.shape[0] // block_rows * block_rows for c in chunks]
    stacked = jnp.concatenate([c[pl.ds(0, n), :] for c, n in zip(chunks, whole)], axis=0)
    share = jnp.dot(stacked, weight_ref[...], preferred_element_type=jnp.float32).astype(
        jnp.bfloat16
    )
    for n in range(share.shape[0] // block_rows):
        first = n * block_rows
        mine_ref[pl.ds(n * half, half), :] = share[first : first + half]
        other_ref[pl.ds(n * half, half), :] = share[first + half : first + block_rows]


def project(block_rows, chunks, weight, estimate=None):
    rows = sum(c.shape[0] // block_rows * block_rows for c in chunks)
    out = jax.ShapeDtypeStruct((rows // 2, weight.shape[1]), jnp.bfloat16)
    return pl.pallas_call(
        functools.partial(project_kernel, block_rows),
        out_shape=(out, out),
        in_specs=vmem(len(chunks) + 1),
        out_specs=tuple(vmem(2)),
        compiler_params=params(),
        cost_estimate=estimate or cost(2 * rows * weight.size, 2 * weight.size),
    )(*chunks, weight)


def total_kernel(*refs):
    terms, out_ref = refs[:-1], refs[-1]
    out_ref[...] = sum(t[...].astype(jnp.float32) for t in terms).astype(out_ref.dtype)


def total(terms):
    return pl.pallas_call(
        total_kernel,
        out_shape=jax.ShapeDtypeStruct(terms[0].shape, jnp.bfloat16),
        in_specs=vmem(len(terms)),
        out_specs=pl.BlockSpec(memory_space=pltpu.VMEM),
        compiler_params=params(),
        cost_estimate=cost(4 * terms[0].size, 10 * terms[0].size),
    )(*terms)


def note(ref, count):
    tail = ref[pl.ds(ref.shape[0] - 8, 8), pl.ds(0, HEAD_DIM)].astype(jnp.float32)
    return tail[0:1, 0:count].astype(jnp.int32)


def pick_kernel(blocks, half, noted_ref, two_ref, *refs):
    sums, outs = refs[:-4], refs[-4:]
    x = lax.axis_index("tp") // 2
    c = lax.axis_index("ctx")
    pieces = [r[pl.ds(n, half), :] for r in sums for n in range(0, r.shape[0], half)]
    targets = jnp.concatenate([note(r, 2 * blocks) for r in (noted_ref, two_ref)], axis=1)
    for k in range(4):
        wanted = (c ^ k) * blocks + x
        piece = pieces[0]
        for n in range(1, len(pieces)):
            here = jnp.broadcast_to(targets[:, n : n + 1] == wanted, piece.shape)
            piece = jnp.where(here, pieces[n], piece)
        outs[k][...] = piece


def pick(blocks, noted, two, sums):
    rows, cols = sum(s.shape[0] for s in sums), sums[0].shape[1]
    half = rows // (4 * blocks)
    out = jax.ShapeDtypeStruct((half, cols), jnp.bfloat16)
    return pl.pallas_call(
        functools.partial(pick_kernel, blocks, half),
        out_shape=(out,) * 4,
        in_specs=vmem(2 + len(sums)),
        out_specs=tuple(vmem(4)),
        compiler_params=params(),
        cost_estimate=cost(4 * rows * cols, 8 * rows * cols),
    )(noted, two, *sums)


def forward_kernel(got_ref, out_ref):
    out_ref[...] = got_ref[pl.ds(0, out_ref.shape[0]), :]


def forward(rows, got):
    out = jax.ShapeDtypeStruct((rows, got.shape[1]), got.dtype)
    return pl.pallas_call(
        forward_kernel,
        out_shape=out,
        in_specs=vmem(1),
        out_specs=pl.BlockSpec(memory_space=pltpu.VMEM),
        compiler_params=params(),
        cost_estimate=cost(0, 0),
    )(got)


def hold_kernel(near_ref, far_ref, out_ref):
    cols = near_ref.shape[1]
    out_ref[:, pl.ds(0, cols)] = near_ref[...]
    out_ref[:, pl.ds(cols, cols)] = far_ref[...]


def hold(near, far):
    rows, cols = near.shape
    return pl.pallas_call(
        hold_kernel,
        out_shape=jax.ShapeDtypeStruct((rows, 2 * cols), near.dtype),
        in_specs=vmem(2),
        out_specs=pl.BlockSpec(memory_space=pltpu.VMEM),
        compiler_params=params(),
        cost_estimate=cost(0, 8 * near.size),
    )(near, far)


def join_kernel(held_ref, two_ref, one_ref, out_ref):
    cols = one_ref.shape[1]
    c = lax.axis_index("ctx")
    pieces = (held_ref[:, pl.ds(0, cols)], one_ref[...], two_ref[...], held_ref[:, pl.ds(cols, cols)])
    for k in range(4):
        out_ref[:, pl.ds(pl.multiple_of((c ^ k) * cols, cols), cols)] = pieces[k]


def join(held, two, one):
    rows, cols = one.shape
    return pl.pallas_call(
        join_kernel,
        out_shape=jax.ShapeDtypeStruct((rows, 4 * cols), jnp.bfloat16),
        in_specs=vmem(3),
        out_specs=pl.BlockSpec(memory_space=pltpu.VMEM),
        compiler_params=params(),
        cost_estimate=cost(0, 16 * one.size),
    )(held, two, one)


def flip(array, axis, bits):
    return lax.ppermute(array, axis, [(i, i ^ bits) for i in range(4)])


def core_total(mine, other):
    return total((mine, flip(other, "tp", 1)))


def stack_kernel(done_ref, mine_ref, got_ref, out_ref):
    rows = done_ref.shape[0]
    out_ref[pl.ds(0, rows), :] = done_ref[...]
    both = mine_ref[...].astype(jnp.float32) + got_ref[...].astype(jnp.float32)
    out_ref[pl.ds(rows, mine_ref.shape[0]), :] = both.astype(out_ref.dtype)


def stack_core_total(done, mine, other):
    rows = done.shape[0] + mine.shape[0]
    return pl.pallas_call(
        stack_kernel,
        out_shape=jax.ShapeDtypeStruct((rows, mine.shape[1]), jnp.bfloat16),
        in_specs=vmem(3),
        out_specs=pl.BlockSpec(memory_space=pltpu.VMEM),
        compiler_params=params(),
        cost_estimate=cost(mine.size, 8 * mine.size),
    )(done, mine, flip(other, "tp", 1))


def chip_total(share):
    return total((share, flip(share, "tp", 2)))


def after(value, *others):
    return lax.optimization_barrier((value, *others))[0]


def small_ring(queries, key_rows, value_rows, doc_start, doc_end, block_target, out_weight):
    rows = queries.shape[0]
    blocks = block_target.shape[0]
    block_rows = rows // blocks
    end, start = doc_end.reshape(1, rows), doc_start.reshape(1, rows)
    own_target = block_target.reshape(1, blocks)
    message = pack(key_rows, value_rows, end, own_target)
    flipped = flip(message, "ctx", 1)
    middle = [(4 * c + t, 4 * (3 - c) + t if c in (1, 2) else 4 * c + (t ^ 1)) for c in range(4) for t in range(4)]
    mid = lax.ppermute(message, ("ctx", "tp"), middle)
    plain, noted = attend(
        blocks, queries, flipped, mid, key_rows, value_rows, end, start, own_target
    )
    rows_1, rows_2 = flip(plain, "ctx", 1), flip(noted, "ctx", 2)
    rows_3 = flip(forward(rows, rows_2), "ctx", 1)
    share_a = core_total(*project(block_rows, (plain, rows_1), out_weight, cost(30 * 10**8, 0)))
    rows_2 = after(rows_2, share_a)
    share_ab = stack_core_total(share_a, *project(block_rows, (rows_2,), out_weight))
    rows_3 = after(rows_3, share_ab)
    share_c = core_total(*project(block_rows, (rows_3,), out_weight))
    sums = (chip_total(share_ab), chip_total(share_c))
    kept, *sent = pick(blocks, noted, rows_2, sums)
    got_3, got_2, got_1 = (flip(sent[k - 1], "ctx", k) for k in (3, 2, 1))
    return join(hold(kept, got_3), got_2, got_1)


def attend_block(soft_state, query_grid, query_pos, query_start, key_block, value_block, key_end, key_pos):
    running_max, weight_sum, weighted = soft_state
    scores = jnp.einsum(
        "rkgd,nkd->rkgn", query_grid, key_block, preferred_element_type=jnp.float32
    ) * HEAD_DIM ** (-0.5)
    visible = (
        (key_pos[None, :] <= query_pos[:, None])
        & (key_pos[None, :] >= query_start[:, None])
        & (key_end[None, :] > query_pos[:, None])
    )
    visible = visible[:, None, None, :]
    new_max = jnp.maximum(running_max, jnp.max(jnp.where(visible, scores, NEG_LARGE), axis=-1))
    weights = jnp.where(visible, jnp.exp(scores - new_max[..., None]), 0.0)
    fading = jnp.exp(running_max - new_max)
    weight_sum = weight_sum * fading + jnp.sum(weights, axis=-1)
    weighted = weighted * fading[..., None] + jnp.einsum(
        "rkgn,nkd->rkgd",
        weights.astype(jnp.bfloat16),
        value_block,
        preferred_element_type=jnp.float32,
    )
    return (new_max, weight_sum, weighted)


def attend_all(queries, query_pos, query_start, key_part, value_part, end_part):
    rows = queries.shape[0]
    key_count = key_part.shape[0]
    kv_here = key_part.shape[1] // HEAD_DIM
    query_grid = queries.reshape(rows, kv_here, -1, HEAD_DIM)
    block_len = math.gcd(key_count, 512)
    block_count = key_count // block_len
    items = (
        key_part.reshape(block_count, block_len, kv_here, HEAD_DIM),
        value_part.reshape(block_count, block_len, kv_here, HEAD_DIM),
        end_part.reshape(block_count, block_len),
        jnp.arange(key_count, dtype=jnp.int32).reshape(block_count, block_len),
    )
    start_state = (
        jnp.full(query_grid.shape[:3], NEG_LARGE, jnp.float32),
        jnp.zeros(query_grid.shape[:3], jnp.float32),
        jnp.zeros(query_grid.shape, jnp.float32),
    )

    def one_block(state, item):
        return attend_block(state, query_grid, query_pos, query_start, *item), None

    (_, weight_sum, weighted), _ = lax.scan(one_block, start_state, items)
    return (weighted / weight_sum[..., None]).astype(jnp.bfloat16).reshape(rows, -1)


def any_ring(queries, key_rows, value_rows, doc_start, doc_end, block_target, out_weight):
    rows = queries.shape[0]
    blocks = block_target.shape[0]
    block_rows = rows // blocks
    ctx_count = lax.axis_size("ctx")
    tp_count = lax.axis_size("tp")
    gather = functools.partial(lax.all_gather, axis_name="ctx", axis=0, tiled=True)
    query_pos = lax.axis_index("ctx") * rows + jnp.arange(rows, dtype=jnp.int32)
    attended = attend_all(
        queries, query_pos, doc_start, gather(key_rows), gather(value_rows), gather(doc_end)
    )
    targets = gather(block_target)
    source = jnp.zeros_like(targets).at[targets].set(jnp.arange(targets.size, dtype=jnp.int32))
    source_rows = (source[:, None] * block_rows + jnp.arange(block_rows, dtype=jnp.int32)).reshape(-1)
    balanced = jnp.take(gather(attended), source_rows, axis=0)
    share = jnp.dot(balanced, out_weight, preferred_element_type=jnp.float32).astype(jnp.bfloat16)
    share = share.reshape(ctx_count, tp_count, rows // tp_count, -1)
    summed = lax.psum_scatter(share, "tp", scatter_dimension=1, tiled=True)
    pieces = lax.all_to_all(summed[:, 0], "ctx", split_axis=0, concat_axis=0, tiled=True)
    return jnp.swapaxes(pieces, 0, 1).reshape(rows // tp_count, -1)


def shards(queries, key_rows, value_rows, doc_start, doc_end, block_target, out_weight):
    ctx_count, tp_count = lax.axis_size("ctx"), lax.axis_size("tp")
    rows, blocks = queries.shape[0], block_target.shape[0]
    longest = rows * ctx_count // 2 - rows
    near = longest <= rows and ctx_count == 4 and tp_count == 4 and blocks == 2
    plan = small_ring if near and rows % (4 * blocks * 2) == 0 else any_ring
    return plan(queries, key_rows, value_rows, doc_start, doc_end, block_target, out_weight)


def solution(mesh):
    in_specs = (
        P(("group", "ctx"), "tp"),
        P(("group", "ctx"), "tp"),
        P(("group", "ctx"), "tp"),
        P(("group", "ctx")),
        P(("group", "ctx")),
        P(("group", "ctx")),
        P("tp", "ctx"),
    )
    out_specs = P(("group", "ctx", "tp"), None)
    return jax.shard_map(shards, mesh=mesh, in_specs=in_specs, out_specs=out_specs, check_vma=False)
```

```python
import functools
import math

import jax
import jax.numpy as jnp
from jax import lax
from jax.experimental import pallas as pl
from jax.experimental.pallas import tpu as pltpu
from jax.sharding import PartitionSpec as P

HEAD_DIM = 128
NEG_LARGE = -1e30
END_PART = 128


def vmem(count):
    return [pl.BlockSpec(memory_space=pltpu.VMEM)] * count


def smem(count):
    return [pl.BlockSpec(memory_space=pltpu.SMEM)] * count


def params():
    return pltpu.CompilerParams(vmem_limit_bytes=16 * 1024 * 1024)


def cost(flops, moved):
    return pl.CostEstimate(flops=int(flops), bytes_accessed=int(moved), transcendentals=0)


def column(row):
    size = row.shape[1]
    return jnp.transpose(jnp.broadcast_to(row, (size, size)))


def pack_kernel(k_ref, v_ref, end_ref, target_ref, message_ref):
    rows, width = k_ref.shape
    message_ref[pl.ds(0, rows), pl.ds(0, width)] = k_ref[...]
    message_ref[pl.ds(0, rows), pl.ds(width, width)] = v_ref[...]
    extra = message_ref.shape[0] - rows
    line = lax.broadcasted_iota(jnp.int32, (extra, rows), 0)
    ends = jnp.broadcast_to(end_ref[...], (extra, rows))
    parts = jnp.where(line == 0, ends // END_PART, jnp.where(line == 1, ends % END_PART, 0))
    message_ref[pl.ds(rows, extra), :] = jnp.zeros((extra, 2 * width), jnp.bfloat16)
    message_ref[pl.ds(rows, extra), pl.ds(0, rows)] = parts.astype(jnp.float32).astype(jnp.bfloat16)
    targets = jnp.broadcast_to(target_ref[...].astype(jnp.float32), (extra, target_ref.shape[1]))
    message_ref[pl.ds(rows, extra), pl.ds(rows, target_ref.shape[1])] = targets.astype(jnp.bfloat16)


def pack(key_rows, value_rows, ends, targets):
    rows, width = key_rows.shape
    return pl.pallas_call(
        pack_kernel,
        out_shape=jax.ShapeDtypeStruct((rows + 16, 2 * width), jnp.bfloat16),
        in_specs=vmem(4),
        out_specs=pl.BlockSpec(memory_space=pltpu.VMEM),
        cost_estimate=cost(10**9, 8 * key_rows.size),
    )(key_rows, value_rows, ends, targets)


def attend_kernel(
    blocks, q_ref, flip_ref, mid_ref, k_ref, v_ref, end_ref, st_ref, own_ref, plain_ref, *part_refs
):
    across = lax.axis_index("ctx") % 2 == 0
    halo = jnp.where(across, mid_ref[...], flip_ref[...])
    near = flip_ref[pl.ds(k_ref.shape[0], 16), pl.ds(k_ref.shape[0], HEAD_DIM)]
    near = near[0:1, 0:blocks].astype(jnp.float32)
    targets = jnp.concatenate([own_ref[...].astype(jnp.float32), near], axis=1)
    count = targets.shape[1]
    targets = jnp.broadcast_to(targets, (8, count)).astype(jnp.bfloat16)
    below = pl.ds(q_ref.shape[0] // blocks, 8)
    part_refs[0][below, :] = jnp.zeros((8, q_ref.shape[1]), jnp.bfloat16)
    part_refs[0][below, pl.ds(0, count)] = targets
    rows = q_ref.shape[0]
    width = k_ref.shape[1]
    kv_here = width // HEAD_DIM
    group = q_ref.shape[1] // HEAD_DIM // kv_here
    core = lax.axis_index("tp") % 2
    base = lax.axis_index("ctx") * rows
    half = rows // blocks // 2
    query_pos = base + lax.broadcasted_iota(jnp.int32, (rows, rows), 0)
    query_start = column(st_ref[...])
    parts = halo[rows : rows + 16, 0:rows].astype(jnp.float32).astype(jnp.int32)
    masks = []
    for shift, key_end in ((rows, parts[0:1] * END_PART + parts[1:2]), (0, end_ref[...])):
        key_pos = base - shift + lax.broadcasted_iota(jnp.int32, (rows, rows), 1)
        masks.append((key_pos <= query_pos) & (key_pos >= query_start) & (key_end > query_pos))
    visible = jnp.concatenate(masks, axis=1)
    visible = jnp.concatenate([visible] * group, axis=0)
    for kv in range(kv_here):
        keys, values = (
            jnp.concatenate(
                [
                    halo[0:rows, first + kv * HEAD_DIM : first + (kv + 1) * HEAD_DIM],
                    ref[:, pl.ds(kv * HEAD_DIM, HEAD_DIM)],
                ],
                axis=0,
            )
            for first, ref in ((0, k_ref), (width, v_ref))
        )
        query = jnp.concatenate(
            [q_ref[:, pl.ds((kv * group + g) * HEAD_DIM, HEAD_DIM)] for g in range(group)], axis=0
        )
        scores = (
            lax.dot_general(
                query, keys, (((1,), (1,)), ((), ())), preferred_element_type=jnp.float32
            )
            * HEAD_DIM**-0.5
        )
        row_max = jnp.max(jnp.where(visible, scores, NEG_LARGE), axis=1, keepdims=True)
        weights = jnp.where(visible, jnp.exp(scores - row_max), 0.0)
        weight_sum = jnp.sum(weights, axis=1, keepdims=True)
        summed = jnp.dot(
            weights.astype(jnp.bfloat16), values, preferred_element_type=jnp.float32
        )
        attended = (summed / weight_sum).astype(jnp.bfloat16)
        for g in range(group):
            for p in range(blocks):
                for h in range(2):
                    first = g * rows + (p * 2 + h) * half
                    place = pl.multiple_of((h ^ core) * half, half)
                    lanes = pl.ds((kv * group + g) * HEAD_DIM, HEAD_DIM)
                    target_rows = pl.ds(p * 2 * half + place, half)
                    plain_ref[target_rows, lanes] = attended[first : first + half]
                    part_refs[p][pl.ds(place, half), lanes] = attended[first : first + half]


def attend(blocks, queries, flipped, mid, keys, values, end, start, own):
    rows, features = queries.shape
    sizes = (rows, rows // blocks + 8) + (rows // blocks,) * (blocks - 1)
    return pl.pallas_call(
        functools.partial(attend_kernel, blocks),
        out_shape=tuple(jax.ShapeDtypeStruct((size, features), jnp.bfloat16) for size in sizes),
        in_specs=vmem(8),
        out_specs=tuple(vmem(1 + blocks)),
        compiler_params=params(),
        cost_estimate=cost(8 * rows * rows * features, 6 * queries.size),
    )(queries, flipped, mid, keys, values, end, start, own)


def project_kernel(block_rows, *refs):
    chunks, weight_ref, mine_ref, other_ref = refs[:-3], refs[-3], refs[-2], refs[-1]
    half = block_rows // 2
    whole = [c.shape[0] // block_rows * block_rows for c in chunks]
    stacked = jnp.concatenate([c[pl.ds(0, n), :] for c, n in zip(chunks, whole)], axis=0)
    share = jnp.dot(stacked, weight_ref[...], preferred_element_type=jnp.float32).astype(
        jnp.bfloat16
    )
    for n in range(share.shape[0] // block_rows):
        first = n * block_rows
        mine_ref[pl.ds(n * half, half), :] = share[first : first + half]
        other_ref[pl.ds(n * half, half), :] = share[first + half : first + block_rows]


def project(block_rows, chunks, weight, estimate=None):
    rows = sum(c.shape[0] // block_rows * block_rows for c in chunks)
    out = jax.ShapeDtypeStruct((rows // 2, weight.shape[1]), jnp.bfloat16)
    return pl.pallas_call(
        functools.partial(project_kernel, block_rows),
        out_shape=(out, out),
        in_specs=vmem(len(chunks) + 1),
        out_specs=tuple(vmem(2)),
        compiler_params=params(),
        cost_estimate=estimate or cost(2 * rows * weight.size, 2 * weight.size),
    )(*chunks, weight)


def total_kernel(*refs):
    terms, out_ref = refs[:-1], refs[-1]
    out_ref[...] = sum(t[...].astype(jnp.float32) for t in terms).astype(out_ref.dtype)


def total(terms):
    return pl.pallas_call(
        total_kernel,
        out_shape=jax.ShapeDtypeStruct(terms[0].shape, jnp.bfloat16),
        in_specs=vmem(len(terms)),
        out_specs=pl.BlockSpec(memory_space=pltpu.VMEM),
        compiler_params=params(),
        cost_estimate=cost(4 * terms[0].size, 10 * terms[0].size),
    )(*terms)


def note(ref, count):
    tail = ref[pl.ds(ref.shape[0] - 8, 8), pl.ds(0, HEAD_DIM)].astype(jnp.float32)
    return tail[0:1, 0:count].astype(jnp.int32)


def pick_kernel(blocks, half, noted_ref, two_ref, *refs):
    sums, outs = refs[:-4], refs[-4:]
    x = lax.axis_index("tp") // 2
    c = lax.axis_index("ctx")
    pieces = [r[pl.ds(n, half), :] for r in sums for n in range(0, r.shape[0], half)]
    targets = jnp.concatenate([note(r, 2 * blocks) for r in (noted_ref, two_ref)], axis=1)
    for k in range(4):
        wanted = (c ^ k) * blocks + x
        piece = pieces[0]
        for n in range(1, len(pieces)):
            here = jnp.broadcast_to(targets[:, n : n + 1] == wanted, piece.shape)
            piece = jnp.where(here, pieces[n], piece)
        outs[k][...] = piece


def pick(blocks, noted, two, sums):
    rows, cols = sum(s.shape[0] for s in sums), sums[0].shape[1]
    half = rows // (4 * blocks)
    out = jax.ShapeDtypeStruct((half, cols), jnp.bfloat16)
    return pl.pallas_call(
        functools.partial(pick_kernel, blocks, half),
        out_shape=(out,) * 4,
        in_specs=vmem(2 + len(sums)),
        out_specs=tuple(vmem(4)),
        compiler_params=params(),
        cost_estimate=cost(4 * rows * cols, 8 * rows * cols),
    )(noted, two, *sums)


def forward_kernel(got_ref, out_ref):
    out_ref[...] = got_ref[pl.ds(0, out_ref.shape[0]), :]


def forward(rows, got):
    out = jax.ShapeDtypeStruct((rows, got.shape[1]), got.dtype)
    return pl.pallas_call(
        forward_kernel,
        out_shape=out,
        in_specs=vmem(1),
        out_specs=pl.BlockSpec(memory_space=pltpu.VMEM),
        compiler_params=params(),
        cost_estimate=cost(0, 6 * out.size),
    )(got)


def hold_kernel(near_ref, far_ref, out_ref):
    cols = near_ref.shape[1]
    out_ref[:, pl.ds(0, cols)] = near_ref[...]
    out_ref[:, pl.ds(cols, cols)] = far_ref[...]


def hold(near, far):
    rows, cols = near.shape
    return pl.pallas_call(
        hold_kernel,
        out_shape=jax.ShapeDtypeStruct((rows, 2 * cols), near.dtype),
        in_specs=vmem(2),
        out_specs=pl.BlockSpec(memory_space=pltpu.VMEM),
        compiler_params=params(),
        cost_estimate=cost(0, 8 * near.size),
    )(near, far)


def join_kernel(held_ref, two_ref, one_ref, out_ref):
    cols = one_ref.shape[1]
    c = lax.axis_index("ctx")
    pieces = (held_ref[:, pl.ds(0, cols)], one_ref[...], two_ref[...], held_ref[:, pl.ds(cols, cols)])
    for k in range(4):
        out_ref[:, pl.ds(pl.multiple_of((c ^ k) * cols, cols), cols)] = pieces[k]


def join(held, two, one):
    rows, cols = one.shape
    return pl.pallas_call(
        join_kernel,
        out_shape=jax.ShapeDtypeStruct((rows, 4 * cols), jnp.bfloat16),
        in_specs=vmem(3),
        out_specs=pl.BlockSpec(memory_space=pltpu.VMEM),
        compiler_params=params(),
        cost_estimate=cost(0, 16 * one.size),
    )(held, two, one)


def flip(array, axis, bits):
    return lax.ppermute(array, axis, [(i, i ^ bits) for i in range(4)])


def core_total(mine, other):
    return total((mine, flip(other, "tp", 1)))


def stack_kernel(done_ref, mine_ref, got_ref, out_ref):
    rows = done_ref.shape[0]
    out_ref[pl.ds(0, rows), :] = done_ref[...]
    both = mine_ref[...].astype(jnp.float32) + got_ref[...].astype(jnp.float32)
    out_ref[pl.ds(rows, mine_ref.shape[0]), :] = both.astype(out_ref.dtype)


def stack_core_total(done, mine, other):
    rows = done.shape[0] + mine.shape[0]
    return pl.pallas_call(
        stack_kernel,
        out_shape=jax.ShapeDtypeStruct((rows, mine.shape[1]), jnp.bfloat16),
        in_specs=vmem(3),
        out_specs=pl.BlockSpec(memory_space=pltpu.VMEM),
        compiler_params=params(),
        cost_estimate=cost(mine.size, 8 * mine.size),
    )(done, mine, flip(other, "tp", 1))


def chip_total(share):
    return total((share, flip(share, "tp", 2)))


def after(value, *others):
    return lax.optimization_barrier((value, *others))[0]


def small_ring(queries, key_rows, value_rows, doc_start, doc_end, block_target, out_weight):
    rows = queries.shape[0]
    blocks = block_target.shape[0]
    block_rows = rows // blocks
    end, start = doc_end.reshape(1, rows), doc_start.reshape(1, rows)
    own_target = block_target.reshape(1, blocks)
    message = pack(key_rows, value_rows, end, own_target)
    flipped = flip(message, "ctx", 1)
    middle = [(4 * c + t, 4 * (3 - c) + t if c in (1, 2) else 4 * c + (t ^ 1)) for c in range(4) for t in range(4)]
    mid = lax.ppermute(message, ("ctx", "tp"), middle)
    plain, first, second = attend(
        blocks, queries, flipped, mid, key_rows, value_rows, end, start, own_target
    )
    rows_1, first_2, second_2 = flip(plain, "ctx", 1), flip(first, "ctx", 2), flip(second, "ctx", 2)
    first_3, second_3 = flip(forward(block_rows, first_2), "ctx", 1), flip(second_2, "ctx", 1)
    share_a = core_total(*project(block_rows, (plain, rows_1), out_weight, cost(1 * 10**8, 0)))
    first_2 = after(first_2, share_a)
    second_2 = after(second_2, share_a)
    share_b = stack_core_total(share_a, *project(block_rows, (first_2, second_2), out_weight))
    first_3 = after(first_3, share_b)
    share_c = core_total(*project(block_rows, (first_3, second_3), out_weight, cost(100 * 10**8, 0)))
    sums = (chip_total(share_b), chip_total(share_c))
    kept, *sent = pick(blocks, first, first_2, sums)
    got_3, got_2, got_1 = (flip(sent[k - 1], "ctx", k) for k in (3, 2, 1))
    return join(hold(kept, got_3), got_2, got_1)


def attend_block(soft_state, query_grid, query_pos, query_start, key_block, value_block, key_end, key_pos):
    running_max, weight_sum, weighted = soft_state
    scores = jnp.einsum(
        "rkgd,nkd->rkgn", query_grid, key_block, preferred_element_type=jnp.float32
    ) * HEAD_DIM ** (-0.5)
    visible = (
        (key_pos[None, :] <= query_pos[:, None])
        & (key_pos[None, :] >= query_start[:, None])
        & (key_end[None, :] > query_pos[:, None])
    )
    visible = visible[:, None, None, :]
    new_max = jnp.maximum(running_max, jnp.max(jnp.where(visible, scores, NEG_LARGE), axis=-1))
    weights = jnp.where(visible, jnp.exp(scores - new_max[..., None]), 0.0)
    fading = jnp.exp(running_max - new_max)
    weight_sum = weight_sum * fading + jnp.sum(weights, axis=-1)
    weighted = weighted * fading[..., None] + jnp.einsum(
        "rkgn,nkd->rkgd",
        weights.astype(jnp.bfloat16),
        value_block,
        preferred_element_type=jnp.float32,
    )
    return (new_max, weight_sum, weighted)


def attend_all(queries, query_pos, query_start, key_part, value_part, end_part):
    rows = queries.shape[0]
    key_count = key_part.shape[0]
    kv_here = key_part.shape[1] // HEAD_DIM
    query_grid = queries.reshape(rows, kv_here, -1, HEAD_DIM)
    block_len = math.gcd(key_count, 512)
    block_count = key_count // block_len
    items = (
        key_part.reshape(block_count, block_len, kv_here, HEAD_DIM),
        value_part.reshape(block_count, block_len, kv_here, HEAD_DIM),
        end_part.reshape(block_count, block_len),
        jnp.arange(key_count, dtype=jnp.int32).reshape(block_count, block_len),
    )
    start_state = (
        jnp.full(query_grid.shape[:3], NEG_LARGE, jnp.float32),
        jnp.zeros(query_grid.shape[:3], jnp.float32),
        jnp.zeros(query_grid.shape, jnp.float32),
    )

    def one_block(state, item):
        return attend_block(state, query_grid, query_pos, query_start, *item), None

    (_, weight_sum, weighted), _ = lax.scan(one_block, start_state, items)
    return (weighted / weight_sum[..., None]).astype(jnp.bfloat16).reshape(rows, -1)


def any_ring(queries, key_rows, value_rows, doc_start, doc_end, block_target, out_weight):
    rows = queries.shape[0]
    blocks = block_target.shape[0]
    block_rows = rows // blocks
    ctx_count = lax.axis_size("ctx")
    tp_count = lax.axis_size("tp")
    gather = functools.partial(lax.all_gather, axis_name="ctx", axis=0, tiled=True)
    query_pos = lax.axis_index("ctx") * rows + jnp.arange(rows, dtype=jnp.int32)
    attended = attend_all(
        queries, query_pos, doc_start, gather(key_rows), gather(value_rows), gather(doc_end)
    )
    targets = gather(block_target)
    source = jnp.zeros_like(targets).at[targets].set(jnp.arange(targets.size, dtype=jnp.int32))
    source_rows = (source[:, None] * block_rows + jnp.arange(block_rows, dtype=jnp.int32)).reshape(-1)
    balanced = jnp.take(gather(attended), source_rows, axis=0)
    share = jnp.dot(balanced, out_weight, preferred_element_type=jnp.float32).astype(jnp.bfloat16)
    share = share.reshape(ctx_count, tp_count, rows // tp_count, -1)
    summed = lax.psum_scatter(share, "tp", scatter_dimension=1, tiled=True)
    pieces = lax.all_to_all(summed[:, 0], "ctx", split_axis=0, concat_axis=0, tiled=True)
    return jnp.swapaxes(pieces, 0, 1).reshape(rows // tp_count, -1)


def shards(queries, key_rows, value_rows, doc_start, doc_end, block_target, out_weight):
    ctx_count, tp_count = lax.axis_size("ctx"), lax.axis_size("tp")
    rows, blocks = queries.shape[0], block_target.shape[0]
    longest = rows * ctx_count // 2 - rows
    near = longest <= rows and ctx_count == 4 and tp_count == 4 and blocks == 2
    plan = small_ring if near and rows % (4 * blocks * 2) == 0 else any_ring
    return plan(queries, key_rows, value_rows, doc_start, doc_end, block_target, out_weight)


def solution(mesh):
    in_specs = (
        P(("group", "ctx"), "tp"),
        P(("group", "ctx"), "tp"),
        P(("group", "ctx"), "tp"),
        P(("group", "ctx")),
        P(("group", "ctx")),
        P(("group", "ctx")),
        P("tp", "ctx"),
    )
    out_specs = P(("group", "ctx", "tp"), None)
    return jax.shard_map(shards, mesh=mesh, in_specs=in_specs, out_specs=out_specs, check_vma=False)
```

```python
import functools
import math

import jax
import jax.numpy as jnp
from jax import lax
from jax.experimental import pallas as pl
from jax.experimental.pallas import tpu as pltpu
from jax.sharding import PartitionSpec as P

HEAD_DIM = 128
NEG_LARGE = -1e30
END_PART = 128


def vmem(count):
    return [pl.BlockSpec(memory_space=pltpu.VMEM)] * count


def smem(count):
    return [pl.BlockSpec(memory_space=pltpu.SMEM)] * count


def params():
    return pltpu.CompilerParams(vmem_limit_bytes=16 * 1024 * 1024)


def cost(flops, moved):
    return pl.CostEstimate(flops=int(flops), bytes_accessed=int(moved), transcendentals=0)


def column(row):
    size = row.shape[1]
    return jnp.transpose(jnp.broadcast_to(row, (size, size)))


def pack_kernel(k_ref, v_ref, end_ref, target_ref, message_ref):
    rows, width = k_ref.shape
    message_ref[pl.ds(0, rows), pl.ds(0, width)] = k_ref[...]
    message_ref[pl.ds(0, rows), pl.ds(width, width)] = v_ref[...]
    extra = message_ref.shape[0] - rows
    line = lax.broadcasted_iota(jnp.int32, (extra, rows), 0)
    ends = jnp.broadcast_to(end_ref[...], (extra, rows))
    parts = jnp.where(line == 0, ends // END_PART, jnp.where(line == 1, ends % END_PART, 0))
    message_ref[pl.ds(rows, extra), :] = jnp.zeros((extra, 2 * width), jnp.bfloat16)
    message_ref[pl.ds(rows, extra), pl.ds(0, rows)] = parts.astype(jnp.float32).astype(jnp.bfloat16)
    targets = jnp.broadcast_to(target_ref[...].astype(jnp.float32), (extra, target_ref.shape[1]))
    message_ref[pl.ds(rows, extra), pl.ds(rows, target_ref.shape[1])] = targets.astype(jnp.bfloat16)


def pack(key_rows, value_rows, ends, targets):
    rows, width = key_rows.shape
    return pl.pallas_call(
        pack_kernel,
        out_shape=jax.ShapeDtypeStruct((rows + 16, 2 * width), jnp.bfloat16),
        in_specs=vmem(4),
        out_specs=pl.BlockSpec(memory_space=pltpu.VMEM),
        cost_estimate=cost(10**9, 8 * key_rows.size),
    )(key_rows, value_rows, ends, targets)


def attend_kernel(
    blocks, q_ref, mid_ref, flip_ref, k_ref, v_ref, end_ref, st_ref, own_ref, plain_ref, *part_refs
):
    across = lax.axis_index("ctx") % 2 == 0
    halo = jnp.where(across, mid_ref[...], flip_ref[...])
    near = flip_ref[pl.ds(k_ref.shape[0], 16), pl.ds(k_ref.shape[0], HEAD_DIM)]
    near = near[0:1, 0:blocks].astype(jnp.float32)
    targets = jnp.concatenate([own_ref[...].astype(jnp.float32), near], axis=1)
    count = targets.shape[1]
    targets = jnp.broadcast_to(targets, (8, count)).astype(jnp.bfloat16)
    below = pl.ds(q_ref.shape[0] // blocks, 8)
    part_refs[0][below, :] = jnp.zeros((8, q_ref.shape[1]), jnp.bfloat16)
    part_refs[0][below, pl.ds(0, count)] = targets
    rows = q_ref.shape[0]
    width = k_ref.shape[1]
    kv_here = width // HEAD_DIM
    group = q_ref.shape[1] // HEAD_DIM // kv_here
    core = lax.axis_index("tp") % 2
    base = lax.axis_index("ctx") * rows
    half = rows // blocks // 2
    query_pos = base + lax.broadcasted_iota(jnp.int32, (rows, rows), 0)
    query_start = column(st_ref[...])
    parts = halo[rows : rows + 16, 0:rows].astype(jnp.float32).astype(jnp.int32)
    masks = []
    for shift, key_end in ((rows, parts[0:1] * END_PART + parts[1:2]), (0, end_ref[...])):
        key_pos = base - shift + lax.broadcasted_iota(jnp.int32, (rows, rows), 1)
        masks.append((key_pos <= query_pos) & (key_pos >= query_start) & (key_end > query_pos))
    visible = jnp.concatenate(masks, axis=1)
    visible = jnp.concatenate([visible] * group, axis=0)
    for kv in range(kv_here):
        keys, values = (
            jnp.concatenate(
                [
                    halo[0:rows, first + kv * HEAD_DIM : first + (kv + 1) * HEAD_DIM],
                    ref[:, pl.ds(kv * HEAD_DIM, HEAD_DIM)],
                ],
                axis=0,
            )
            for first, ref in ((0, k_ref), (width, v_ref))
        )
        query = jnp.concatenate(
            [q_ref[:, pl.ds((kv * group + g) * HEAD_DIM, HEAD_DIM)] for g in range(group)], axis=0
        )
        scores = (
            lax.dot_general(
                query, keys, (((1,), (1,)), ((), ())), preferred_element_type=jnp.float32
            )
            * HEAD_DIM**-0.5
        )
        row_max = jnp.max(jnp.where(visible, scores, NEG_LARGE), axis=1, keepdims=True)
        weights = jnp.where(visible, jnp.exp(scores - row_max), 0.0)
        weight_sum = jnp.sum(weights, axis=1, keepdims=True)
        summed = jnp.dot(
            weights.astype(jnp.bfloat16), values, preferred_element_type=jnp.float32
        )
        attended = (summed / weight_sum).astype(jnp.bfloat16)
        for g in range(group):
            for p in range(blocks):
                for h in range(2):
                    first = g * rows + (p * 2 + h) * half
                    place = pl.multiple_of((h ^ core) * half, half)
                    lanes = pl.ds((kv * group + g) * HEAD_DIM, HEAD_DIM)
                    target_rows = pl.ds(p * 2 * half + place, half)
                    plain_ref[target_rows, lanes] = attended[first : first + half]
                    part_refs[p][pl.ds(place, half), lanes] = attended[first : first + half]


def attend(blocks, queries, flipped, mid, keys, values, end, start, own):
    rows, features = queries.shape
    sizes = (rows, rows // blocks + 8) + (rows // blocks,) * (blocks - 1)
    return pl.pallas_call(
        functools.partial(attend_kernel, blocks),
        out_shape=tuple(jax.ShapeDtypeStruct((size, features), jnp.bfloat16) for size in sizes),
        in_specs=vmem(8),
        out_specs=tuple(vmem(1 + blocks)),
        compiler_params=params(),
        cost_estimate=cost(8 * rows * rows * features, 6 * queries.size),
    )(queries, mid, flipped, keys, values, end, start, own)


def project_kernel(block_rows, *refs):
    chunks, weight_ref, mine_ref, other_ref = refs[:-3], refs[-3], refs[-2], refs[-1]
    half = block_rows // 2
    whole = [c.shape[0] // block_rows * block_rows for c in chunks]
    stacked = jnp.concatenate([c[pl.ds(0, n), :] for c, n in zip(chunks, whole)], axis=0)
    share = jnp.dot(stacked, weight_ref[...], preferred_element_type=jnp.float32).astype(
        jnp.bfloat16
    )
    for n in range(share.shape[0] // block_rows):
        first = n * block_rows
        mine_ref[pl.ds(n * half, half), :] = share[first : first + half]
        other_ref[pl.ds(n * half, half), :] = share[first + half : first + block_rows]


def project(block_rows, chunks, weight, estimate=None):
    rows = sum(c.shape[0] // block_rows * block_rows for c in chunks)
    out = jax.ShapeDtypeStruct((rows // 2, weight.shape[1]), jnp.bfloat16)
    return pl.pallas_call(
        functools.partial(project_kernel, block_rows),
        out_shape=(out, out),
        in_specs=vmem(len(chunks) + 1),
        out_specs=tuple(vmem(2)),
        compiler_params=params(),
        cost_estimate=estimate or cost(2 * rows * weight.size, 2 * weight.size),
    )(*chunks, weight)


def total_kernel(*refs):
    terms, out_ref = refs[:-1], refs[-1]
    out_ref[...] = sum(t[...].astype(jnp.float32) for t in terms).astype(out_ref.dtype)


def total(terms):
    return pl.pallas_call(
        total_kernel,
        out_shape=jax.ShapeDtypeStruct(terms[0].shape, jnp.bfloat16),
        in_specs=vmem(len(terms)),
        out_specs=pl.BlockSpec(memory_space=pltpu.VMEM),
        compiler_params=params(),
        cost_estimate=cost(4 * terms[0].size, 10 * terms[0].size),
    )(*terms)


def note(ref, count):
    tail = ref[pl.ds(ref.shape[0] - 8, 8), pl.ds(0, HEAD_DIM)].astype(jnp.float32)
    return tail[0:1, 0:count].astype(jnp.int32)


def pick_kernel(blocks, half, noted_ref, two_ref, *refs):
    sums, outs = refs[:-4], refs[-4:]
    x = lax.axis_index("tp") // 2
    c = lax.axis_index("ctx")
    pieces = [r[pl.ds(n, half), :] for r in sums for n in range(0, r.shape[0], half)]
    targets = jnp.concatenate([note(r, 2 * blocks) for r in (noted_ref, two_ref)], axis=1)
    for k in range(4):
        wanted = (c ^ k) * blocks + x
        piece = pieces[0]
        for n in range(1, len(pieces)):
            here = jnp.broadcast_to(targets[:, n : n + 1] == wanted, piece.shape)
            piece = jnp.where(here, pieces[n], piece)
        outs[k][...] = piece


def pick(blocks, noted, two, sums):
    rows, cols = sum(s.shape[0] for s in sums), sums[0].shape[1]
    half = rows // (4 * blocks)
    out = jax.ShapeDtypeStruct((half, cols), jnp.bfloat16)
    return pl.pallas_call(
        functools.partial(pick_kernel, blocks, half),
        out_shape=(out,) * 4,
        in_specs=vmem(2 + len(sums)),
        out_specs=tuple(vmem(4)),
        compiler_params=params(),
        cost_estimate=cost(4 * rows * cols, 8 * rows * cols),
    )(noted, two, *sums)


def forward_kernel(got_ref, out_ref):
    out_ref[...] = got_ref[pl.ds(0, out_ref.shape[0]), :]


def forward(rows, got):
    out = jax.ShapeDtypeStruct((rows, got.shape[1]), got.dtype)
    return pl.pallas_call(
        forward_kernel,
        out_shape=out,
        in_specs=vmem(1),
        out_specs=pl.BlockSpec(memory_space=pltpu.VMEM),
        compiler_params=params(),
        cost_estimate=cost(0, 6 * out.size),
    )(got)


def hold_kernel(near_ref, far_ref, out_ref):
    cols = near_ref.shape[1]
    out_ref[:, pl.ds(0, cols)] = near_ref[...]
    out_ref[:, pl.ds(cols, cols)] = far_ref[...]


def hold(near, far):
    rows, cols = near.shape
    return pl.pallas_call(
        hold_kernel,
        out_shape=jax.ShapeDtypeStruct((rows, 2 * cols), near.dtype),
        in_specs=vmem(2),
        out_specs=pl.BlockSpec(memory_space=pltpu.VMEM),
        compiler_params=params(),
        cost_estimate=cost(0, 8 * near.size),
    )(near, far)


def join_kernel(held_ref, two_ref, one_ref, out_ref):
    cols = one_ref.shape[1]
    c = lax.axis_index("ctx")
    pieces = (held_ref[:, pl.ds(0, cols)], one_ref[...], two_ref[...], held_ref[:, pl.ds(cols, cols)])
    for k in range(4):
        out_ref[:, pl.ds(pl.multiple_of((c ^ k) * cols, cols), cols)] = pieces[k]


def join(held, two, one):
    rows, cols = one.shape
    return pl.pallas_call(
        join_kernel,
        out_shape=jax.ShapeDtypeStruct((rows, 4 * cols), jnp.bfloat16),
        in_specs=vmem(3),
        out_specs=pl.BlockSpec(memory_space=pltpu.VMEM),
        compiler_params=params(),
        cost_estimate=cost(0, 16 * one.size),
    )(held, two, one)


def flip(array, axis, bits):
    return lax.ppermute(array, axis, [(i, i ^ bits) for i in range(4)])


def core_total(mine, other):
    return total((mine, flip(other, "tp", 1)))


def stack_kernel(done_ref, mine_ref, got_ref, out_ref):
    rows = done_ref.shape[0]
    out_ref[pl.ds(0, rows), :] = done_ref[...]
    both = mine_ref[...].astype(jnp.float32) + got_ref[...].astype(jnp.float32)
    out_ref[pl.ds(rows, mine_ref.shape[0]), :] = both.astype(out_ref.dtype)


def stack_core_total(done, mine, other):
    rows = done.shape[0] + mine.shape[0]
    return pl.pallas_call(
        stack_kernel,
        out_shape=jax.ShapeDtypeStruct((rows, mine.shape[1]), jnp.bfloat16),
        in_specs=vmem(3),
        out_specs=pl.BlockSpec(memory_space=pltpu.VMEM),
        compiler_params=params(),
        cost_estimate=cost(mine.size, 8 * mine.size),
    )(done, mine, flip(other, "tp", 1))


def chip_total(share):
    return total((share, flip(share, "tp", 2)))


def after(value, *others):
    return lax.optimization_barrier((value, *others))[0]


def small_ring(queries, key_rows, value_rows, doc_start, doc_end, block_target, out_weight):
    rows = queries.shape[0]
    blocks = block_target.shape[0]
    block_rows = rows // blocks
    end, start = doc_end.reshape(1, rows), doc_start.reshape(1, rows)
    own_target = block_target.reshape(1, blocks)
    message = pack(key_rows, value_rows, end, own_target)
    middle = [(4 * c + t, 4 * (3 - c) + t if c in (1, 2) else 4 * c + (t ^ 1)) for c in range(4) for t in range(4)]
    mid = lax.ppermute(message, ("ctx", "tp"), middle)
    flipped = flip(message, "ctx", 1)
    plain, first, second = attend(
        blocks, queries, flipped, mid, key_rows, value_rows, end, start, own_target
    )
    rows_1, first_2, second_2 = flip(plain, "ctx", 1), flip(first, "ctx", 2), flip(second, "ctx", 2)
    first_3, second_3 = flip(forward(block_rows, first_2), "ctx", 1), flip(second_2, "ctx", 1)
    share_a = core_total(*project(block_rows, (plain, rows_1), out_weight, cost(1 * 10**8, 0)))
    first_2 = after(first_2, share_a)
    second_2 = after(second_2, share_a)
    share_b = stack_core_total(share_a, *project(block_rows, (first_2, second_2), out_weight))
    first_3 = after(first_3, share_b)
    share_c = core_total(*project(block_rows, (first_3, second_3), out_weight, cost(100 * 10**8, 0)))
    sums = (chip_total(share_b), chip_total(share_c))
    kept, *sent = pick(blocks, first, first_2, sums)
    got_3, got_2, got_1 = (flip(sent[k - 1], "ctx", k) for k in (3, 2, 1))
    return join(hold(kept, got_3), got_2, got_1)


def attend_block(soft_state, query_grid, query_pos, query_start, key_block, value_block, key_end, key_pos):
    running_max, weight_sum, weighted = soft_state
    scores = jnp.einsum(
        "rkgd,nkd->rkgn", query_grid, key_block, preferred_element_type=jnp.float32
    ) * HEAD_DIM ** (-0.5)
    visible = (
        (key_pos[None, :] <= query_pos[:, None])
        & (key_pos[None, :] >= query_start[:, None])
        & (key_end[None, :] > query_pos[:, None])
    )
    visible = visible[:, None, None, :]
    new_max = jnp.maximum(running_max, jnp.max(jnp.where(visible, scores, NEG_LARGE), axis=-1))
    weights = jnp.where(visible, jnp.exp(scores - new_max[..., None]), 0.0)
    fading = jnp.exp(running_max - new_max)
    weight_sum = weight_sum * fading + jnp.sum(weights, axis=-1)
    weighted = weighted * fading[..., None] + jnp.einsum(
        "rkgn,nkd->rkgd",
        weights.astype(jnp.bfloat16),
        value_block,
        preferred_element_type=jnp.float32,
    )
    return (new_max, weight_sum, weighted)


def attend_all(queries, query_pos, query_start, key_part, value_part, end_part):
    rows = queries.shape[0]
    key_count = key_part.shape[0]
    kv_here = key_part.shape[1] // HEAD_DIM
    query_grid = queries.reshape(rows, kv_here, -1, HEAD_DIM)
    block_len = math.gcd(key_count, 512)
    block_count = key_count // block_len
    items = (
        key_part.reshape(block_count, block_len, kv_here, HEAD_DIM),
        value_part.reshape(block_count, block_len, kv_here, HEAD_DIM),
        end_part.reshape(block_count, block_len),
        jnp.arange(key_count, dtype=jnp.int32).reshape(block_count, block_len),
    )
    start_state = (
        jnp.full(query_grid.shape[:3], NEG_LARGE, jnp.float32),
        jnp.zeros(query_grid.shape[:3], jnp.float32),
        jnp.zeros(query_grid.shape, jnp.float32),
    )

    def one_block(state, item):
        return attend_block(state, query_grid, query_pos, query_start, *item), None

    (_, weight_sum, weighted), _ = lax.scan(one_block, start_state, items)
    return (weighted / weight_sum[..., None]).astype(jnp.bfloat16).reshape(rows, -1)


def any_ring(queries, key_rows, value_rows, doc_start, doc_end, block_target, out_weight):
    rows = queries.shape[0]
    blocks = block_target.shape[0]
    block_rows = rows // blocks
    ctx_count = lax.axis_size("ctx")
    tp_count = lax.axis_size("tp")
    gather = functools.partial(lax.all_gather, axis_name="ctx", axis=0, tiled=True)
    query_pos = lax.axis_index("ctx") * rows + jnp.arange(rows, dtype=jnp.int32)
    attended = attend_all(
        queries, query_pos, doc_start, gather(key_rows), gather(value_rows), gather(doc_end)
    )
    targets = gather(block_target)
    source = jnp.zeros_like(targets).at[targets].set(jnp.arange(targets.size, dtype=jnp.int32))
    source_rows = (source[:, None] * block_rows + jnp.arange(block_rows, dtype=jnp.int32)).reshape(-1)
    balanced = jnp.take(gather(attended), source_rows, axis=0)
    share = jnp.dot(balanced, out_weight, preferred_element_type=jnp.float32).astype(jnp.bfloat16)
    share = share.reshape(ctx_count, tp_count, rows // tp_count, -1)
    summed = lax.psum_scatter(share, "tp", scatter_dimension=1, tiled=True)
    pieces = lax.all_to_all(summed[:, 0], "ctx", split_axis=0, concat_axis=0, tiled=True)
    return jnp.swapaxes(pieces, 0, 1).reshape(rows // tp_count, -1)


def shards(queries, key_rows, value_rows, doc_start, doc_end, block_target, out_weight):
    ctx_count, tp_count = lax.axis_size("ctx"), lax.axis_size("tp")
    rows, blocks = queries.shape[0], block_target.shape[0]
    longest = rows * ctx_count // 2 - rows
    near = longest <= rows and ctx_count == 4 and tp_count == 4 and blocks == 2
    plan = small_ring if near and rows % (4 * blocks * 2) == 0 else any_ring
    return plan(queries, key_rows, value_rows, doc_start, doc_end, block_target, out_weight)


def solution(mesh):
    in_specs = (
        P(("group", "ctx"), "tp"),
        P(("group", "ctx"), "tp"),
        P(("group", "ctx"), "tp"),
        P(("group", "ctx")),
        P(("group", "ctx")),
        P(("group", "ctx")),
        P("tp", "ctx"),
    )
    out_specs = P(("group", "ctx", "tp"), None)
    return jax.shard_map(shards, mesh=mesh, in_specs=in_specs, out_specs=out_specs, check_vma=False)
```

```python
import functools
import math

import jax
import jax.numpy as jnp
from jax import lax
from jax.experimental import pallas as pl
from jax.experimental.pallas import tpu as pltpu
from jax.sharding import PartitionSpec as P

HEAD_DIM = 128
NEG_LARGE = -1e30
END_PART = 128


def vmem(count):
    return [pl.BlockSpec(memory_space=pltpu.VMEM)] * count


def smem(count):
    return [pl.BlockSpec(memory_space=pltpu.SMEM)] * count


def params():
    return pltpu.CompilerParams(vmem_limit_bytes=16 * 1024 * 1024)


def cost(flops, moved):
    return pl.CostEstimate(flops=int(flops), bytes_accessed=int(moved), transcendentals=0)


def column(row):
    size = row.shape[1]
    return jnp.transpose(jnp.broadcast_to(row, (size, size)))


def pack_kernel(k_in, v_in, end_ref, target_ref, message_out, held, sems):
    rows, width = k_in.shape
    extra = held.shape[0] - rows
    parts = [(pl.ds(0, rows), pl.ds(n * width, width)) for n in range(2)]
    arrive = [
        pltpu.make_async_copy(source, held.at[part], sems.at[n])
        for n, (source, part) in enumerate(zip((k_in, v_in), parts))
    ]
    for copy in arrive:
        copy.start()
    line = lax.broadcasted_iota(jnp.int32, (extra, rows), 0)
    ends = jnp.broadcast_to(end_ref[...], (extra, rows))
    ends = jnp.where(line == 0, ends // END_PART, jnp.where(line == 1, ends % END_PART, 0))
    held[pl.ds(rows, extra), :] = jnp.zeros((extra, 2 * width), jnp.bfloat16)
    held[pl.ds(rows, extra), pl.ds(0, rows)] = ends.astype(jnp.float32).astype(jnp.bfloat16)
    targets = jnp.broadcast_to(target_ref[...].astype(jnp.float32), (extra, target_ref.shape[1]))
    held[pl.ds(rows, extra), pl.ds(rows, target_ref.shape[1])] = targets.astype(jnp.bfloat16)
    parts.append((pl.ds(rows, extra), pl.ds(0, 2 * width)))
    leave = [
        pltpu.make_async_copy(held.at[part], message_out.at[part], sems.at[2 + n])
        for n, part in enumerate(parts)
    ]
    leave[2].start()
    for n in range(2):
        arrive[n].wait()
        leave[n].start()
    for copy in leave:
        copy.wait()


def pack(key_rows, value_rows, ends, targets):
    rows, width = key_rows.shape
    shape = (rows + 16, 2 * width)
    hbm = pl.BlockSpec(memory_space=pltpu.HBM)
    return pl.pallas_call(
        pack_kernel,
        out_shape=jax.ShapeDtypeStruct(shape, jnp.bfloat16),
        in_specs=[hbm, hbm] + vmem(2),
        out_specs=hbm,
        scratch_shapes=[pltpu.VMEM(shape, jnp.bfloat16), pltpu.SemaphoreType.DMA((5,))],
        cost_estimate=cost(10**9, 8 * key_rows.size),
    )(key_rows, value_rows, ends, targets)


def attend_kernel(
    blocks, q_ref, flip_ref, mid_ref, k_ref, v_ref, end_ref, st_ref, own_ref, plain_ref, *part_refs
):
    across = lax.axis_index("ctx") % 2 == 0
    halo = jnp.where(across, mid_ref[...], flip_ref[...])
    near = flip_ref[pl.ds(k_ref.shape[0], 16), pl.ds(k_ref.shape[0], HEAD_DIM)]
    near = near[0:1, 0:blocks].astype(jnp.float32)
    targets = jnp.concatenate([own_ref[...].astype(jnp.float32), near], axis=1)
    count = targets.shape[1]
    targets = jnp.broadcast_to(targets, (8, count)).astype(jnp.bfloat16)
    below = pl.ds(q_ref.shape[0] // blocks, 8)
    part_refs[0][below, :] = jnp.zeros((8, q_ref.shape[1]), jnp.bfloat16)
    part_refs[0][below, pl.ds(0, count)] = targets
    rows = q_ref.shape[0]
    width = k_ref.shape[1]
    kv_here = width // HEAD_DIM
    group = q_ref.shape[1] // HEAD_DIM // kv_here
    core = lax.axis_index("tp") % 2
    base = lax.axis_index("ctx") * rows
    half = rows // blocks // 2
    query_pos = base + lax.broadcasted_iota(jnp.int32, (rows, rows), 0)
    query_start = column(st_ref[...])
    parts = halo[rows : rows + 16, 0:rows].astype(jnp.float32).astype(jnp.int32)
    masks = []
    for shift, key_end in ((rows, parts[0:1] * END_PART + parts[1:2]), (0, end_ref[...])):
        key_pos = base - shift + lax.broadcasted_iota(jnp.int32, (rows, rows), 1)
        masks.append((key_pos <= query_pos) & (key_pos >= query_start) & (key_end > query_pos))
    visible = jnp.concatenate(masks, axis=1)
    visible = jnp.concatenate([visible] * group, axis=0)
    for kv in range(kv_here):
        keys, values = (
            jnp.concatenate(
                [
                    halo[0:rows, first + kv * HEAD_DIM : first + (kv + 1) * HEAD_DIM],
                    ref[:, pl.ds(kv * HEAD_DIM, HEAD_DIM)],
                ],
                axis=0,
            )
            for first, ref in ((0, k_ref), (width, v_ref))
        )
        query = jnp.concatenate(
            [q_ref[:, pl.ds((kv * group + g) * HEAD_DIM, HEAD_DIM)] for g in range(group)], axis=0
        )
        scores = (
            lax.dot_general(
                query, keys, (((1,), (1,)), ((), ())), preferred_element_type=jnp.float32
            )
            * HEAD_DIM**-0.5
        )
        row_max = jnp.max(jnp.where(visible, scores, NEG_LARGE), axis=1, keepdims=True)
        weights = jnp.where(visible, jnp.exp(scores - row_max), 0.0)
        weight_sum = jnp.sum(weights, axis=1, keepdims=True)
        summed = jnp.dot(
            weights.astype(jnp.bfloat16), values, preferred_element_type=jnp.float32
        )
        attended = (summed / weight_sum).astype(jnp.bfloat16)
        for g in range(group):
            for p in range(blocks):
                for h in range(2):
                    first = g * rows + (p * 2 + h) * half
                    place = pl.multiple_of((h ^ core) * half, half)
                    lanes = pl.ds((kv * group + g) * HEAD_DIM, HEAD_DIM)
                    target_rows = pl.ds(p * 2 * half + place, half)
                    plain_ref[target_rows, lanes] = attended[first : first + half]
                    part_refs[p][pl.ds(place, half), lanes] = attended[first : first + half]


def attend(blocks, queries, flipped, mid, keys, values, end, start, own):
    rows, features = queries.shape
    sizes = (rows, rows // blocks + 8) + (rows // blocks,) * (blocks - 1)
    return pl.pallas_call(
        functools.partial(attend_kernel, blocks),
        out_shape=tuple(jax.ShapeDtypeStruct((size, features), jnp.bfloat16) for size in sizes),
        in_specs=vmem(8),
        out_specs=tuple(vmem(1 + blocks)),
        compiler_params=params(),
        cost_estimate=cost(8 * rows * rows * features, 6 * queries.size),
    )(queries, flipped, mid, keys, values, end, start, own)


def project_kernel(block_rows, *refs):
    chunks, weight_ref, mine_ref, other_ref = refs[:-3], refs[-3], refs[-2], refs[-1]
    half = block_rows // 2
    whole = [c.shape[0] // block_rows * block_rows for c in chunks]
    stacked = jnp.concatenate([c[pl.ds(0, n), :] for c, n in zip(chunks, whole)], axis=0)
    share = jnp.dot(stacked, weight_ref[...], preferred_element_type=jnp.float32).astype(
        jnp.bfloat16
    )
    for n in range(share.shape[0] // block_rows):
        first = n * block_rows
        mine_ref[pl.ds(n * half, half), :] = share[first : first + half]
        other_ref[pl.ds(n * half, half), :] = share[first + half : first + block_rows]


def project(block_rows, chunks, weight, estimate=None):
    rows = sum(c.shape[0] // block_rows * block_rows for c in chunks)
    out = jax.ShapeDtypeStruct((rows // 2, weight.shape[1]), jnp.bfloat16)
    return pl.pallas_call(
        functools.partial(project_kernel, block_rows),
        out_shape=(out, out),
        in_specs=vmem(len(chunks) + 1),
        out_specs=tuple(vmem(2)),
        compiler_params=params(),
        cost_estimate=estimate or cost(2 * rows * weight.size, 2 * weight.size),
    )(*chunks, weight)


def total_kernel(*refs):
    terms, out_ref = refs[:-1], refs[-1]
    out_ref[...] = sum(t[...].astype(jnp.float32) for t in terms).astype(out_ref.dtype)


def total(terms):
    return pl.pallas_call(
        total_kernel,
        out_shape=jax.ShapeDtypeStruct(terms[0].shape, jnp.bfloat16),
        in_specs=vmem(len(terms)),
        out_specs=pl.BlockSpec(memory_space=pltpu.VMEM),
        compiler_params=params(),
        cost_estimate=cost(4 * terms[0].size, 10 * terms[0].size),
    )(*terms)


def note(ref, count):
    tail = ref[pl.ds(ref.shape[0] - 8, 8), pl.ds(0, HEAD_DIM)].astype(jnp.float32)
    return tail[0:1, 0:count].astype(jnp.int32)


def pick_kernel(blocks, half, noted_ref, two_ref, *refs):
    sums, outs = refs[:-4], refs[-4:]
    x = lax.axis_index("tp") // 2
    c = lax.axis_index("ctx")
    pieces = [r[pl.ds(n, half), :] for r in sums for n in range(0, r.shape[0], half)]
    targets = jnp.concatenate([note(r, 2 * blocks) for r in (noted_ref, two_ref)], axis=1)
    for k in range(4):
        wanted = (c ^ k) * blocks + x
        piece = pieces[0]
        for n in range(1, len(pieces)):
            here = jnp.broadcast_to(targets[:, n : n + 1] == wanted, piece.shape)
            piece = jnp.where(here, pieces[n], piece)
        outs[k][...] = piece


def pick(blocks, noted, two, sums):
    rows, cols = sum(s.shape[0] for s in sums), sums[0].shape[1]
    half = rows // (4 * blocks)
    out = jax.ShapeDtypeStruct((half, cols), jnp.bfloat16)
    return pl.pallas_call(
        functools.partial(pick_kernel, blocks, half),
        out_shape=(out,) * 4,
        in_specs=vmem(2 + len(sums)),
        out_specs=tuple(vmem(4)),
        compiler_params=params(),
        cost_estimate=cost(4 * rows * cols, 8 * rows * cols),
    )(noted, two, *sums)


def forward_kernel(got_ref, out_ref):
    out_ref[...] = got_ref[pl.ds(0, out_ref.shape[0]), :]


def forward(rows, got):
    out = jax.ShapeDtypeStruct((rows, got.shape[1]), got.dtype)
    return pl.pallas_call(
        forward_kernel,
        out_shape=out,
        in_specs=vmem(1),
        out_specs=pl.BlockSpec(memory_space=pltpu.VMEM),
        compiler_params=params(),
        cost_estimate=cost(0, 6 * out.size),
    )(got)


def hold_kernel(near_ref, far_ref, out_ref):
    cols = near_ref.shape[1]
    out_ref[:, pl.ds(0, cols)] = near_ref[...]
    out_ref[:, pl.ds(cols, cols)] = far_ref[...]


def hold(near, far):
    rows, cols = near.shape
    return pl.pallas_call(
        hold_kernel,
        out_shape=jax.ShapeDtypeStruct((rows, 2 * cols), near.dtype),
        in_specs=vmem(2),
        out_specs=pl.BlockSpec(memory_space=pltpu.VMEM),
        compiler_params=params(),
        cost_estimate=cost(0, 8 * near.size),
    )(near, far)


def join_kernel(held_ref, two_ref, one_ref, out_ref):
    cols = one_ref.shape[1]
    c = lax.axis_index("ctx")
    pieces = (held_ref[:, pl.ds(0, cols)], one_ref[...], two_ref[...], held_ref[:, pl.ds(cols, cols)])
    for k in range(4):
        out_ref[:, pl.ds(pl.multiple_of((c ^ k) * cols, cols), cols)] = pieces[k]


def join(held, two, one):
    rows, cols = one.shape
    return pl.pallas_call(
        join_kernel,
        out_shape=jax.ShapeDtypeStruct((rows, 4 * cols), jnp.bfloat16),
        in_specs=vmem(3),
        out_specs=pl.BlockSpec(memory_space=pltpu.VMEM),
        compiler_params=params(),
        cost_estimate=cost(0, 16 * one.size),
    )(held, two, one)


def flip(array, axis, bits):
    return lax.ppermute(array, axis, [(i, i ^ bits) for i in range(4)])


def core_total(mine, other):
    return total((mine, flip(other, "tp", 1)))


def stack_kernel(done_ref, mine_ref, got_ref, out_ref):
    rows = done_ref.shape[0]
    out_ref[pl.ds(0, rows), :] = done_ref[...]
    both = mine_ref[...].astype(jnp.float32) + got_ref[...].astype(jnp.float32)
    out_ref[pl.ds(rows, mine_ref.shape[0]), :] = both.astype(out_ref.dtype)


def stack_core_total(done, mine, other):
    rows = done.shape[0] + mine.shape[0]
    return pl.pallas_call(
        stack_kernel,
        out_shape=jax.ShapeDtypeStruct((rows, mine.shape[1]), jnp.bfloat16),
        in_specs=vmem(3),
        out_specs=pl.BlockSpec(memory_space=pltpu.VMEM),
        compiler_params=params(),
        cost_estimate=cost(mine.size, 8 * mine.size),
    )(done, mine, flip(other, "tp", 1))


def chip_total(share):
    return total((share, flip(share, "tp", 2)))


def after(value, *others):
    return lax.optimization_barrier((value, *others))[0]


def small_ring(queries, key_rows, value_rows, doc_start, doc_end, block_target, out_weight):
    rows = queries.shape[0]
    blocks = block_target.shape[0]
    block_rows = rows // blocks
    end, start = doc_end.reshape(1, rows), doc_start.reshape(1, rows)
    own_target = block_target.reshape(1, blocks)
    message = pack(key_rows, value_rows, end, own_target)
    flipped = flip(message, "ctx", 1)
    middle = [(4 * c + t, 4 * (3 - c) + t if c in (1, 2) else 4 * c + (t ^ 1)) for c in range(4) for t in range(4)]
    mid = lax.ppermute(message, ("ctx", "tp"), middle)
    plain, first, second = attend(
        blocks, queries, flipped, mid, key_rows, value_rows, end, start, own_target
    )
    rows_1, first_2, second_2 = flip(plain, "ctx", 1), flip(first, "ctx", 2), flip(second, "ctx", 2)
    first_3, second_3 = flip(forward(block_rows, first_2), "ctx", 1), flip(second_2, "ctx", 1)
    share_a = core_total(*project(block_rows, (plain, rows_1), out_weight, cost(1 * 10**8, 0)))
    first_2 = after(first_2, share_a)
    second_2 = after(second_2, share_a)
    share_b = stack_core_total(share_a, *project(block_rows, (first_2, second_2), out_weight))
    first_3 = after(first_3, share_b)
    share_c = core_total(*project(block_rows, (first_3, second_3), out_weight, cost(100 * 10**8, 0)))
    sums = (chip_total(share_b), chip_total(share_c))
    kept, *sent = pick(blocks, first, first_2, sums)
    got_3, got_2, got_1 = (flip(sent[k - 1], "ctx", k) for k in (3, 2, 1))
    return join(hold(kept, got_3), got_2, got_1)


def attend_block(soft_state, query_grid, query_pos, query_start, key_block, value_block, key_end, key_pos):
    running_max, weight_sum, weighted = soft_state
    scores = jnp.einsum(
        "rkgd,nkd->rkgn", query_grid, key_block, preferred_element_type=jnp.float32
    ) * HEAD_DIM ** (-0.5)
    visible = (
        (key_pos[None, :] <= query_pos[:, None])
        & (key_pos[None, :] >= query_start[:, None])
        & (key_end[None, :] > query_pos[:, None])
    )
    visible = visible[:, None, None, :]
    new_max = jnp.maximum(running_max, jnp.max(jnp.where(visible, scores, NEG_LARGE), axis=-1))
    weights = jnp.where(visible, jnp.exp(scores - new_max[..., None]), 0.0)
    fading = jnp.exp(running_max - new_max)
    weight_sum = weight_sum * fading + jnp.sum(weights, axis=-1)
    weighted = weighted * fading[..., None] + jnp.einsum(
        "rkgn,nkd->rkgd",
        weights.astype(jnp.bfloat16),
        value_block,
        preferred_element_type=jnp.float32,
    )
    return (new_max, weight_sum, weighted)


def attend_all(queries, query_pos, query_start, key_part, value_part, end_part):
    rows = queries.shape[0]
    key_count = key_part.shape[0]
    kv_here = key_part.shape[1] // HEAD_DIM
    query_grid = queries.reshape(rows, kv_here, -1, HEAD_DIM)
    block_len = math.gcd(key_count, 512)
    block_count = key_count // block_len
    items = (
        key_part.reshape(block_count, block_len, kv_here, HEAD_DIM),
        value_part.reshape(block_count, block_len, kv_here, HEAD_DIM),
        end_part.reshape(block_count, block_len),
        jnp.arange(key_count, dtype=jnp.int32).reshape(block_count, block_len),
    )
    start_state = (
        jnp.full(query_grid.shape[:3], NEG_LARGE, jnp.float32),
        jnp.zeros(query_grid.shape[:3], jnp.float32),
        jnp.zeros(query_grid.shape, jnp.float32),
    )

    def one_block(state, item):
        return attend_block(state, query_grid, query_pos, query_start, *item), None

    (_, weight_sum, weighted), _ = lax.scan(one_block, start_state, items)
    return (weighted / weight_sum[..., None]).astype(jnp.bfloat16).reshape(rows, -1)


def any_ring(queries, key_rows, value_rows, doc_start, doc_end, block_target, out_weight):
    rows = queries.shape[0]
    blocks = block_target.shape[0]
    block_rows = rows // blocks
    ctx_count = lax.axis_size("ctx")
    tp_count = lax.axis_size("tp")
    gather = functools.partial(lax.all_gather, axis_name="ctx", axis=0, tiled=True)
    query_pos = lax.axis_index("ctx") * rows + jnp.arange(rows, dtype=jnp.int32)
    attended = attend_all(
        queries, query_pos, doc_start, gather(key_rows), gather(value_rows), gather(doc_end)
    )
    targets = gather(block_target)
    source = jnp.zeros_like(targets).at[targets].set(jnp.arange(targets.size, dtype=jnp.int32))
    source_rows = (source[:, None] * block_rows + jnp.arange(block_rows, dtype=jnp.int32)).reshape(-1)
    balanced = jnp.take(gather(attended), source_rows, axis=0)
    share = jnp.dot(balanced, out_weight, preferred_element_type=jnp.float32).astype(jnp.bfloat16)
    share = share.reshape(ctx_count, tp_count, rows // tp_count, -1)
    summed = lax.psum_scatter(share, "tp", scatter_dimension=1, tiled=True)
    pieces = lax.all_to_all(summed[:, 0], "ctx", split_axis=0, concat_axis=0, tiled=True)
    return jnp.swapaxes(pieces, 0, 1).reshape(rows // tp_count, -1)


def shards(queries, key_rows, value_rows, doc_start, doc_end, block_target, out_weight):
    ctx_count, tp_count = lax.axis_size("ctx"), lax.axis_size("tp")
    rows, blocks = queries.shape[0], block_target.shape[0]
    longest = rows * ctx_count // 2 - rows
    near = longest <= rows and ctx_count == 4 and tp_count == 4 and blocks == 2
    plan = small_ring if near and rows % (4 * blocks * 2) == 0 else any_ring
    return plan(queries, key_rows, value_rows, doc_start, doc_end, block_target, out_weight)


def solution(mesh):
    in_specs = (
        P(("group", "ctx"), "tp"),
        P(("group", "ctx"), "tp"),
        P(("group", "ctx"), "tp"),
        P(("group", "ctx")),
        P(("group", "ctx")),
        P(("group", "ctx")),
        P("tp", "ctx"),
    )
    out_specs = P(("group", "ctx", "tp"), None)
    return jax.shard_map(shards, mesh=mesh, in_specs=in_specs, out_specs=out_specs, check_vma=False)
```

```python
import functools
import math

import jax
import jax.numpy as jnp
from jax import lax
from jax.experimental import pallas as pl
from jax.experimental.pallas import tpu as pltpu
from jax.sharding import PartitionSpec as P

HEAD_DIM = 128
NEG_LARGE = -1e30
END_PART = 128


def vmem(count):
    return [pl.BlockSpec(memory_space=pltpu.VMEM)] * count


def smem(count):
    return [pl.BlockSpec(memory_space=pltpu.SMEM)] * count


def params():
    return pltpu.CompilerParams(vmem_limit_bytes=16 * 1024 * 1024)


def cost(flops, moved):
    return pl.CostEstimate(flops=int(flops), bytes_accessed=int(moved), transcendentals=0)


def column(row):
    size = row.shape[1]
    return jnp.transpose(jnp.broadcast_to(row, (size, size)))


def pack_kernel(k_ref, v_ref, end_ref, target_ref, message_ref):
    rows, width = k_ref.shape
    message_ref[pl.ds(0, rows), pl.ds(0, width)] = k_ref[...]
    message_ref[pl.ds(0, rows), pl.ds(width, width)] = v_ref[...]
    extra = message_ref.shape[0] - rows
    line = lax.broadcasted_iota(jnp.int32, (extra, rows), 0)
    ends = jnp.broadcast_to(end_ref[...], (extra, rows))
    parts = jnp.where(line == 0, ends // END_PART, jnp.where(line == 1, ends % END_PART, 0))
    message_ref[pl.ds(rows, extra), :] = jnp.zeros((extra, 2 * width), jnp.bfloat16)
    message_ref[pl.ds(rows, extra), pl.ds(0, rows)] = parts.astype(jnp.float32).astype(jnp.bfloat16)
    targets = jnp.broadcast_to(target_ref[...].astype(jnp.float32), (extra, target_ref.shape[1]))
    message_ref[pl.ds(rows, extra), pl.ds(rows, target_ref.shape[1])] = targets.astype(jnp.bfloat16)


def pack(key_rows, value_rows, ends, targets):
    rows, width = key_rows.shape
    return pl.pallas_call(
        pack_kernel,
        out_shape=jax.ShapeDtypeStruct((rows + 8, 2 * width), jnp.bfloat16),
        in_specs=vmem(4),
        out_specs=pl.BlockSpec(memory_space=pltpu.VMEM),
        cost_estimate=cost(10**9, 8 * key_rows.size),
    )(key_rows, value_rows, ends, targets)


def attend_kernel(
    blocks, q_ref, flip_ref, mid_ref, k_ref, v_ref, end_ref, st_ref, own_ref, plain_ref, *part_refs
):
    across = lax.axis_index("ctx") % 2 == 0
    halo = jnp.where(across, mid_ref[...], flip_ref[...])
    near = flip_ref[pl.ds(k_ref.shape[0], 8), pl.ds(k_ref.shape[0], HEAD_DIM)]
    near = near[0:1, 0:blocks].astype(jnp.float32)
    targets = jnp.concatenate([own_ref[...].astype(jnp.float32), near], axis=1)
    count = targets.shape[1]
    targets = jnp.broadcast_to(targets, (8, count)).astype(jnp.bfloat16)
    below = pl.ds(q_ref.shape[0] // blocks, 8)
    part_refs[0][below, :] = jnp.zeros((8, q_ref.shape[1]), jnp.bfloat16)
    part_refs[0][below, pl.ds(0, count)] = targets
    rows = q_ref.shape[0]
    width = k_ref.shape[1]
    kv_here = width // HEAD_DIM
    group = q_ref.shape[1] // HEAD_DIM // kv_here
    core = lax.axis_index("tp") % 2
    base = lax.axis_index("ctx") * rows
    half = rows // blocks // 2
    query_pos = base + lax.broadcasted_iota(jnp.int32, (rows, rows), 0)
    query_start = column(st_ref[...])
    parts = halo[rows : rows + 8, 0:rows].astype(jnp.float32).astype(jnp.int32)
    masks = []
    for shift, key_end in ((rows, parts[0:1] * END_PART + parts[1:2]), (0, end_ref[...])):
        key_pos = base - shift + lax.broadcasted_iota(jnp.int32, (rows, rows), 1)
        masks.append((key_pos <= query_pos) & (key_pos >= query_start) & (key_end > query_pos))
    visible = jnp.concatenate(masks, axis=1)
    visible = jnp.concatenate([visible] * group, axis=0)
    for kv in range(kv_here):
        keys, values = (
            jnp.concatenate(
                [
                    halo[0:rows, first + kv * HEAD_DIM : first + (kv + 1) * HEAD_DIM],
                    ref[:, pl.ds(kv * HEAD_DIM, HEAD_DIM)],
                ],
                axis=0,
            )
            for first, ref in ((0, k_ref), (width, v_ref))
        )
        query = jnp.concatenate(
            [q_ref[:, pl.ds((kv * group + g) * HEAD_DIM, HEAD_DIM)] for g in range(group)], axis=0
        )
        scores = (
            lax.dot_general(
                query, keys, (((1,), (1,)), ((), ())), preferred_element_type=jnp.float32
            )
            * HEAD_DIM**-0.5
        )
        row_max = jnp.max(jnp.where(visible, scores, NEG_LARGE), axis=1, keepdims=True)
        weights = jnp.where(visible, jnp.exp(scores - row_max), 0.0)
        weight_sum = jnp.sum(weights, axis=1, keepdims=True)
        summed = jnp.dot(
            weights.astype(jnp.bfloat16), values, preferred_element_type=jnp.float32
        )
        attended = (summed / weight_sum).astype(jnp.bfloat16)
        for g in range(group):
            for p in range(blocks):
                for h in range(2):
                    first = g * rows + (p * 2 + h) * half
                    place = pl.multiple_of((h ^ core) * half, half)
                    lanes = pl.ds((kv * group + g) * HEAD_DIM, HEAD_DIM)
                    target_rows = pl.ds(p * 2 * half + place, half)
                    plain_ref[target_rows, lanes] = attended[first : first + half]
                    part_refs[p][pl.ds(place, half), lanes] = attended[first : first + half]


def attend(blocks, queries, flipped, mid, keys, values, end, start, own):
    rows, features = queries.shape
    sizes = (rows, rows // blocks + 8) + (rows // blocks,) * (blocks - 1)
    return pl.pallas_call(
        functools.partial(attend_kernel, blocks),
        out_shape=tuple(jax.ShapeDtypeStruct((size, features), jnp.bfloat16) for size in sizes),
        in_specs=vmem(8),
        out_specs=tuple(vmem(1 + blocks)),
        compiler_params=params(),
        cost_estimate=cost(8 * rows * rows * features, 6 * queries.size),
    )(queries, flipped, mid, keys, values, end, start, own)


def project_kernel(block_rows, *refs):
    chunks, weight_ref, mine_ref, other_ref = refs[:-3], refs[-3], refs[-2], refs[-1]
    half = block_rows // 2
    whole = [c.shape[0] // block_rows * block_rows for c in chunks]
    stacked = jnp.concatenate([c[pl.ds(0, n), :] for c, n in zip(chunks, whole)], axis=0)
    share = jnp.dot(stacked, weight_ref[...], preferred_element_type=jnp.float32).astype(
        jnp.bfloat16
    )
    for n in range(share.shape[0] // block_rows):
        first = n * block_rows
        mine_ref[pl.ds(n * half, half), :] = share[first : first + half]
        other_ref[pl.ds(n * half, half), :] = share[first + half : first + block_rows]


def project(block_rows, chunks, weight, estimate=None):
    rows = sum(c.shape[0] // block_rows * block_rows for c in chunks)
    out = jax.ShapeDtypeStruct((rows // 2, weight.shape[1]), jnp.bfloat16)
    return pl.pallas_call(
        functools.partial(project_kernel, block_rows),
        out_shape=(out, out),
        in_specs=vmem(len(chunks) + 1),
        out_specs=tuple(vmem(2)),
        compiler_params=params(),
        cost_estimate=estimate or cost(2 * rows * weight.size, 2 * weight.size),
    )(*chunks, weight)


def total_kernel(*refs):
    terms, out_ref = refs[:-1], refs[-1]
    out_ref[...] = sum(t[...].astype(jnp.float32) for t in terms).astype(out_ref.dtype)


def total(terms):
    return pl.pallas_call(
        total_kernel,
        out_shape=jax.ShapeDtypeStruct(terms[0].shape, jnp.bfloat16),
        in_specs=vmem(len(terms)),
        out_specs=pl.BlockSpec(memory_space=pltpu.VMEM),
        compiler_params=params(),
        cost_estimate=cost(4 * terms[0].size, 10 * terms[0].size),
    )(*terms)


def note(ref, count):
    tail = ref[pl.ds(ref.shape[0] - 8, 8), pl.ds(0, HEAD_DIM)].astype(jnp.float32)
    return tail[0:1, 0:count].astype(jnp.int32)


def pick_kernel(blocks, half, noted_ref, two_ref, *refs):
    sums, outs = refs[:-4], refs[-4:]
    x = lax.axis_index("tp") // 2
    c = lax.axis_index("ctx")
    pieces = [r[pl.ds(n, half), :] for r in sums for n in range(0, r.shape[0], half)]
    targets = jnp.concatenate([note(r, 2 * blocks) for r in (noted_ref, two_ref)], axis=1)
    for k in range(4):
        wanted = (c ^ k) * blocks + x
        piece = pieces[0]
        for n in range(1, len(pieces)):
            here = jnp.broadcast_to(targets[:, n : n + 1] == wanted, piece.shape)
            piece = jnp.where(here, pieces[n], piece)
        outs[k][...] = piece


def pick(blocks, noted, two, sums):
    rows, cols = sum(s.shape[0] for s in sums), sums[0].shape[1]
    half = rows // (4 * blocks)
    out = jax.ShapeDtypeStruct((half, cols), jnp.bfloat16)
    return pl.pallas_call(
        functools.partial(pick_kernel, blocks, half),
        out_shape=(out,) * 4,
        in_specs=vmem(2 + len(sums)),
        out_specs=tuple(vmem(4)),
        compiler_params=params(),
        cost_estimate=cost(4 * rows * cols, 8 * rows * cols),
    )(noted, two, *sums)


def forward_kernel(got_ref, out_ref):
    out_ref[...] = got_ref[pl.ds(0, out_ref.shape[0]), :]


def forward(rows, got):
    out = jax.ShapeDtypeStruct((rows, got.shape[1]), got.dtype)
    return pl.pallas_call(
        forward_kernel,
        out_shape=out,
        in_specs=vmem(1),
        out_specs=pl.BlockSpec(memory_space=pltpu.VMEM),
        compiler_params=params(),
        cost_estimate=cost(0, 6 * out.size),
    )(got)


def hold_kernel(near_ref, far_ref, out_ref):
    cols = near_ref.shape[1]
    out_ref[:, pl.ds(0, cols)] = near_ref[...]
    out_ref[:, pl.ds(cols, cols)] = far_ref[...]


def hold(near, far):
    rows, cols = near.shape
    return pl.pallas_call(
        hold_kernel,
        out_shape=jax.ShapeDtypeStruct((rows, 2 * cols), near.dtype),
        in_specs=vmem(2),
        out_specs=pl.BlockSpec(memory_space=pltpu.VMEM),
        compiler_params=params(),
        cost_estimate=cost(0, 8 * near.size),
    )(near, far)


def join_kernel(held_ref, two_ref, one_ref, out_ref):
    cols = one_ref.shape[1]
    c = lax.axis_index("ctx")
    pieces = (held_ref[:, pl.ds(0, cols)], one_ref[...], two_ref[...], held_ref[:, pl.ds(cols, cols)])
    for k in range(4):
        out_ref[:, pl.ds(pl.multiple_of((c ^ k) * cols, cols), cols)] = pieces[k]


def join(held, two, one):
    rows, cols = one.shape
    return pl.pallas_call(
        join_kernel,
        out_shape=jax.ShapeDtypeStruct((rows, 4 * cols), jnp.bfloat16),
        in_specs=vmem(3),
        out_specs=pl.BlockSpec(memory_space=pltpu.VMEM),
        compiler_params=params(),
        cost_estimate=cost(0, 16 * one.size),
    )(held, two, one)


def flip(array, axis, bits):
    return lax.ppermute(array, axis, [(i, i ^ bits) for i in range(4)])


def core_total(mine, other):
    return total((mine, flip(other, "tp", 1)))


def stack_kernel(done_ref, mine_ref, got_ref, out_ref):
    rows = done_ref.shape[0]
    out_ref[pl.ds(0, rows), :] = done_ref[...]
    both = mine_ref[...].astype(jnp.float32) + got_ref[...].astype(jnp.float32)
    out_ref[pl.ds(rows, mine_ref.shape[0]), :] = both.astype(out_ref.dtype)


def stack_core_total(done, mine, other):
    rows = done.shape[0] + mine.shape[0]
    return pl.pallas_call(
        stack_kernel,
        out_shape=jax.ShapeDtypeStruct((rows, mine.shape[1]), jnp.bfloat16),
        in_specs=vmem(3),
        out_specs=pl.BlockSpec(memory_space=pltpu.VMEM),
        compiler_params=params(),
        cost_estimate=cost(mine.size, 8 * mine.size),
    )(done, mine, flip(other, "tp", 1))


def chip_total(share):
    return total((share, flip(share, "tp", 2)))


def after(value, *others):
    return lax.optimization_barrier((value, *others))[0]


def small_ring(queries, key_rows, value_rows, doc_start, doc_end, block_target, out_weight):
    rows = queries.shape[0]
    blocks = block_target.shape[0]
    block_rows = rows // blocks
    end, start = doc_end.reshape(1, rows), doc_start.reshape(1, rows)
    own_target = block_target.reshape(1, blocks)
    message = pack(key_rows, value_rows, end, own_target)
    flipped = flip(message, "ctx", 1)
    middle = [(4 * c + t, 4 * (3 - c) + t if c in (1, 2) else 4 * c + (t ^ 1)) for c in range(4) for t in range(4)]
    mid = lax.ppermute(message, ("ctx", "tp"), middle)
    plain, first, second = attend(
        blocks, queries, flipped, mid, key_rows, value_rows, end, start, own_target
    )
    rows_1, first_2, second_2 = flip(plain, "ctx", 1), flip(first, "ctx", 2), flip(second, "ctx", 2)
    first_3, second_3 = flip(forward(block_rows, first_2), "ctx", 1), flip(second_2, "ctx", 1)
    share_a = core_total(*project(block_rows, (plain, rows_1), out_weight, cost(1 * 10**8, 0)))
    first_2 = after(first_2, share_a)
    second_2 = after(second_2, share_a)
    share_b = stack_core_total(share_a, *project(block_rows, (first_2, second_2), out_weight))
    first_3 = after(first_3, share_b)
    share_c = core_total(*project(block_rows, (first_3, second_3), out_weight, cost(100 * 10**8, 0)))
    sums = (chip_total(share_b), chip_total(share_c))
    kept, *sent = pick(blocks, first, first_2, sums)
    got_3, got_2, got_1 = (flip(sent[k - 1], "ctx", k) for k in (3, 2, 1))
    return join(hold(kept, got_3), got_2, got_1)


def attend_block(soft_state, query_grid, query_pos, query_start, key_block, value_block, key_end, key_pos):
    running_max, weight_sum, weighted = soft_state
    scores = jnp.einsum(
        "rkgd,nkd->rkgn", query_grid, key_block, preferred_element_type=jnp.float32
    ) * HEAD_DIM ** (-0.5)
    visible = (
        (key_pos[None, :] <= query_pos[:, None])
        & (key_pos[None, :] >= query_start[:, None])
        & (key_end[None, :] > query_pos[:, None])
    )
    visible = visible[:, None, None, :]
    new_max = jnp.maximum(running_max, jnp.max(jnp.where(visible, scores, NEG_LARGE), axis=-1))
    weights = jnp.where(visible, jnp.exp(scores - new_max[..., None]), 0.0)
    fading = jnp.exp(running_max - new_max)
    weight_sum = weight_sum * fading + jnp.sum(weights, axis=-1)
    weighted = weighted * fading[..., None] + jnp.einsum(
        "rkgn,nkd->rkgd",
        weights.astype(jnp.bfloat16),
        value_block,
        preferred_element_type=jnp.float32,
    )
    return (new_max, weight_sum, weighted)


def attend_all(queries, query_pos, query_start, key_part, value_part, end_part):
    rows = queries.shape[0]
    key_count = key_part.shape[0]
    kv_here = key_part.shape[1] // HEAD_DIM
    query_grid = queries.reshape(rows, kv_here, -1, HEAD_DIM)
    block_len = math.gcd(key_count, 512)
    block_count = key_count // block_len
    items = (
        key_part.reshape(block_count, block_len, kv_here, HEAD_DIM),
        value_part.reshape(block_count, block_len, kv_here, HEAD_DIM),
        end_part.reshape(block_count, block_len),
        jnp.arange(key_count, dtype=jnp.int32).reshape(block_count, block_len),
    )
    start_state = (
        jnp.full(query_grid.shape[:3], NEG_LARGE, jnp.float32),
        jnp.zeros(query_grid.shape[:3], jnp.float32),
        jnp.zeros(query_grid.shape, jnp.float32),
    )

    def one_block(state, item):
        return attend_block(state, query_grid, query_pos, query_start, *item), None

    (_, weight_sum, weighted), _ = lax.scan(one_block, start_state, items)
    return (weighted / weight_sum[..., None]).astype(jnp.bfloat16).reshape(rows, -1)


def any_ring(queries, key_rows, value_rows, doc_start, doc_end, block_target, out_weight):
    rows = queries.shape[0]
    blocks = block_target.shape[0]
    block_rows = rows // blocks
    ctx_count = lax.axis_size("ctx")
    tp_count = lax.axis_size("tp")
    gather = functools.partial(lax.all_gather, axis_name="ctx", axis=0, tiled=True)
    query_pos = lax.axis_index("ctx") * rows + jnp.arange(rows, dtype=jnp.int32)
    attended = attend_all(
        queries, query_pos, doc_start, gather(key_rows), gather(value_rows), gather(doc_end)
    )
    targets = gather(block_target)
    source = jnp.zeros_like(targets).at[targets].set(jnp.arange(targets.size, dtype=jnp.int32))
    source_rows = (source[:, None] * block_rows + jnp.arange(block_rows, dtype=jnp.int32)).reshape(-1)
    balanced = jnp.take(gather(attended), source_rows, axis=0)
    share = jnp.dot(balanced, out_weight, preferred_element_type=jnp.float32).astype(jnp.bfloat16)
    share = share.reshape(ctx_count, tp_count, rows // tp_count, -1)
    summed = lax.psum_scatter(share, "tp", scatter_dimension=1, tiled=True)
    pieces = lax.all_to_all(summed[:, 0], "ctx", split_axis=0, concat_axis=0, tiled=True)
    return jnp.swapaxes(pieces, 0, 1).reshape(rows // tp_count, -1)


def shards(queries, key_rows, value_rows, doc_start, doc_end, block_target, out_weight):
    ctx_count, tp_count = lax.axis_size("ctx"), lax.axis_size("tp")
    rows, blocks = queries.shape[0], block_target.shape[0]
    longest = rows * ctx_count // 2 - rows
    near = longest <= rows and ctx_count == 4 and tp_count == 4 and blocks == 2
    plan = small_ring if near and rows % (4 * blocks * 2) == 0 else any_ring
    return plan(queries, key_rows, value_rows, doc_start, doc_end, block_target, out_weight)


def solution(mesh):
    in_specs = (
        P(("group", "ctx"), "tp"),
        P(("group", "ctx"), "tp"),
        P(("group", "ctx"), "tp"),
        P(("group", "ctx")),
        P(("group", "ctx")),
        P(("group", "ctx")),
        P("tp", "ctx"),
    )
    out_specs = P(("group", "ctx", "tp"), None)
    return jax.shard_map(shards, mesh=mesh, in_specs=in_specs, out_specs=out_specs, check_vma=False)
```

```python
import functools
import math

import jax
import jax.numpy as jnp
from jax import lax
from jax.experimental import pallas as pl
from jax.experimental.pallas import tpu as pltpu
from jax.sharding import PartitionSpec as P

HEAD_DIM = 128
NEG_LARGE = -1e30
END_PART = 128


def vmem(count):
    return [pl.BlockSpec(memory_space=pltpu.VMEM)] * count


def smem(count):
    return [pl.BlockSpec(memory_space=pltpu.SMEM)] * count


def params():
    return pltpu.CompilerParams(vmem_limit_bytes=16 * 1024 * 1024)


def cost(flops, moved):
    return pl.CostEstimate(flops=int(flops), bytes_accessed=int(moved), transcendentals=0)


def column(row):
    size = row.shape[1]
    return jnp.transpose(jnp.broadcast_to(row, (size, size)))


def pack_kernel(k_ref, v_ref, end_ref, target_ref, message_ref):
    rows, width = k_ref.shape
    message_ref[pl.ds(0, rows), pl.ds(0, width)] = k_ref[...]
    message_ref[pl.ds(0, rows), pl.ds(width, width)] = v_ref[...]
    extra = message_ref.shape[0] - rows
    line = lax.broadcasted_iota(jnp.int32, (extra, rows), 0)
    ends = jnp.broadcast_to(end_ref[...], (extra, rows))
    parts = jnp.where(line == 0, ends // END_PART, jnp.where(line == 1, ends % END_PART, 0))
    message_ref[pl.ds(rows, extra), :] = jnp.zeros((extra, 2 * width), jnp.bfloat16)
    message_ref[pl.ds(rows, extra), pl.ds(0, rows)] = parts.astype(jnp.float32).astype(jnp.bfloat16)
    targets = jnp.broadcast_to(target_ref[...].astype(jnp.float32), (extra, target_ref.shape[1]))
    message_ref[pl.ds(rows, extra), pl.ds(rows, target_ref.shape[1])] = targets.astype(jnp.bfloat16)


def pack(key_rows, value_rows, ends, targets):
    rows, width = key_rows.shape
    return pl.pallas_call(
        pack_kernel,
        out_shape=jax.ShapeDtypeStruct((rows + 16, 2 * width), jnp.bfloat16),
        in_specs=vmem(4),
        out_specs=pl.BlockSpec(memory_space=pltpu.VMEM),
        cost_estimate=cost(10**9, 8 * key_rows.size),
    )(key_rows, value_rows, ends, targets)


def attend_kernel(
    blocks, q_ref, flip_ref, mid_ref, k_ref, v_ref, end_ref, st_ref, own_ref, plain_ref, *part_refs
):
    across = lax.axis_index("ctx") % 2 == 0
    halo = jnp.where(across, mid_ref[...], flip_ref[...])
    near = flip_ref[pl.ds(k_ref.shape[0], 16), pl.ds(k_ref.shape[0], HEAD_DIM)]
    near = near[0:1, 0:blocks].astype(jnp.float32)
    targets = jnp.concatenate([own_ref[...].astype(jnp.float32), near], axis=1)
    count = targets.shape[1]
    targets = jnp.broadcast_to(targets, (8, count)).astype(jnp.bfloat16)
    below = pl.ds(q_ref.shape[0] // blocks, 8)
    part_refs[0][below, :] = jnp.zeros((8, q_ref.shape[1]), jnp.bfloat16)
    part_refs[0][below, pl.ds(0, count)] = targets
    rows = q_ref.shape[0]
    width = k_ref.shape[1]
    kv_here = width // HEAD_DIM
    group = q_ref.shape[1] // HEAD_DIM // kv_here
    core = lax.axis_index("tp") % 2
    base = lax.axis_index("ctx") * rows
    half = rows // blocks // 2
    query_pos = base + lax.broadcasted_iota(jnp.int32, (rows, rows), 0)
    query_start = column(st_ref[...])
    parts = halo[rows : rows + 16, 0:rows].astype(jnp.float32).astype(jnp.int32)
    masks = []
    for shift, key_end in ((rows, parts[0:1] * END_PART + parts[1:2]), (0, end_ref[...])):
        key_pos = base - shift + lax.broadcasted_iota(jnp.int32, (rows, rows), 1)
        masks.append((key_pos <= query_pos) & (key_pos >= query_start) & (key_end > query_pos))
    visible = jnp.concatenate(masks, axis=1)
    visible = jnp.concatenate([visible] * group, axis=0)
    for kv in range(kv_here):
        keys, values = (
            jnp.concatenate(
                [
                    halo[0:rows, first + kv * HEAD_DIM : first + (kv + 1) * HEAD_DIM],
                    ref[:, pl.ds(kv * HEAD_DIM, HEAD_DIM)],
                ],
                axis=0,
            )
            for first, ref in ((0, k_ref), (width, v_ref))
        )
        query = jnp.concatenate(
            [q_ref[:, pl.ds((kv * group + g) * HEAD_DIM, HEAD_DIM)] for g in range(group)], axis=0
        )
        scores = (
            lax.dot_general(
                query, keys, (((1,), (1,)), ((), ())), preferred_element_type=jnp.float32
            )
            * HEAD_DIM**-0.5
        )
        row_max = jnp.max(jnp.where(visible, scores, NEG_LARGE), axis=1, keepdims=True)
        weights = jnp.where(visible, jnp.exp(scores - row_max), 0.0)
        weight_sum = jnp.sum(weights, axis=1, keepdims=True)
        summed = jnp.dot(
            weights.astype(jnp.bfloat16), values, preferred_element_type=jnp.float32
        )
        attended = (summed / weight_sum).astype(jnp.bfloat16)
        for g in range(group):
            for p in range(blocks):
                for h in range(2):
                    first = g * rows + (p * 2 + h) * half
                    place = pl.multiple_of((h ^ core) * half, half)
                    lanes = pl.ds((kv * group + g) * HEAD_DIM, HEAD_DIM)
                    target_rows = pl.ds(p * 2 * half + place, half)
                    plain_ref[target_rows, lanes] = attended[first : first + half]
                    part_refs[p][pl.ds(place, half), lanes] = attended[first : first + half]


def attend(blocks, queries, flipped, mid, keys, values, end, start, own):
    rows, features = queries.shape
    sizes = (rows, rows // blocks + 8) + (rows // blocks,) * (blocks - 1)
    return pl.pallas_call(
        functools.partial(attend_kernel, blocks),
        out_shape=tuple(jax.ShapeDtypeStruct((size, features), jnp.bfloat16) for size in sizes),
        in_specs=vmem(8),
        out_specs=tuple(vmem(1 + blocks)),
        compiler_params=params(),
        cost_estimate=cost(8 * rows * rows * features, 6 * queries.size),
    )(queries, flipped, mid, keys, values, end, start, own)


def project_kernel(block_rows, *refs):
    chunks, weight_ref, mine_ref, other_ref = refs[:-3], refs[-3], refs[-2], refs[-1]
    half = block_rows // 2
    whole = [c.shape[0] // block_rows * block_rows for c in chunks]
    stacked = jnp.concatenate([c[pl.ds(0, n), :] for c, n in zip(chunks, whole)], axis=0)
    share = jnp.dot(stacked, weight_ref[...], preferred_element_type=jnp.float32).astype(
        jnp.bfloat16
    )
    for n in range(share.shape[0] // block_rows):
        first = n * block_rows
        mine_ref[pl.ds(n * half, half), :] = share[first : first + half]
        other_ref[pl.ds(n * half, half), :] = share[first + half : first + block_rows]


def project(block_rows, chunks, weight, estimate=None):
    rows = sum(c.shape[0] // block_rows * block_rows for c in chunks)
    out = jax.ShapeDtypeStruct((rows // 2, weight.shape[1]), jnp.bfloat16)
    return pl.pallas_call(
        functools.partial(project_kernel, block_rows),
        out_shape=(out, out),
        in_specs=vmem(len(chunks) + 1),
        out_specs=tuple(vmem(2)),
        compiler_params=params(),
        cost_estimate=estimate or cost(2 * rows * weight.size, 2 * weight.size),
    )(*chunks, weight)


def total_kernel(*refs):
    terms, out_ref = refs[:-1], refs[-1]
    out_ref[...] = sum(t[...].astype(jnp.float32) for t in terms).astype(out_ref.dtype)


def total(terms):
    return pl.pallas_call(
        total_kernel,
        out_shape=jax.ShapeDtypeStruct(terms[0].shape, jnp.bfloat16),
        in_specs=vmem(len(terms)),
        out_specs=pl.BlockSpec(memory_space=pltpu.VMEM),
        compiler_params=params(),
        cost_estimate=cost(4 * terms[0].size, 10 * terms[0].size),
    )(*terms)


def note(ref, count):
    tail = ref[pl.ds(ref.shape[0] - 8, 8), pl.ds(0, HEAD_DIM)].astype(jnp.float32)
    return tail[0:1, 0:count].astype(jnp.int32)


def pick_kernel(blocks, half, noted_ref, two_ref, *refs):
    sums, outs = refs[:-4], refs[-4:]
    x = lax.axis_index("tp") // 2
    c = lax.axis_index("ctx")
    pieces = [r[pl.ds(n, half), :] for r in sums for n in range(0, r.shape[0], half)]
    targets = jnp.concatenate([note(r, 2 * blocks) for r in (noted_ref, two_ref)], axis=1)
    for k in range(4):
        wanted = (c ^ k) * blocks + x
        piece = pieces[0]
        for n in range(1, len(pieces)):
            here = jnp.broadcast_to(targets[:, n : n + 1] == wanted, piece.shape)
            piece = jnp.where(here, pieces[n], piece)
        outs[k][...] = piece


def pick(blocks, noted, two, sums):
    rows, cols = sum(s.shape[0] for s in sums), sums[0].shape[1]
    half = rows // (4 * blocks)
    out = jax.ShapeDtypeStruct((half, cols), jnp.bfloat16)
    return pl.pallas_call(
        functools.partial(pick_kernel, blocks, half),
        out_shape=(out,) * 4,
        in_specs=vmem(2 + len(sums)),
        out_specs=tuple(vmem(4)),
        compiler_params=params(),
        cost_estimate=cost(4 * rows * cols, 8 * rows * cols),
    )(noted, two, *sums)


def forward_kernel(got_ref, out_ref):
    out_ref[...] = got_ref[pl.ds(0, out_ref.shape[0]), :]


def forward(rows, got):
    out = jax.ShapeDtypeStruct((rows, got.shape[1]), got.dtype)
    return pl.pallas_call(
        forward_kernel,
        out_shape=out,
        in_specs=vmem(1),
        out_specs=pl.BlockSpec(memory_space=pltpu.VMEM),
        compiler_params=params(),
        cost_estimate=cost(0, 6 * out.size),
    )(got)


def hold_kernel(near_ref, far_ref, out_ref):
    cols = near_ref.shape[1]
    out_ref[:, pl.ds(0, cols)] = near_ref[...]
    out_ref[:, pl.ds(cols, cols)] = far_ref[...]


def hold(near, far):
    rows, cols = near.shape
    return pl.pallas_call(
        hold_kernel,
        out_shape=jax.ShapeDtypeStruct((rows, 2 * cols), near.dtype),
        in_specs=vmem(2),
        out_specs=pl.BlockSpec(memory_space=pltpu.VMEM),
        compiler_params=params(),
        cost_estimate=cost(0, 8 * near.size),
    )(near, far)


def join_kernel(held_ref, one_ref, two_ref, out_ref):
    cols = one_ref.shape[1]
    c = lax.axis_index("ctx")
    pieces = (held_ref[:, pl.ds(0, cols)], one_ref[...], two_ref[...], held_ref[:, pl.ds(cols, cols)])
    for k in range(4):
        out_ref[:, pl.ds(pl.multiple_of((c ^ k) * cols, cols), cols)] = pieces[k]


def join(held, one, two):
    rows, cols = one.shape
    return pl.pallas_call(
        join_kernel,
        out_shape=jax.ShapeDtypeStruct((rows, 4 * cols), jnp.bfloat16),
        in_specs=vmem(3),
        out_specs=pl.BlockSpec(memory_space=pltpu.VMEM),
        compiler_params=params(),
        cost_estimate=cost(0, 16 * one.size),
    )(held, one, two)


def flip(array, axis, bits):
    return lax.ppermute(array, axis, [(i, i ^ bits) for i in range(4)])


def core_total(mine, other):
    return total((mine, flip(other, "tp", 1)))


def stack_kernel(done_ref, mine_ref, got_ref, out_ref):
    rows = done_ref.shape[0]
    out_ref[pl.ds(0, rows), :] = done_ref[...]
    both = mine_ref[...].astype(jnp.float32) + got_ref[...].astype(jnp.float32)
    out_ref[pl.ds(rows, mine_ref.shape[0]), :] = both.astype(out_ref.dtype)


def stack_core_total(done, mine, other):
    rows = done.shape[0] + mine.shape[0]
    return pl.pallas_call(
        stack_kernel,
        out_shape=jax.ShapeDtypeStruct((rows, mine.shape[1]), jnp.bfloat16),
        in_specs=vmem(3),
        out_specs=pl.BlockSpec(memory_space=pltpu.VMEM),
        compiler_params=params(),
        cost_estimate=cost(mine.size, 8 * mine.size),
    )(done, mine, flip(other, "tp", 1))


def chip_total(share):
    return total((share, flip(share, "tp", 2)))


def after(value, *others):
    return lax.optimization_barrier((value, *others))[0]


def small_ring(queries, key_rows, value_rows, doc_start, doc_end, block_target, out_weight):
    rows = queries.shape[0]
    blocks = block_target.shape[0]
    block_rows = rows // blocks
    end, start = doc_end.reshape(1, rows), doc_start.reshape(1, rows)
    own_target = block_target.reshape(1, blocks)
    message = pack(key_rows, value_rows, end, own_target)
    flipped = flip(message, "ctx", 1)
    middle = [(4 * c + t, 4 * (3 - c) + t if c in (1, 2) else 4 * c + (t ^ 1)) for c in range(4) for t in range(4)]
    mid = lax.ppermute(message, ("ctx", "tp"), middle)
    plain, first, second = attend(
        blocks, queries, flipped, mid, key_rows, value_rows, end, start, own_target
    )
    rows_1, first_2, second_2 = flip(plain, "ctx", 1), flip(first, "ctx", 2), flip(second, "ctx", 2)
    first_3, second_3 = flip(forward(block_rows, first_2), "ctx", 1), flip(second_2, "ctx", 1)
    share_a = core_total(*project(block_rows, (plain, rows_1), out_weight, cost(1 * 10**8, 0)))
    first_2 = after(first_2, share_a)
    second_2 = after(second_2, share_a)
    share_b = stack_core_total(share_a, *project(block_rows, (first_2, second_2), out_weight))
    first_3 = after(first_3, share_b)
    share_c = core_total(*project(block_rows, (first_3, second_3), out_weight, cost(100 * 10**8, 0)))
    sums = (chip_total(share_b), chip_total(share_c))
    kept, *sent = pick(blocks, first, first_2, sums)
    got_3, got_1, got_2 = (flip(sent[k - 1], "ctx", k) for k in (3, 1, 2))
    return join(hold(kept, got_3), got_1, got_2)


def attend_block(soft_state, query_grid, query_pos, query_start, key_block, value_block, key_end, key_pos):
    running_max, weight_sum, weighted = soft_state
    scores = jnp.einsum(
        "rkgd,nkd->rkgn", query_grid, key_block, preferred_element_type=jnp.float32
    ) * HEAD_DIM ** (-0.5)
    visible = (
        (key_pos[None, :] <= query_pos[:, None])
        & (key_pos[None, :] >= query_start[:, None])
        & (key_end[None, :] > query_pos[:, None])
    )
    visible = visible[:, None, None, :]
    new_max = jnp.maximum(running_max, jnp.max(jnp.where(visible, scores, NEG_LARGE), axis=-1))
    weights = jnp.where(visible, jnp.exp(scores - new_max[..., None]), 0.0)
    fading = jnp.exp(running_max - new_max)
    weight_sum = weight_sum * fading + jnp.sum(weights, axis=-1)
    weighted = weighted * fading[..., None] + jnp.einsum(
        "rkgn,nkd->rkgd",
        weights.astype(jnp.bfloat16),
        value_block,
        preferred_element_type=jnp.float32,
    )
    return (new_max, weight_sum, weighted)


def attend_all(queries, query_pos, query_start, key_part, value_part, end_part):
    rows = queries.shape[0]
    key_count = key_part.shape[0]
    kv_here = key_part.shape[1] // HEAD_DIM
    query_grid = queries.reshape(rows, kv_here, -1, HEAD_DIM)
    block_len = math.gcd(key_count, 512)
    block_count = key_count // block_len
    items = (
        key_part.reshape(block_count, block_len, kv_here, HEAD_DIM),
        value_part.reshape(block_count, block_len, kv_here, HEAD_DIM),
        end_part.reshape(block_count, block_len),
        jnp.arange(key_count, dtype=jnp.int32).reshape(block_count, block_len),
    )
    start_state = (
        jnp.full(query_grid.shape[:3], NEG_LARGE, jnp.float32),
        jnp.zeros(query_grid.shape[:3], jnp.float32),
        jnp.zeros(query_grid.shape, jnp.float32),
    )

    def one_block(state, item):
        return attend_block(state, query_grid, query_pos, query_start, *item), None

    (_, weight_sum, weighted), _ = lax.scan(one_block, start_state, items)
    return (weighted / weight_sum[..., None]).astype(jnp.bfloat16).reshape(rows, -1)


def any_ring(queries, key_rows, value_rows, doc_start, doc_end, block_target, out_weight):
    rows = queries.shape[0]
    blocks = block_target.shape[0]
    block_rows = rows // blocks
    ctx_count = lax.axis_size("ctx")
    tp_count = lax.axis_size("tp")
    gather = functools.partial(lax.all_gather, axis_name="ctx", axis=0, tiled=True)
    query_pos = lax.axis_index("ctx") * rows + jnp.arange(rows, dtype=jnp.int32)
    attended = attend_all(
        queries, query_pos, doc_start, gather(key_rows), gather(value_rows), gather(doc_end)
    )
    targets = gather(block_target)
    source = jnp.zeros_like(targets).at[targets].set(jnp.arange(targets.size, dtype=jnp.int32))
    source_rows = (source[:, None] * block_rows + jnp.arange(block_rows, dtype=jnp.int32)).reshape(-1)
    balanced = jnp.take(gather(attended), source_rows, axis=0)
    share = jnp.dot(balanced, out_weight, preferred_element_type=jnp.float32).astype(jnp.bfloat16)
    share = share.reshape(ctx_count, tp_count, rows // tp_count, -1)
    summed = lax.psum_scatter(share, "tp", scatter_dimension=1, tiled=True)
    pieces = lax.all_to_all(summed[:, 0], "ctx", split_axis=0, concat_axis=0, tiled=True)
    return jnp.swapaxes(pieces, 0, 1).reshape(rows // tp_count, -1)


def shards(queries, key_rows, value_rows, doc_start, doc_end, block_target, out_weight):
    ctx_count, tp_count = lax.axis_size("ctx"), lax.axis_size("tp")
    rows, blocks = queries.shape[0], block_target.shape[0]
    longest = rows * ctx_count // 2 - rows
    near = longest <= rows and ctx_count == 4 and tp_count == 4 and blocks == 2
    plan = small_ring if near and rows % (4 * blocks * 2) == 0 else any_ring
    return plan(queries, key_rows, value_rows, doc_start, doc_end, block_target, out_weight)


def solution(mesh):
    in_specs = (
        P(("group", "ctx"), "tp"),
        P(("group", "ctx"), "tp"),
        P(("group", "ctx"), "tp"),
        P(("group", "ctx")),
        P(("group", "ctx")),
        P(("group", "ctx")),
        P("tp", "ctx"),
    )
    out_specs = P(("group", "ctx", "tp"), None)
    return jax.shard_map(shards, mesh=mesh, in_specs=in_specs, out_specs=out_specs, check_vma=False)
```

```python
import functools
import math

import jax
import jax.numpy as jnp
from jax import lax
from jax.experimental import pallas as pl
from jax.experimental.pallas import tpu as pltpu
from jax.sharding import PartitionSpec as P

HEAD_DIM = 128
NEG_LARGE = -1e30
END_PART = 128


def vmem(count):
    return [pl.BlockSpec(memory_space=pltpu.VMEM)] * count


def smem(count):
    return [pl.BlockSpec(memory_space=pltpu.SMEM)] * count


def params():
    return pltpu.CompilerParams(vmem_limit_bytes=16 * 1024 * 1024)


def cost(flops, moved):
    return pl.CostEstimate(flops=int(flops), bytes_accessed=int(moved), transcendentals=0)


def column(row):
    size = row.shape[1]
    return jnp.transpose(jnp.broadcast_to(row, (size, size)))


def pack_kernel(k_ref, v_ref, end_ref, target_ref, message_ref):
    rows, width = k_ref.shape
    message_ref[pl.ds(0, rows), pl.ds(0, width)] = k_ref[...]
    message_ref[pl.ds(0, rows), pl.ds(width, width)] = v_ref[...]
    extra = message_ref.shape[0] - rows
    line = lax.broadcasted_iota(jnp.int32, (extra, rows), 0)
    ends = jnp.broadcast_to(end_ref[...], (extra, rows))
    parts = jnp.where(line == 0, ends // END_PART, jnp.where(line == 1, ends % END_PART, 0))
    message_ref[pl.ds(rows, extra), :] = jnp.zeros((extra, 2 * width), jnp.bfloat16)
    message_ref[pl.ds(rows, extra), pl.ds(0, rows)] = parts.astype(jnp.float32).astype(jnp.bfloat16)
    targets = jnp.broadcast_to(target_ref[...].astype(jnp.float32), (extra, target_ref.shape[1]))
    message_ref[pl.ds(rows, extra), pl.ds(rows, target_ref.shape[1])] = targets.astype(jnp.bfloat16)


def pack(key_rows, value_rows, ends, targets):
    rows, width = key_rows.shape
    return pl.pallas_call(
        pack_kernel,
        out_shape=jax.ShapeDtypeStruct((rows + 16, 2 * width), jnp.bfloat16),
        in_specs=vmem(4),
        out_specs=pl.BlockSpec(memory_space=pltpu.VMEM),
        cost_estimate=cost(10**9, 8 * key_rows.size),
    )(key_rows, value_rows, ends, targets)


def attend_kernel(
    blocks, q_ref, flip_ref, mid_ref, k_ref, v_ref, end_ref, st_ref, own_ref, plain_ref, *part_refs
):
    across = lax.axis_index("ctx") % 2 == 0
    halo = jnp.where(across, mid_ref[...], flip_ref[...])
    near = flip_ref[pl.ds(k_ref.shape[0], 16), pl.ds(k_ref.shape[0], HEAD_DIM)]
    near = near[0:1, 0:blocks].astype(jnp.float32)
    targets = jnp.concatenate([own_ref[...].astype(jnp.float32), near], axis=1)
    count = targets.shape[1]
    targets = jnp.broadcast_to(targets, (8, count)).astype(jnp.bfloat16)
    below = pl.ds(q_ref.shape[0] // blocks, 8)
    part_refs[0][below, :] = jnp.zeros((8, q_ref.shape[1]), jnp.bfloat16)
    part_refs[0][below, pl.ds(0, count)] = targets
    rows = q_ref.shape[0]
    width = k_ref.shape[1]
    kv_here = width // HEAD_DIM
    group = q_ref.shape[1] // HEAD_DIM // kv_here
    core = lax.axis_index("tp") % 2
    base = lax.axis_index("ctx") * rows
    half = rows // blocks // 2
    query_pos = base + lax.broadcasted_iota(jnp.int32, (rows, rows), 0)
    query_start = column(st_ref[...])
    parts = halo[rows : rows + 16, 0:rows].astype(jnp.float32).astype(jnp.int32)
    masks = []
    for shift, key_end in ((rows, parts[0:1] * END_PART + parts[1:2]), (0, end_ref[...])):
        key_pos = base - shift + lax.broadcasted_iota(jnp.int32, (rows, rows), 1)
        masks.append((key_pos <= query_pos) & (key_pos >= query_start) & (key_end > query_pos))
    visible = jnp.concatenate(masks, axis=1)
    visible = jnp.concatenate([visible] * group, axis=0)
    for kv in range(kv_here):
        keys, values = (
            jnp.concatenate(
                [
                    halo[0:rows, first + kv * HEAD_DIM : first + (kv + 1) * HEAD_DIM],
                    ref[:, pl.ds(kv * HEAD_DIM, HEAD_DIM)],
                ],
                axis=0,
            )
            for first, ref in ((0, k_ref), (width, v_ref))
        )
        query = jnp.concatenate(
            [q_ref[:, pl.ds((kv * group + g) * HEAD_DIM, HEAD_DIM)] for g in range(group)], axis=0
        )
        scores = (
            lax.dot_general(
                query, keys, (((1,), (1,)), ((), ())), preferred_element_type=jnp.float32
            )
            * HEAD_DIM**-0.5
        )
        row_max = jnp.max(jnp.where(visible, scores, NEG_LARGE), axis=1, keepdims=True)
        weights = jnp.where(visible, jnp.exp(scores - row_max), 0.0)
        weight_sum = jnp.sum(weights, axis=1, keepdims=True)
        summed = jnp.dot(
            weights.astype(jnp.bfloat16), values, preferred_element_type=jnp.float32
        )
        attended = (summed / weight_sum).astype(jnp.bfloat16)
        for g in range(group):
            for p in range(blocks):
                for h in range(2):
                    first = g * rows + (p * 2 + h) * half
                    place = pl.multiple_of((h ^ core) * half, half)
                    lanes = pl.ds((kv * group + g) * HEAD_DIM, HEAD_DIM)
                    target_rows = pl.ds(p * 2 * half + place, half)
                    plain_ref[target_rows, lanes] = attended[first : first + half]
                    part_refs[p][pl.ds(place, half), lanes] = attended[first : first + half]


def attend(blocks, queries, flipped, mid, keys, values, end, start, own):
    rows, features = queries.shape
    sizes = (rows, rows // blocks + 8) + (rows // blocks,) * (blocks - 1)
    return pl.pallas_call(
        functools.partial(attend_kernel, blocks),
        out_shape=tuple(jax.ShapeDtypeStruct((size, features), jnp.bfloat16) for size in sizes),
        in_specs=vmem(8),
        out_specs=tuple(vmem(1 + blocks)),
        compiler_params=params(),
        cost_estimate=cost(8 * rows * rows * features, 6 * queries.size),
    )(queries, flipped, mid, keys, values, end, start, own)


def project_kernel(block_rows, *refs):
    chunks, weight_ref, mine_ref, other_ref = refs[:-3], refs[-3], refs[-2], refs[-1]
    half = block_rows // 2
    whole = [c.shape[0] // block_rows * block_rows for c in chunks]
    stacked = jnp.concatenate([c[pl.ds(0, n), :] for c, n in zip(chunks, whole)], axis=0)
    share = jnp.dot(stacked, weight_ref[...], preferred_element_type=jnp.float32).astype(
        jnp.bfloat16
    )
    for n in range(share.shape[0] // block_rows):
        first = n * block_rows
        mine_ref[pl.ds(n * half, half), :] = share[first : first + half]
        other_ref[pl.ds(n * half, half), :] = share[first + half : first + block_rows]


def project(block_rows, chunks, weight, estimate=None):
    rows = sum(c.shape[0] // block_rows * block_rows for c in chunks)
    out = jax.ShapeDtypeStruct((rows // 2, weight.shape[1]), jnp.bfloat16)
    return pl.pallas_call(
        functools.partial(project_kernel, block_rows),
        out_shape=(out, out),
        in_specs=vmem(len(chunks) + 1),
        out_specs=tuple(vmem(2)),
        compiler_params=params(),
        cost_estimate=estimate or cost(2 * rows * weight.size, 2 * weight.size),
    )(*chunks, weight)


def total_kernel(*refs):
    terms, out_ref = refs[:-1], refs[-1]
    out_ref[...] = sum(t[...].astype(jnp.float32) for t in terms).astype(out_ref.dtype)


def total(terms):
    return pl.pallas_call(
        total_kernel,
        out_shape=jax.ShapeDtypeStruct(terms[0].shape, jnp.bfloat16),
        in_specs=vmem(len(terms)),
        out_specs=pl.BlockSpec(memory_space=pltpu.VMEM),
        compiler_params=params(),
        cost_estimate=cost(4 * terms[0].size, 10 * terms[0].size),
    )(*terms)


def note(ref, count):
    tail = ref[pl.ds(ref.shape[0] - 8, 8), pl.ds(0, HEAD_DIM)].astype(jnp.float32)
    return tail[0:1, 0:count].astype(jnp.int32)


def pick_kernel(blocks, half, noted_ref, two_ref, *refs):
    sums, outs = refs[:-4], refs[-4:]
    x = lax.axis_index("tp") // 2
    c = lax.axis_index("ctx")
    *sums, mine_ref, got_ref = sums
    pieces = [r[pl.ds(n, half), :] for r in sums for n in range(0, r.shape[0], half)]
    last = mine_ref[...].astype(jnp.float32) + got_ref[...].astype(jnp.float32)
    last = last.astype(jnp.bfloat16)
    pieces += [last[n : n + half] for n in range(0, last.shape[0], half)]
    targets = jnp.concatenate([note(r, 2 * blocks) for r in (noted_ref, two_ref)], axis=1)
    for k in range(4):
        wanted = (c ^ k) * blocks + x
        piece = pieces[0]
        for n in range(1, len(pieces)):
            here = jnp.broadcast_to(targets[:, n : n + 1] == wanted, piece.shape)
            piece = jnp.where(here, pieces[n], piece)
        outs[k][...] = piece


def pick(blocks, noted, two, sums):
    rows, cols = sum(s.shape[0] for s in sums[:-1]), sums[0].shape[1]
    half = rows // (4 * blocks)
    out = jax.ShapeDtypeStruct((half, cols), jnp.bfloat16)
    return pl.pallas_call(
        functools.partial(pick_kernel, blocks, half),
        out_shape=(out,) * 4,
        in_specs=vmem(2 + len(sums)),
        out_specs=tuple(vmem(4)),
        compiler_params=params(),
        cost_estimate=cost(4 * rows * cols, 8 * rows * cols),
    )(noted, two, *sums)


def forward_kernel(got_ref, out_ref):
    out_ref[...] = got_ref[pl.ds(0, out_ref.shape[0]), :]


def forward(rows, got):
    out = jax.ShapeDtypeStruct((rows, got.shape[1]), got.dtype)
    return pl.pallas_call(
        forward_kernel,
        out_shape=out,
        in_specs=vmem(1),
        out_specs=pl.BlockSpec(memory_space=pltpu.VMEM),
        compiler_params=params(),
        cost_estimate=cost(0, 6 * out.size),
    )(got)


def hold_kernel(near_ref, far_ref, out_ref):
    cols = near_ref.shape[1]
    out_ref[:, pl.ds(0, cols)] = near_ref[...]
    out_ref[:, pl.ds(cols, cols)] = far_ref[...]


def hold(near, far):
    rows, cols = near.shape
    return pl.pallas_call(
        hold_kernel,
        out_shape=jax.ShapeDtypeStruct((rows, 2 * cols), near.dtype),
        in_specs=vmem(2),
        out_specs=pl.BlockSpec(memory_space=pltpu.VMEM),
        compiler_params=params(),
        cost_estimate=cost(0, 8 * near.size),
    )(near, far)


def join_kernel(held_ref, two_ref, one_ref, out_ref):
    cols = one_ref.shape[1]
    c = lax.axis_index("ctx")
    pieces = (held_ref[:, pl.ds(0, cols)], one_ref[...], two_ref[...], held_ref[:, pl.ds(cols, cols)])
    for k in range(4):
        out_ref[:, pl.ds(pl.multiple_of((c ^ k) * cols, cols), cols)] = pieces[k]


def join(held, two, one):
    rows, cols = one.shape
    return pl.pallas_call(
        join_kernel,
        out_shape=jax.ShapeDtypeStruct((rows, 4 * cols), jnp.bfloat16),
        in_specs=vmem(3),
        out_specs=pl.BlockSpec(memory_space=pltpu.VMEM),
        compiler_params=params(),
        cost_estimate=cost(0, 16 * one.size),
    )(held, two, one)


def flip(array, axis, bits):
    return lax.ppermute(array, axis, [(i, i ^ bits) for i in range(4)])


def core_total(mine, other):
    return total((mine, flip(other, "tp", 1)))


def stack_kernel(done_ref, mine_ref, got_ref, out_ref):
    rows = done_ref.shape[0]
    out_ref[pl.ds(0, rows), :] = done_ref[...]
    both = mine_ref[...].astype(jnp.float32) + got_ref[...].astype(jnp.float32)
    out_ref[pl.ds(rows, mine_ref.shape[0]), :] = both.astype(out_ref.dtype)


def stack_core_total(done, mine, other):
    rows = done.shape[0] + mine.shape[0]
    return pl.pallas_call(
        stack_kernel,
        out_shape=jax.ShapeDtypeStruct((rows, mine.shape[1]), jnp.bfloat16),
        in_specs=vmem(3),
        out_specs=pl.BlockSpec(memory_space=pltpu.VMEM),
        compiler_params=params(),
        cost_estimate=cost(mine.size, 8 * mine.size),
    )(done, mine, flip(other, "tp", 1))


def chip_total(share):
    return total((share, flip(share, "tp", 2)))


def after(value, *others):
    return lax.optimization_barrier((value, *others))[0]


def small_ring(queries, key_rows, value_rows, doc_start, doc_end, block_target, out_weight):
    rows = queries.shape[0]
    blocks = block_target.shape[0]
    block_rows = rows // blocks
    end, start = doc_end.reshape(1, rows), doc_start.reshape(1, rows)
    own_target = block_target.reshape(1, blocks)
    message = pack(key_rows, value_rows, end, own_target)
    flipped = flip(message, "ctx", 1)
    middle = [(4 * c + t, 4 * (3 - c) + t if c in (1, 2) else 4 * c + (t ^ 1)) for c in range(4) for t in range(4)]
    mid = lax.ppermute(message, ("ctx", "tp"), middle)
    plain, first, second = attend(
        blocks, queries, flipped, mid, key_rows, value_rows, end, start, own_target
    )
    rows_1, first_2, second_2 = flip(plain, "ctx", 1), flip(first, "ctx", 2), flip(second, "ctx", 2)
    first_3, second_3 = flip(forward(block_rows, first_2), "ctx", 1), flip(second_2, "ctx", 1)
    share_a = core_total(*project(block_rows, (plain, rows_1), out_weight, cost(1 * 10**8, 0)))
    first_2 = after(first_2, share_a)
    second_2 = after(second_2, share_a)
    share_b = stack_core_total(share_a, *project(block_rows, (first_2, second_2), out_weight))
    first_3 = after(first_3, share_b)
    share_c = core_total(*project(block_rows, (first_3, second_3), out_weight, cost(100 * 10**8, 0)))
    sums = (chip_total(share_b), share_c, flip(share_c, "tp", 2))
    kept, *sent = pick(blocks, first, first_2, sums)
    got_3, got_2, got_1 = (flip(sent[k - 1], "ctx", k) for k in (3, 2, 1))
    return join(hold(kept, got_3), got_2, got_1)


def attend_block(soft_state, query_grid, query_pos, query_start, key_block, value_block, key_end, key_pos):
    running_max, weight_sum, weighted = soft_state
    scores = jnp.einsum(
        "rkgd,nkd->rkgn", query_grid, key_block, preferred_element_type=jnp.float32
    ) * HEAD_DIM ** (-0.5)
    visible = (
        (key_pos[None, :] <= query_pos[:, None])
        & (key_pos[None, :] >= query_start[:, None])
        & (key_end[None, :] > query_pos[:, None])
    )
    visible = visible[:, None, None, :]
    new_max = jnp.maximum(running_max, jnp.max(jnp.where(visible, scores, NEG_LARGE), axis=-1))
    weights = jnp.where(visible, jnp.exp(scores - new_max[..., None]), 0.0)
    fading = jnp.exp(running_max - new_max)
    weight_sum = weight_sum * fading + jnp.sum(weights, axis=-1)
    weighted = weighted * fading[..., None] + jnp.einsum(
        "rkgn,nkd->rkgd",
        weights.astype(jnp.bfloat16),
        value_block,
        preferred_element_type=jnp.float32,
    )
    return (new_max, weight_sum, weighted)


def attend_all(queries, query_pos, query_start, key_part, value_part, end_part):
    rows = queries.shape[0]
    key_count = key_part.shape[0]
    kv_here = key_part.shape[1] // HEAD_DIM
    query_grid = queries.reshape(rows, kv_here, -1, HEAD_DIM)
    block_len = math.gcd(key_count, 512)
    block_count = key_count // block_len
    items = (
        key_part.reshape(block_count, block_len, kv_here, HEAD_DIM),
        value_part.reshape(block_count, block_len, kv_here, HEAD_DIM),
        end_part.reshape(block_count, block_len),
        jnp.arange(key_count, dtype=jnp.int32).reshape(block_count, block_len),
    )
    start_state = (
        jnp.full(query_grid.shape[:3], NEG_LARGE, jnp.float32),
        jnp.zeros(query_grid.shape[:3], jnp.float32),
        jnp.zeros(query_grid.shape, jnp.float32),
    )

    def one_block(state, item):
        return attend_block(state, query_grid, query_pos, query_start, *item), None

    (_, weight_sum, weighted), _ = lax.scan(one_block, start_state, items)
    return (weighted / weight_sum[..., None]).astype(jnp.bfloat16).reshape(rows, -1)


def any_ring(queries, key_rows, value_rows, doc_start, doc_end, block_target, out_weight):
    rows = queries.shape[0]
    blocks = block_target.shape[0]
    block_rows = rows // blocks
    ctx_count = lax.axis_size("ctx")
    tp_count = lax.axis_size("tp")
    gather = functools.partial(lax.all_gather, axis_name="ctx", axis=0, tiled=True)
    query_pos = lax.axis_index("ctx") * rows + jnp.arange(rows, dtype=jnp.int32)
    attended = attend_all(
        queries, query_pos, doc_start, gather(key_rows), gather(value_rows), gather(doc_end)
    )
    targets = gather(block_target)
    source = jnp.zeros_like(targets).at[targets].set(jnp.arange(targets.size, dtype=jnp.int32))
    source_rows = (source[:, None] * block_rows + jnp.arange(block_rows, dtype=jnp.int32)).reshape(-1)
    balanced = jnp.take(gather(attended), source_rows, axis=0)
    share = jnp.dot(balanced, out_weight, preferred_element_type=jnp.float32).astype(jnp.bfloat16)
    share = share.reshape(ctx_count, tp_count, rows // tp_count, -1)
    summed = lax.psum_scatter(share, "tp", scatter_dimension=1, tiled=True)
    pieces = lax.all_to_all(summed[:, 0], "ctx", split_axis=0, concat_axis=0, tiled=True)
    return jnp.swapaxes(pieces, 0, 1).reshape(rows // tp_count, -1)


def shards(queries, key_rows, value_rows, doc_start, doc_end, block_target, out_weight):
    ctx_count, tp_count = lax.axis_size("ctx"), lax.axis_size("tp")
    rows, blocks = queries.shape[0], block_target.shape[0]
    longest = rows * ctx_count // 2 - rows
    near = longest <= rows and ctx_count == 4 and tp_count == 4 and blocks == 2
    plan = small_ring if near and rows % (4 * blocks * 2) == 0 else any_ring
    return plan(queries, key_rows, value_rows, doc_start, doc_end, block_target, out_weight)


def solution(mesh):
    in_specs = (
        P(("group", "ctx"), "tp"),
        P(("group", "ctx"), "tp"),
        P(("group", "ctx"), "tp"),
        P(("group", "ctx")),
        P(("group", "ctx")),
        P(("group", "ctx")),
        P("tp", "ctx"),
    )
    out_specs = P(("group", "ctx", "tp"), None)
    return jax.shard_map(shards, mesh=mesh, in_specs=in_specs, out_specs=out_specs, check_vma=False)
```

```python
import functools
import math

import jax
import jax.numpy as jnp
from jax import lax
from jax.experimental import pallas as pl
from jax.experimental.pallas import tpu as pltpu
from jax.sharding import PartitionSpec as P

HEAD_DIM = 128
NEG_LARGE = -1e30
END_PART = 128


def vmem(count):
    return [pl.BlockSpec(memory_space=pltpu.VMEM)] * count


def smem(count):
    return [pl.BlockSpec(memory_space=pltpu.SMEM)] * count


def params():
    return pltpu.CompilerParams(vmem_limit_bytes=16 * 1024 * 1024)


def cost(flops, moved):
    return pl.CostEstimate(flops=int(flops), bytes_accessed=int(moved), transcendentals=0)


def column(row):
    size = row.shape[1]
    return jnp.transpose(jnp.broadcast_to(row, (size, size)))


def pack_kernel(k_ref, v_ref, end_ref, target_ref, message_ref):
    rows, width = k_ref.shape
    message_ref[pl.ds(0, rows), pl.ds(0, width)] = k_ref[...]
    message_ref[pl.ds(0, rows), pl.ds(width, width)] = v_ref[...]
    extra = message_ref.shape[0] - rows
    line = lax.broadcasted_iota(jnp.int32, (extra, rows), 0)
    ends = jnp.broadcast_to(end_ref[...], (extra, rows))
    parts = jnp.where(line == 0, ends // END_PART, jnp.where(line == 1, ends % END_PART, 0))
    message_ref[pl.ds(rows, extra), :] = jnp.zeros((extra, 2 * width), jnp.bfloat16)
    message_ref[pl.ds(rows, extra), pl.ds(0, rows)] = parts.astype(jnp.float32).astype(jnp.bfloat16)
    targets = jnp.broadcast_to(target_ref[...].astype(jnp.float32), (extra, target_ref.shape[1]))
    message_ref[pl.ds(rows, extra), pl.ds(rows, target_ref.shape[1])] = targets.astype(jnp.bfloat16)


def pack(key_rows, value_rows, ends, targets):
    rows, width = key_rows.shape
    return pl.pallas_call(
        pack_kernel,
        out_shape=jax.ShapeDtypeStruct((rows + 8, 2 * width), jnp.bfloat16),
        in_specs=vmem(4),
        out_specs=pl.BlockSpec(memory_space=pltpu.VMEM),
        cost_estimate=cost(10**9, 8 * key_rows.size),
    )(key_rows, value_rows, ends, targets)


def attend_kernel(
    blocks, q_ref, flip_ref, mid_ref, k_ref, v_ref, end_ref, st_ref, own_ref, plain_ref, *part_refs
):
    across = lax.axis_index("ctx") % 2 == 0
    halo = jnp.where(across, mid_ref[...], flip_ref[...])
    near = flip_ref[pl.ds(k_ref.shape[0], 8), pl.ds(k_ref.shape[0], HEAD_DIM)]
    near = near[0:1, 0:blocks].astype(jnp.float32)
    targets = jnp.concatenate([own_ref[...].astype(jnp.float32), near], axis=1)
    count = targets.shape[1]
    targets = jnp.broadcast_to(targets, (8, count)).astype(jnp.bfloat16)
    below = pl.ds(q_ref.shape[0] // blocks, 8)
    part_refs[0][below, :] = jnp.zeros((8, q_ref.shape[1]), jnp.bfloat16)
    part_refs[0][below, pl.ds(0, count)] = targets
    rows = q_ref.shape[0]
    width = k_ref.shape[1]
    kv_here = width // HEAD_DIM
    group = q_ref.shape[1] // HEAD_DIM // kv_here
    core = lax.axis_index("tp") % 2
    base = lax.axis_index("ctx") * rows
    half = rows // blocks // 2
    query_pos = base + lax.broadcasted_iota(jnp.int32, (rows, rows), 0)
    query_start = column(st_ref[...])
    parts = halo[rows : rows + 8, 0:rows].astype(jnp.float32).astype(jnp.int32)
    masks = []
    for shift, key_end in ((rows, parts[0:1] * END_PART + parts[1:2]), (0, end_ref[...])):
        key_pos = base - shift + lax.broadcasted_iota(jnp.int32, (rows, rows), 1)
        masks.append((key_pos <= query_pos) & (key_pos >= query_start) & (key_end > query_pos))
    visible = jnp.concatenate(masks, axis=1)
    visible = jnp.concatenate([visible] * group, axis=0)
    for kv in range(kv_here):
        keys, values = (
            jnp.concatenate(
                [
                    halo[0:rows, first + kv * HEAD_DIM : first + (kv + 1) * HEAD_DIM],
                    ref[:, pl.ds(kv * HEAD_DIM, HEAD_DIM)],
                ],
                axis=0,
            )
            for first, ref in ((0, k_ref), (width, v_ref))
        )
        query = jnp.concatenate(
            [q_ref[:, pl.ds((kv * group + g) * HEAD_DIM, HEAD_DIM)] for g in range(group)], axis=0
        )
        scores = (
            lax.dot_general(
                query, keys, (((1,), (1,)), ((), ())), preferred_element_type=jnp.float32
            )
            * HEAD_DIM**-0.5
        )
        row_max = jnp.max(jnp.where(visible, scores, NEG_LARGE), axis=1, keepdims=True)
        weights = jnp.where(visible, jnp.exp(scores - row_max), 0.0)
        weight_sum = jnp.sum(weights, axis=1, keepdims=True)
        summed = jnp.dot(
            weights.astype(jnp.bfloat16), values, preferred_element_type=jnp.float32
        )
        attended = (summed / weight_sum).astype(jnp.bfloat16)
        for g in range(group):
            for p in range(blocks):
                for h in range(2):
                    first = g * rows + (p * 2 + h) * half
                    place = pl.multiple_of((h ^ core) * half, half)
                    lanes = pl.ds((kv * group + g) * HEAD_DIM, HEAD_DIM)
                    target_rows = pl.ds(p * 2 * half + place, half)
                    plain_ref[target_rows, lanes] = attended[first : first + half]
                    part_refs[p][pl.ds(place, half), lanes] = attended[first : first + half]


def attend(blocks, queries, flipped, mid, keys, values, end, start, own):
    rows, features = queries.shape
    sizes = (rows, rows // blocks + 8) + (rows // blocks,) * (blocks - 1)
    return pl.pallas_call(
        functools.partial(attend_kernel, blocks),
        out_shape=tuple(jax.ShapeDtypeStruct((size, features), jnp.bfloat16) for size in sizes),
        in_specs=vmem(8),
        out_specs=tuple(vmem(1 + blocks)),
        compiler_params=params(),
        cost_estimate=cost(8 * rows * rows * features, 6 * queries.size),
    )(queries, flipped, mid, keys, values, end, start, own)


def project_kernel(block_rows, *refs):
    chunks, weight_ref, mine_ref, other_ref = refs[:-3], refs[-3], refs[-2], refs[-1]
    half = block_rows // 2
    whole = [c.shape[0] // block_rows * block_rows for c in chunks]
    stacked = jnp.concatenate([c[pl.ds(0, n), :] for c, n in zip(chunks, whole)], axis=0)
    share = jnp.dot(stacked, weight_ref[...], preferred_element_type=jnp.float32).astype(
        jnp.bfloat16
    )
    for n in range(share.shape[0] // block_rows):
        first = n * block_rows
        mine_ref[pl.ds(n * half, half), :] = share[first : first + half]
        other_ref[pl.ds(n * half, half), :] = share[first + half : first + block_rows]


def project(block_rows, chunks, weight, estimate=None):
    rows = sum(c.shape[0] // block_rows * block_rows for c in chunks)
    out = jax.ShapeDtypeStruct((rows // 2, weight.shape[1]), jnp.bfloat16)
    return pl.pallas_call(
        functools.partial(project_kernel, block_rows),
        out_shape=(out, out),
        in_specs=vmem(len(chunks) + 1),
        out_specs=tuple(vmem(2)),
        compiler_params=params(),
        cost_estimate=estimate or cost(2 * rows * weight.size, 2 * weight.size),
    )(*chunks, weight)


def total_kernel(*refs):
    terms, out_ref = refs[:-1], refs[-1]
    out_ref[...] = sum(t[...].astype(jnp.float32) for t in terms).astype(out_ref.dtype)


def total(terms):
    return pl.pallas_call(
        total_kernel,
        out_shape=jax.ShapeDtypeStruct(terms[0].shape, jnp.bfloat16),
        in_specs=vmem(len(terms)),
        out_specs=pl.BlockSpec(memory_space=pltpu.VMEM),
        compiler_params=params(),
        cost_estimate=cost(4 * terms[0].size, 10 * terms[0].size),
    )(*terms)


def note(ref, count):
    tail = ref[pl.ds(ref.shape[0] - 8, 8), pl.ds(0, HEAD_DIM)].astype(jnp.float32)
    return tail[0:1, 0:count].astype(jnp.int32)


def pick_kernel(blocks, half, noted_ref, two_ref, *refs):
    sums, outs = refs[:-4], refs[-4:]
    x = lax.axis_index("tp") // 2
    c = lax.axis_index("ctx")
    *sums, mine_ref, got_ref = sums
    pieces = [r[pl.ds(n, half), :] for r in sums for n in range(0, r.shape[0], half)]
    last = mine_ref[...].astype(jnp.float32) + got_ref[...].astype(jnp.float32)
    last = last.astype(jnp.bfloat16)
    pieces += [last[n : n + half] for n in range(0, last.shape[0], half)]
    targets = jnp.concatenate([note(r, 2 * blocks) for r in (noted_ref, two_ref)], axis=1)
    for k in range(4):
        wanted = (c ^ k) * blocks + x
        piece = pieces[0]
        for n in range(1, len(pieces)):
            here = jnp.broadcast_to(targets[:, n : n + 1] == wanted, piece.shape)
            piece = jnp.where(here, pieces[n], piece)
        outs[k][...] = piece


def pick(blocks, noted, two, sums):
    rows, cols = sum(s.shape[0] for s in sums[:-1]), sums[0].shape[1]
    half = rows // (4 * blocks)
    out = jax.ShapeDtypeStruct((half, cols), jnp.bfloat16)
    return pl.pallas_call(
        functools.partial(pick_kernel, blocks, half),
        out_shape=(out,) * 4,
        in_specs=vmem(2 + len(sums)),
        out_specs=tuple(vmem(4)),
        compiler_params=params(),
        cost_estimate=cost(4 * rows * cols, 8 * rows * cols),
    )(noted, two, *sums)


def forward_kernel(got_ref, out_ref):
    out_ref[...] = got_ref[pl.ds(0, out_ref.shape[0]), :]


def forward(rows, got):
    out = jax.ShapeDtypeStruct((rows, got.shape[1]), got.dtype)
    return pl.pallas_call(
        forward_kernel,
        out_shape=out,
        in_specs=vmem(1),
        out_specs=pl.BlockSpec(memory_space=pltpu.VMEM),
        compiler_params=params(),
        cost_estimate=cost(0, 6 * out.size),
    )(got)


def hold_kernel(near_ref, far_ref, out_ref):
    cols = near_ref.shape[1]
    out_ref[:, pl.ds(0, cols)] = near_ref[...]
    out_ref[:, pl.ds(cols, cols)] = far_ref[...]


def hold(near, far):
    rows, cols = near.shape
    return pl.pallas_call(
        hold_kernel,
        out_shape=jax.ShapeDtypeStruct((rows, 2 * cols), near.dtype),
        in_specs=vmem(2),
        out_specs=pl.BlockSpec(memory_space=pltpu.VMEM),
        compiler_params=params(),
        cost_estimate=cost(0, 8 * near.size),
    )(near, far)


def join_kernel(held_ref, two_ref, one_ref, out_ref):
    cols = one_ref.shape[1]
    c = lax.axis_index("ctx")
    pieces = (held_ref[:, pl.ds(0, cols)], one_ref[...], two_ref[...], held_ref[:, pl.ds(cols, cols)])
    for k in range(4):
        out_ref[:, pl.ds(pl.multiple_of((c ^ k) * cols, cols), cols)] = pieces[k]


def join(held, two, one):
    rows, cols = one.shape
    return pl.pallas_call(
        join_kernel,
        out_shape=jax.ShapeDtypeStruct((rows, 4 * cols), jnp.bfloat16),
        in_specs=vmem(3),
        out_specs=pl.BlockSpec(memory_space=pltpu.VMEM),
        compiler_params=params(),
        cost_estimate=cost(0, 16 * one.size),
    )(held, two, one)


def flip(array, axis, bits):
    return lax.ppermute(array, axis, [(i, i ^ bits) for i in range(4)])


def core_total(mine, other):
    return total((mine, flip(other, "tp", 1)))


def stack_kernel(done_ref, mine_ref, got_ref, out_ref):
    rows = done_ref.shape[0]
    out_ref[pl.ds(0, rows), :] = done_ref[...]
    both = mine_ref[...].astype(jnp.float32) + got_ref[...].astype(jnp.float32)
    out_ref[pl.ds(rows, mine_ref.shape[0]), :] = both.astype(out_ref.dtype)


def stack_core_total(done, mine, other):
    rows = done.shape[0] + mine.shape[0]
    return pl.pallas_call(
        stack_kernel,
        out_shape=jax.ShapeDtypeStruct((rows, mine.shape[1]), jnp.bfloat16),
        in_specs=vmem(3),
        out_specs=pl.BlockSpec(memory_space=pltpu.VMEM),
        compiler_params=params(),
        cost_estimate=cost(mine.size, 8 * mine.size),
    )(done, mine, flip(other, "tp", 1))


def chip_total(share):
    return total((share, flip(share, "tp", 2)))


def after(value, *others):
    return lax.optimization_barrier((value, *others))[0]


def small_ring(queries, key_rows, value_rows, doc_start, doc_end, block_target, out_weight):
    rows = queries.shape[0]
    blocks = block_target.shape[0]
    block_rows = rows // blocks
    end, start = doc_end.reshape(1, rows), doc_start.reshape(1, rows)
    own_target = block_target.reshape(1, blocks)
    message = pack(key_rows, value_rows, end, own_target)
    flipped = flip(message, "ctx", 1)
    middle = [(4 * c + t, 4 * (3 - c) + t if c in (1, 2) else 4 * c + (t ^ 1)) for c in range(4) for t in range(4)]
    mid = lax.ppermute(message, ("ctx", "tp"), middle)
    plain, first, second = attend(
        blocks, queries, flipped, mid, key_rows, value_rows, end, start, own_target
    )
    rows_1, first_2, second_2 = flip(plain, "ctx", 1), flip(first, "ctx", 2), flip(second, "ctx", 2)
    first_3, second_3 = flip(forward(block_rows, first_2), "ctx", 1), flip(second_2, "ctx", 1)
    share_a = core_total(*project(block_rows, (plain, rows_1), out_weight, cost(1 * 10**8, 0)))
    first_2 = after(first_2, share_a)
    second_2 = after(second_2, share_a)
    share_b = stack_core_total(share_a, *project(block_rows, (first_2, second_2), out_weight))
    first_3 = after(first_3, share_b)
    share_c = core_total(*project(block_rows, (first_3, second_3), out_weight, cost(100 * 10**8, 0)))
    sums = (chip_total(share_b), share_c, flip(share_c, "tp", 2))
    kept, *sent = pick(blocks, first, first_2, sums)
    got_3, got_2, got_1 = (flip(sent[k - 1], "ctx", k) for k in (3, 2, 1))
    return join(hold(kept, got_3), got_2, got_1)


def attend_block(soft_state, query_grid, query_pos, query_start, key_block, value_block, key_end, key_pos):
    running_max, weight_sum, weighted = soft_state
    scores = jnp.einsum(
        "rkgd,nkd->rkgn", query_grid, key_block, preferred_element_type=jnp.float32
    ) * HEAD_DIM ** (-0.5)
    visible = (
        (key_pos[None, :] <= query_pos[:, None])
        & (key_pos[None, :] >= query_start[:, None])
        & (key_end[None, :] > query_pos[:, None])
    )
    visible = visible[:, None, None, :]
    new_max = jnp.maximum(running_max, jnp.max(jnp.where(visible, scores, NEG_LARGE), axis=-1))
    weights = jnp.where(visible, jnp.exp(scores - new_max[..., None]), 0.0)
    fading = jnp.exp(running_max - new_max)
    weight_sum = weight_sum * fading + jnp.sum(weights, axis=-1)
    weighted = weighted * fading[..., None] + jnp.einsum(
        "rkgn,nkd->rkgd",
        weights.astype(jnp.bfloat16),
        value_block,
        preferred_element_type=jnp.float32,
    )
    return (new_max, weight_sum, weighted)


def attend_all(queries, query_pos, query_start, key_part, value_part, end_part):
    rows = queries.shape[0]
    key_count = key_part.shape[0]
    kv_here = key_part.shape[1] // HEAD_DIM
    query_grid = queries.reshape(rows, kv_here, -1, HEAD_DIM)
    block_len = math.gcd(key_count, 512)
    block_count = key_count // block_len
    items = (
        key_part.reshape(block_count, block_len, kv_here, HEAD_DIM),
        value_part.reshape(block_count, block_len, kv_here, HEAD_DIM),
        end_part.reshape(block_count, block_len),
        jnp.arange(key_count, dtype=jnp.int32).reshape(block_count, block_len),
    )
    start_state = (
        jnp.full(query_grid.shape[:3], NEG_LARGE, jnp.float32),
        jnp.zeros(query_grid.shape[:3], jnp.float32),
        jnp.zeros(query_grid.shape, jnp.float32),
    )

    def one_block(state, item):
        return attend_block(state, query_grid, query_pos, query_start, *item), None

    (_, weight_sum, weighted), _ = lax.scan(one_block, start_state, items)
    return (weighted / weight_sum[..., None]).astype(jnp.bfloat16).reshape(rows, -1)


def any_ring(queries, key_rows, value_rows, doc_start, doc_end, block_target, out_weight):
    rows = queries.shape[0]
    blocks = block_target.shape[0]
    block_rows = rows // blocks
    ctx_count = lax.axis_size("ctx")
    tp_count = lax.axis_size("tp")
    gather = functools.partial(lax.all_gather, axis_name="ctx", axis=0, tiled=True)
    query_pos = lax.axis_index("ctx") * rows + jnp.arange(rows, dtype=jnp.int32)
    attended = attend_all(
        queries, query_pos, doc_start, gather(key_rows), gather(value_rows), gather(doc_end)
    )
    targets = gather(block_target)
    source = jnp.zeros_like(targets).at[targets].set(jnp.arange(targets.size, dtype=jnp.int32))
    source_rows = (source[:, None] * block_rows + jnp.arange(block_rows, dtype=jnp.int32)).reshape(-1)
    balanced = jnp.take(gather(attended), source_rows, axis=0)
    share = jnp.dot(balanced, out_weight, preferred_element_type=jnp.float32).astype(jnp.bfloat16)
    share = share.reshape(ctx_count, tp_count, rows // tp_count, -1)
    summed = lax.psum_scatter(share, "tp", scatter_dimension=1, tiled=True)
    pieces = lax.all_to_all(summed[:, 0], "ctx", split_axis=0, concat_axis=0, tiled=True)
    return jnp.swapaxes(pieces, 0, 1).reshape(rows // tp_count, -1)


def shards(queries, key_rows, value_rows, doc_start, doc_end, block_target, out_weight):
    ctx_count, tp_count = lax.axis_size("ctx"), lax.axis_size("tp")
    rows, blocks = queries.shape[0], block_target.shape[0]
    longest = rows * ctx_count // 2 - rows
    near = longest <= rows and ctx_count == 4 and tp_count == 4 and blocks == 2
    plan = small_ring if near and rows % (4 * blocks * 2) == 0 else any_ring
    return plan(queries, key_rows, value_rows, doc_start, doc_end, block_target, out_weight)


def solution(mesh):
    in_specs = (
        P(("group", "ctx"), "tp"),
        P(("group", "ctx"), "tp"),
        P(("group", "ctx"), "tp"),
        P(("group", "ctx")),
        P(("group", "ctx")),
        P(("group", "ctx")),
        P("tp", "ctx"),
    )
    out_specs = P(("group", "ctx", "tp"), None)
    return jax.shard_map(shards, mesh=mesh, in_specs=in_specs, out_specs=out_specs, check_vma=False)
```
